256 devices in a mesh: freq: 8 (over z_hi, core), frames: 32 (over z_lo, x, y).
Axes of the slice: x: 4, y: 4, z: 8 (z_hi: 4, z_lo: 2; z = z_hi * 2 + z_lo), core: 2. Of those that a mesh axis runs over, the one named last changes fastest.
Arguments:
- signal: float32 [32, 8, 1048576], P('frames', 'freq'), may hold values from -6 to 6
- templates: float32 [64, 32768], P(None, ('freq', 'frames')), may hold values from 0.03 to 3.6, as said below
- activations: float32 [64, 8192], P('freq', 'frames'), may hold values from 0.3 to 36, as said below
Outputs:
- final_activations: float32 [64, 8192], P('freq', 'frames')
- final_templates: float32 [64, 32768], P(None, ('freq', 'frames'))
The draws below stay inside these ranges and needn't reach their ends.
Inputs may be any that keep to these rules, and one draw needn't show every extreme that they name: `templates`: all entries are positive. `activations`: all entries are positive.
All inputs are finite; a program needn't handle non-finite values.
Results may differ from the reference program's by a relative error of at most 0.00011.
Values sent between devices are 32-bit elements; how exact they have to be, the bound alone decides.
A program may use at most 64 MiB of HBM per device.

```python
import math
import jax
import jax.numpy as jnp
from jax import lax

FRAME_LEN = 65536
SPLIT = 256
RANK = 64
FR_DEV = 32
BINS = 32768
BLK = 256
FRAMES = 8192
BLOCKS = 32
SUBS = 8


def positive_field(seed_key, row_count, column_count, low_value, high_value):
    values = jnp.exp(jax.random.uniform(seed_key, (row_count, column_count), jnp.float32, math.log(low_value), math.log(high_value)))
    rising = jnp.exp(math.log(3.0) * jnp.arange(column_count, dtype=jnp.int32).astype(jnp.float32) / column_count)
    return values * rising[None, :]


def draw_signal(key, part):
    hop_len = FRAME_LEN // 2
    row_count = BLOCKS * SUBS * FR_DEV
    piece_count = BLOCKS * SUBS
    note_count = 32
    harmonics = 4
    period = 4 * FRAME_LEN
    base_pitch = jax.random.randint(jax.random.fold_in(key, 31), (note_count,), 8, period // (2 * harmonics), jnp.int32)
    orders = jnp.arange(1, harmonics + 1, dtype=jnp.int32)
    pitch = (base_pitch[:, None] * orders[None, :]).reshape(note_count * harmonics)
    start_phase = jax.random.uniform(jax.random.fold_in(key, 32), (note_count * harmonics,), jnp.float32, 0.0, 2.0 * math.pi)
    positions = jnp.arange(hop_len, dtype=jnp.int32)
    low_part = positions % 256
    high_part = positions // 256
    inner = (pitch[:, None] * high_part[None, :] % period * 256 + pitch[:, None] * low_part[None, :]) % period
    inner_angle = 2.0 * math.pi / period * inner.astype(jnp.float32)
    table = jnp.concatenate([jnp.cos(inner_angle), jnp.sin(inner_angle)], 0)
    rows = jnp.arange(row_count, dtype=jnp.int32)
    row_turn = (pitch % 8)[None, :] * (rows % 8)[:, None] % 8
    theta = start_phase[None, :] + 2.0 * math.pi / 8.0 * row_turn.astype(jnp.float32)
    envelope = jnp.exp(jax.random.uniform(jax.random.fold_in(key, 33), (piece_count, note_count), jnp.float32, math.log(0.02), math.log(0.4)))
    harmonic_weight = jax.random.uniform(jax.random.fold_in(key, 34), (note_count, harmonics), jnp.float32, 0.4, 1.0) / orders[None, :].astype(jnp.float32)
    amplitude = (jnp.repeat(envelope, FR_DEV, axis=0)[:, :, None] * harmonic_weight[None, :, :]).reshape(row_count, note_count * harmonics)
    coefficient = jnp.concatenate([amplitude * jnp.sin(theta), amplitude * jnp.cos(theta)], 1)
    tone = jnp.dot(coefficient, table, precision=lax.Precision.HIGHEST, preferred_element_type=jnp.float32)
    noise = jax.random.normal(jax.random.fold_in(key, 35), (row_count, hop_len), jnp.float32)
    tilt = jax.random.uniform(jax.random.fold_in(key, 36), (piece_count,), jnp.float32, -0.8, 0.8)
    noise_gain = jnp.exp(jax.random.uniform(jax.random.fold_in(key, 37), (piece_count,), jnp.float32, math.log(0.25), math.log(0.75)))
    row_tilt = jnp.repeat(tilt, FR_DEV)[:, None]
    row_gain = jnp.repeat(noise_gain, FR_DEV)[:, None]
    shifted = jnp.concatenate([jnp.zeros((row_count, 1), jnp.float32), noise[:, :-1]], 1)
    colored = (noise + row_tilt * shifted) * row_gain
    values = jnp.clip(tone + colored, -6.0, 6.0)
    return values.reshape(BLOCKS, SUBS, FR_DEV * hop_len)


def draw_templates(key, part):
    values = positive_field(jax.random.fold_in(key, 11), RANK, BINS, 0.03, 0.3)
    return values


def draw_activations(key, part):
    values = positive_field(jax.random.fold_in(key, 21), RANK, FRAMES, 0.3, 3.0)
    return values


def setup_inputs(seed: int = 0) -> dict:
    keys = jax.random.split(jax.random.key(seed), 4)
    return {
        "signal": draw_signal(jax.random.fold_in(keys[3], 71), 0),
        "templates": draw_templates(jax.random.fold_in(keys[3], 71), 0),
        "activations": draw_activations(jax.random.fold_in(keys[3], 71), 0),
    }


PRECISE = lax.Precision.HIGHEST

def hann_window():
    positions = jnp.arange(FRAME_LEN, dtype=jnp.int32).astype(jnp.float32)
    return 0.5 - 0.5 * jnp.cos(2.0 * math.pi / FRAME_LEN * positions)

def magnitudes(signal):
    hop_len = FRAME_LEN // 2
    sample_rows = jnp.concatenate([signal.reshape(FRAMES, hop_len), jnp.zeros((1, hop_len), signal.dtype)], 0)
    window = hann_window()
    group_size = math.gcd(FRAMES, 64)

    def per_block(offset):
        first_half = lax.dynamic_slice_in_dim(sample_rows, offset, group_size, 0)
        second_half = lax.dynamic_slice_in_dim(sample_rows, offset + 1, group_size, 0)
        frames = jnp.concatenate([first_half, second_half], 1) * window
        transform = jnp.fft.rfft(frames, axis=1)[:, :BINS]
        real_part = jnp.real(transform)
        imag_part = jnp.imag(transform)
        magnitude = jnp.sqrt(real_part * real_part + imag_part * imag_part) * (8.0 / SPLIT)
        return magnitude.astype(jnp.float32)
    offsets = jnp.arange(FRAMES // group_size, dtype=jnp.int32) * group_size
    return lax.map(per_block, offsets).reshape(FRAMES, BINS)

def quotient(spectrum_rows, basis, act_block):
    approx = lax.dot_general(act_block, basis, (((0,), (0,)), ((), ())), precision=PRECISE, preferred_element_type=jnp.float32)
    return spectrum_rows / approx

def update_activity(spectrum, basis, activity):
    totals = lax.optimization_barrier(jnp.sum(basis, axis=1))

    def per_block(offset):
        act_block = lax.dynamic_slice_in_dim(activity, offset, BLK, 1)
        spectrum_rows = lax.dynamic_slice_in_dim(spectrum, offset, BLK, 0)
        ratio_rows = quotient(spectrum_rows, basis, act_block)
        numerator = lax.dot_general(basis, ratio_rows, (((1,), (1,)), ((), ())), precision=PRECISE, preferred_element_type=jnp.float32)
        return act_block * (numerator / totals[:, None])
    offsets = jnp.arange(FRAMES // BLK, dtype=jnp.int32) * BLK
    blocks = lax.map(per_block, offsets)
    return jnp.transpose(blocks, (1, 0, 2)).reshape(RANK, FRAMES)

def update_basis(spectrum, basis, activity):

    def accumulate(running, offset):
        act_block = lax.dynamic_slice_in_dim(activity, offset, BLK, 1)
        spectrum_rows = lax.dynamic_slice_in_dim(spectrum, offset, BLK, 0)
        ratio_rows = quotient(spectrum_rows, basis, act_block)
        return (running + jnp.dot(act_block, ratio_rows, precision=PRECISE, preferred_element_type=jnp.float32), None)
    offsets = jnp.arange(FRAMES // BLK, dtype=jnp.int32) * BLK
    numerator, unused = lax.scan(accumulate, jnp.zeros((RANK, BINS), jnp.float32), offsets)
    totals = lax.optimization_barrier(jnp.sum(activity, axis=1))
    return basis * (numerator / totals[:, None])

def reference(signal, templates, activations):
    spectrum = magnitudes(signal)
    middle = update_activity(spectrum, templates, activations)
    final_templates = update_basis(spectrum, templates, middle)
    final_activations = update_activity(spectrum, final_templates, middle)
    return (final_activations, final_templates)
```

```python
import math

import jax
import jax.numpy as jnp
import ml_dtypes
import numpy as np
from jax import lax
from jax.experimental import pallas as pl
from jax.experimental.pallas import tpu as pltpu
from jax.sharding import PartitionSpec as P

MESH = pl.DeviceIdType.MESH
F32 = jnp.float32
BF16 = jnp.bfloat16


def halves(table):
    high = table.astype(ml_dtypes.bfloat16)
    low = (table - high.astype(np.float64)).astype(ml_dtypes.bfloat16)
    return high, low


def build_tables():
    rows = np.arange(256)
    lanes = np.arange(128)
    m = (rows[:, None] * 128 + lanes[None, :]).astype(np.float64)
    window = (0.5 - 0.5 * np.cos(2 * math.pi / 65536 * m)).astype(np.float32)
    first = []
    twiddle = []
    for odd in (0, 1):
        k1 = 2 * np.arange(128) + odd
        angle = 2 * math.pi / 512 * (k1[:, None] * rows[None, :] % 512)
        real, imag = np.cos(angle), -np.sin(angle)
        if not odd:
            imag[0] = 1.0 - 2.0 * (rows % 2)
        first.append(np.concatenate([real, imag], 0))
        twiddle.append(2 * math.pi / 65536 * (k1[:, None] * lanes[None, :]))
    twiddle = np.concatenate(twiddle, 0)
    first = np.stack([np.stack(halves(part)) for part in first])
    second = []
    special = []
    lam = np.arange(128)
    z, x, rev, other = lam % 8, lam // 8 % 4, lam // 32 % 2, lam // 64
    for core in (0, 1):
        base = 8 * (2 * (z // 2) + (core ^ other)) + 4 * (z % 2) + x
        k2 = np.where(rev == 1, 127 - base, base)
        angle = 2 * math.pi / 128 * (lanes[:, None] * k2[None, :] % 128)
        cos, sin = np.cos(angle) / 32, np.sin(angle) / 32
        second.append(np.stack(halves(np.concatenate([np.concatenate([cos, -sin], 1), np.concatenate([sin, cos], 1)], 0))))
        angle = 2 * math.pi / 128 * (lanes[:, None] * (base + 0.5 * rev)[None, :])
        cos, sin = np.cos(angle) / 32, np.sin(angle) / 32
        keep, turn = (1 - rev)[None, :], rev[None, :]
        special.append(
            np.stack(
                halves(
                    np.concatenate(
                        [np.concatenate([cos * keep, -sin * keep], 1), np.concatenate([cos * turn, -sin * turn], 1)], 0
                    )
                )
            )
        )
    sigma = np.where(lanes < 64, 2 * lanes, 2 * (lanes - 64) + 1)
    perms = []
    for order in (sigma, (128 - sigma) % 128):
        perm = np.zeros((128, 128))
        perm[order, lanes] = 1.0
        perms += [perm, perm.T]
    perms = np.stack(perms).astype(ml_dtypes.bfloat16)
    return (
        window,
        np.cos(twiddle).astype(np.float32),
        np.sin(twiddle).astype(np.float32),
        first,
        np.stack(second),
        np.stack(special),
        perms,
    )


def split(value):
    high = value.astype(BF16)
    return high, (value - high.astype(F32)).astype(BF16)


def dot(a, b):
    return jnp.dot(a, b, preferred_element_type=F32)


def dot_t(a, b):
    return lax.dot_general(a, b, (((1,), (1,)), ((), ())), preferred_element_type=F32)


def moved(value, perm):
    high = value.astype(BF16)
    rest = value - high.astype(F32)
    middle = rest.astype(BF16)
    low = (rest - middle.astype(F32)).astype(BF16)
    return dot(high, perm) + dot(middle, perm) + dot(low, perm)


def doubled(value):
    high, low = split(value)
    lane = lax.broadcasted_iota(jnp.int32, value.shape, 1)
    both = jnp.where(lane < 64, high.astype(F32), low.astype(F32)).astype(BF16)
    return jnp.concatenate([both, both], 1)


def kernel(
    sig_hbm, templ, act, window, tcos, tsin, first, second, special, perms,
    out_act, out_templ,
    sigv, hg, ht, mag, zrow, mag0, sg, tsend, w, wn, num,
    r1a, r1b, r2a, r2b, q1a, q1b, q2a, q2b, rz,
    acc, sx, rx, sy, ry, tsx, trx, try_, trz, tsy, tsz, fin, fo,
    lsem, ssem, rsem,
):
    f = lax.axis_index("freq")
    t = lax.axis_index("frames")
    b = f % 2
    z_hi = f // 2
    z_lo = t // 16
    x = t // 4 % 4
    y = t % 4
    z = z_hi * 2 + z_lo
    partner = (f + 1 - 2 * b, t)

    def at_x(d):
        return (f, z_lo * 16 + (x + d) % 4 * 4 + y)

    def at_y(d):
        return (f, z_lo * 16 + x * 4 + (y + d) % 4)

    def at_z(d):
        other = (z + d) % 8
        return (other // 2 * 2 + b, other % 2 * 16 + x * 4 + y)

    def at_f(d):
        return ((f + d) % 8, t)

    def at_line(d):
        place = (t * 8 + f + d + 256) % 256
        return (place % 8, place // 8)

    greet = [partner] + [at_x(d) for d in (1, 2, 3)] + [at_y(d) for d in (1, 2, 3)]
    greet += [at_z(d) for d in range(1, 8)] + [at_f(d) for d in range(1, 8)] + [at_line(-1), at_line(1)]
    barrier = pltpu.get_barrier_semaphore()
    for device in greet:
        pl.semaphore_signal(barrier, inc=1, device_id=device, device_id_type=MESH)
    pl.semaphore_wait(barrier, len(greet))

    used = [0]

    def slot():
        used[0] += 1
        return used[0] - 1

    def remote(src, dst, index, device):
        return pltpu.make_async_remote_copy(
            src_ref=src, dst_ref=dst, send_sem=ssem.at[index], recv_sem=rsem.at[index],
            device_id=device, device_id_type=MESH,
        )

    loads = [
        pltpu.make_async_copy(sig_hbm.at[pl.ds(8 * i, 8)], sigv.at[pl.ds(8 * i, 8)], lsem.at[i]) for i in range(4)
    ]
    for load in loads:
        load.start()
    halo = remote(sig_hbm.at[0], sigv.at[32], slot(), at_line(-1))
    halo.start()
    h_copies = [remote(act, hg.at[f], slot(), at_f(d)) for d in range(1, 8)]
    for copy in h_copies:
        copy.start()
    hg[pl.ds(f, 1)] = act[...][None]

    flip = y // 2
    w[y, x, z] = moved(templ[...], perms[2 * flip])

    def gather_steps(buf):
        zc = [remote(buf.at[y, x, z], buf.at[y, x, z], slot(), at_z(d)) for d in range(1, 8)]
        lo, hi = pl.ds(0, 32), pl.ds(32, 32)

        def pair(region, right, left):
            return [remote(region, region, slot(), right), remote(region, region, slot(), left)]

        yl, yr, xl, xr = (y + 3) % 4, (y + 1) % 4, (x + 3) % 4, (x + 1) % 4
        a_own = buf.at[y, x, :, lo]
        b_own = buf.at[y, x, :, hi]
        p2s1 = pair(a_own, at_x(1), at_x(3)) + pair(b_own, at_y(1), at_y(3))

        def forward(to_right, right, to_left, left):
            return [remote(to_right, to_right, slot(), right), remote(to_left, to_left, slot(), left)]

        p2s2 = forward(buf.at[y, xl, pl.ds(0, 4), lo], at_x(1), buf.at[y, xr, pl.ds(4, 4), lo], at_x(3))
        p2s2 += forward(buf.at[yl, x, pl.ds(0, 4), hi], at_y(1), buf.at[yr, x, pl.ds(4, 4), hi], at_y(3))
        p3s1 = pair(buf.at[y, :, :, lo], at_y(1), at_y(3)) + pair(buf.at[:, x, :, hi], at_x(1), at_x(3))
        p3s2 = forward(buf.at[yl, pl.ds(0, 2), :, lo], at_y(1), buf.at[yr, pl.ds(2, 2), :, lo], at_y(3))
        p3s2 += forward(buf.at[pl.ds(0, 2), xl, :, hi], at_x(1), buf.at[pl.ds(2, 2), xr, :, hi], at_x(3))
        return [zc, p2s1, p2s2, p3s1, p3s2]

    def start(copies):
        for copy in copies:
            copy.start()

    def arrive(copies):
        for copy in copies:
            copy.wait_recv()

    def sent(copies):
        for copy in copies:
            copy.wait_send()

    w_steps = gather_steps(w)
    start(w_steps[0])
    s_slots = [slot() for _ in range(4)]

    def s_copy(group, index):
        return remote(tsend.at[group], sg.at[4 * b + group], index, partner)

    zrow[...] = jnp.zeros_like(zrow)

    def pair_step(group, p):
        n = group * 8 + 2 * p
        step = group * 4 + p
        for when, stage in ((1, 0), (3, 1), (5, 2), (12, 3)):
            @pl.when(step == when)
            def _(stage=stage):
                arrive(w_steps[stage])
                start(w_steps[stage + 1])

        win = window[...]
        h0, h1, h2 = sigv[n], sigv[n + 1], sigv[n + 2]
        a0, a1 = h0 * win, h1 * win
        b1, b2 = h1 - a1, h2 - h2 * win
        ev, ov = [], []
        for parity, block in ((0, jnp.concatenate([a0 + b1, a1 + b2], 1)), (1, jnp.concatenate([a0 - b1, a1 - b2], 1))):
            high, low = split(block)
            d_high, d_low = first[parity, 0], first[parity, 1]
            part = dot(d_high, high) + dot(d_high, low) + dot(d_low, high)
            (ev if parity == 0 else ov).append(part)
        pieces = []
        for frame in range(2):
            for parity, part in ((0, ev[0]), (1, ov[0])):
                real = part[:128, 128 * frame:128 * frame + 128]
                imag = part[128:, 128 * frame:128 * frame + 128]
                tc = tcos[128 * parity:128 * parity + 128, :]
                ts = tsin[128 * parity:128 * parity + 128, :]
                piece = jnp.concatenate([real * tc + imag * ts, imag * tc - real * ts], 1)
                if parity == 0:
                    zrow[pl.ds(2 * p + frame, 1), :] = piece[:1]
                pieces.append(piece)
        m_high, m_low = second[b, 0], second[b, 1]
        for frame in range(2):
            high, low = split(jnp.concatenate(pieces[2 * frame:2 * frame + 2], 0))
            out = dot(high, m_high) + dot(low, m_high) + dot(high, m_low)
            real, imag = out[:, :128], out[:, 128:]
            mag[2 * p + frame] = jnp.sqrt(real * real + imag * imag)

    lane = lax.broadcasted_iota(jnp.int32, (128, 128), 1)
    row = lax.broadcasted_iota(jnp.int32, (128, 128), 0)
    mirrored = lane // 32 % 2 == 1
    top = row == 0

    def turn(group, j):
        m = mag[j]
        low = jnp.concatenate([m[:64], m[128:192]], 0)
        high = jnp.concatenate([m[64:128], m[192:]], 0)
        extra = jnp.broadcast_to(mag0[pl.ds(j, 1), :], (128, 128))
        high_row = jnp.broadcast_to(high[:1], (128, 128))
        low = jnp.where(top, jnp.where(mirrored, high_row, extra), low)
        high = jnp.where(top & mirrored, extra, high)
        low, high = low.T, high.T
        for ref, index, off in ((sg, 4 * b + group, 0), (tsend, group, 64)):
            for value, place, part in ((low, 0, 0), (high, 1, 0), (high, 2, 1), (low, 3, 1)):
                ref[index, pl.ds(256 * place + j, 32, stride=8), :] = value[off + 32 * part:off + 32 * part + 32]

    def group_step(group, _):
        @pl.when(group == 0)
        def _():
            loads[0].wait()
            loads[1].wait()

        @pl.when(group == 1)
        def _():
            loads[2].wait()

        @pl.when(group == 2)
        def _():
            loads[3].wait()

        @pl.when(group == 3)
        def _():
            halo.wait_recv()
            sigv[32] = sigv[32] * jnp.where(t * 8 + f == 255, 0.0, 1.0)

        def body(p, _):
            pair_step(group, p)
            return 0

        lax.fori_loop(0, 4, body, 0)
        high, low = split(zrow[...])
        out = dot(high, special[b, 0]) + dot(low, special[b, 0]) + dot(high, special[b, 1])
        mag0[...] = jnp.sqrt(out[:, :128] * out[:, :128] + out[:, 128:] * out[:, 128:])

        def turn_body(j, _):
            turn(group, 2 * j)
            turn(group, 2 * j + 1)
            return 0

        lax.fori_loop(0, 4, turn_body, 0)
        for g in range(4):
            @pl.when(group == g)
            def _(g=g):
                s_copy(g, s_slots[g]).start()
        return 0

    lax.fori_loop(0, 4, group_step, 0)

    arrive(h_copies)
    rows64 = hg[...].reshape(64, 256)
    ht[...] = jnp.concatenate([rows64, rows64], 0).T
    h2 = ht[pl.ds(pl.multiple_of(64 * z_hi, 64), 64), :]
    arrive(w_steps[4])
    for g in range(4):
        s_copy(g, s_slots[g]).wait_recv()

    def frames_block(yy, xx):
        cols = []
        for k in range(8):
            place = pl.multiple_of(((yy * 4 + xx) * 8 + k) * 8, 8)
            cols.append(jnp.concatenate([sg[g, pl.ds(place, 8), :] for g in range(8)], 0))
        return jnp.concatenate(cols, 1)

    def ratio_of(buf, lhs, yy, xx):
        wide = jnp.concatenate([buf[yy, xx, k] for k in range(8)], 1)
        high, low = split(wide)
        approx = dot(lhs, jnp.concatenate([high, high, low, low], 0))
        return frames_block(yy, xx) / approx, high, low

    def gain_block(buf, lhs, yy, xx):
        ratio, high, low = ratio_of(buf, lhs, yy, xx)
        r_high, r_low = split(ratio)
        left = jnp.concatenate([r_high, r_low, jnp.ones((16, 1024), BF16)], 0)
        acc[...] += dot_t(left, jnp.concatenate([high, low], 0))

    def gain(stage, index):
        total = acc[...]
        part = jnp.concatenate([total[:64] + total[64:128], total[128:136]], 0)
        stage_send, stage_recv = stage
        stage_send[...] = part + pltpu.roll(part, 64, 1)
        copy = remote(stage_send, stage_recv, index, partner)
        copy.start()
        copy.wait_recv()
        both = stage_send[...] + stage_recv[...]
        return both[:64] / both[64:65], copy

    lhs1 = doubled(h2)
    acc[...] = jnp.zeros_like(acc)

    def first_body(i, _):
        gain_block(w, lhs1, i // 4, i % 4)
        return 0

    lax.fori_loop(0, 16, first_body, 0)
    gain1, mid_copy = gain((sx, rx), slot())
    mid = h2 * gain1
    mid_lhs = doubled(mid)
    mid_t = jnp.concatenate([mid, mid], 0).T
    mid_left = doubled(mid_t[:64])

    tsx[...] = jnp.broadcast_to(jnp.sum(mid, axis=0, keepdims=True), (8, 128))
    tx_copies = [remote(tsx, trx.at[d - 1], slot(), at_x(d)) for d in (1, 2, 3)]
    start(tx_copies)

    def num_block(yy, xx):
        ratio, _, _ = ratio_of(w, mid_lhs, yy, xx)
        high, low = split(ratio)
        out = dot(mid_left, jnp.concatenate([high, high, low, low], 0))
        for k in range(8):
            num[yy, xx, k] = out[:, 128 * k:128 * k + 128]

    lo, hi = pl.ds(0, 32), pl.ds(32, 32)
    yl, yr, yo = (y + 3) % 4, (y + 1) % 4, (y + 2) % 4
    xl, xr, xo = (x + 3) % 4, (x + 1) % 4, (x + 2) % 4

    def num_run(blocks):
        def body(i, _):
            dy, dx = blocks(i)
            num_block((y + dy) % 4, (x + dx) % 4)
            return 0
        return body

    def run(count, blocks):
        lax.fori_loop(0, count, num_run(blocks), 0)

    run(4, lambda i: (2, i))
    a1 = [
        remote(num.at[yo, pl.ds(0, 2), :, lo], r1a.at[0], slot(), at_y(1)),
        remote(num.at[yo, pl.ds(2, 2), :, lo], r1a.at[1], slot(), at_y(3)),
    ]
    start(a1)
    run(3, lambda i: ((i + 3) % 4, 2))
    b1 = [
        remote(num.at[pl.ds(0, 2), xo, :, hi], r1b.at[0], slot(), at_x(1)),
        remote(num.at[pl.ds(2, 2), xo, :, hi], r1b.at[1], slot(), at_x(3)),
    ]
    start(b1)
    run(3, lambda i: (1, (i + 3) % 4))
    run(3, lambda i: (3, (i + 3) % 4))

    def add_loop(count, fn):
        def body(i, _):
            fn(i)
            return 0
        lax.fori_loop(0, count, body, 0)

    arrive(a1)

    def add_a1(i):
        num[yr, i // 8, i % 8, lo] += r1a[0, i // 8, i % 8]
        num[yl, 2 + i // 8, i % 8, lo] += r1a[1, i // 8, i % 8]

    add_loop(16, add_a1)
    a2 = [
        remote(num.at[yr, :, :, lo], r2a.at[0], slot(), at_y(1)),
        remote(num.at[yl, :, :, lo], r2a.at[1], slot(), at_y(3)),
    ]
    start(a2)
    run(2, lambda i: (0, 1 + 2 * i))
    arrive(b1)

    def add_b1(i):
        num[i // 8, xr, i % 8, hi] += r1b[0, i // 8, i % 8]
        num[2 + i // 8, xl, i % 8, hi] += r1b[1, i // 8, i % 8]

    add_loop(16, add_b1)
    b2 = [
        remote(num.at[:, xr, :, hi], r2b.at[0], slot(), at_x(1)),
        remote(num.at[:, xl, :, hi], r2b.at[1], slot(), at_x(3)),
    ]
    start(b2)
    run(1, lambda i: (0, 0))

    arrive(tx_copies)
    tsy[...] = tsx[...] + trx[0] + trx[1] + trx[2]
    ty_copies = [remote(tsy, try_.at[d - 1], slot(), at_y(d)) for d in (1, 2, 3)]
    start(ty_copies)

    arrive(a2)

    def add_a2(i):
        num[y, i // 8, i % 8, lo] += r2a[0, i // 8, i % 8] + r2a[1, i // 8, i % 8]

    add_loop(32, add_a2)
    c1 = [
        remote(num.at[y, xo, pl.ds(0, 4), lo], q1a.at[0], slot(), at_x(1)),
        remote(num.at[y, xo, pl.ds(4, 4), lo], q1a.at[1], slot(), at_x(3)),
    ]
    start(c1)
    arrive(b2)

    def add_b2(i):
        num[i // 8, x, i % 8, hi] += r2b[0, i // 8, i % 8] + r2b[1, i // 8, i % 8]

    add_loop(32, add_b2)
    d1 = [
        remote(num.at[yo, x, pl.ds(0, 4), hi], q1b.at[0], slot(), at_y(1)),
        remote(num.at[yo, x, pl.ds(4, 4), hi], q1b.at[1], slot(), at_y(3)),
    ]
    start(d1)
    arrive(c1)

    def add_c1(i):
        num[y, xr, i, lo] += q1a[0, i]
        num[y, xl, 4 + i, lo] += q1a[1, i]

    add_loop(4, add_c1)
    c2 = [
        remote(num.at[y, xr, :, lo], q2a.at[0], slot(), at_x(1)),
        remote(num.at[y, xl, :, lo], q2a.at[1], slot(), at_x(3)),
    ]
    start(c2)
    arrive(d1)

    def add_d1(i):
        num[yr, x, i, hi] += q1b[0, i]
        num[yl, x, 4 + i, hi] += q1b[1, i]

    add_loop(4, add_d1)
    d2 = [
        remote(num.at[yr, x, :, hi], q2b.at[0], slot(), at_y(1)),
        remote(num.at[yl, x, :, hi], q2b.at[1], slot(), at_y(3)),
    ]
    start(d2)

    arrive(ty_copies)
    tsz[...] = tsy[...] + try_[0] + try_[1] + try_[2]
    tz_copies = [remote(tsz, trz.at[d - 1], slot(), at_z(d)) for d in range(1, 8)]
    start(tz_copies)

    arrive(c2)
    arrive(d2)

    def add_cd2(i):
        num[y, x, i, lo] += q2a[0, i] + q2a[1, i]
        num[y, x, i, hi] += q2b[0, i] + q2b[1, i]

    add_loop(8, add_cd2)
    z_copies = [remote(num.at[y, x, (z + d) % 8], rz.at[d - 1], slot(), at_z(d)) for d in range(1, 8)]
    start(z_copies)
    arrive(tz_copies)
    totals = tsz[...]
    for d in range(7):
        totals = totals + trz[d]
    totals = jnp.broadcast_to(totals[:1], (128, 128)).T[:64]
    arrive(z_copies)
    whole = num[y, x, z]
    for d in range(7):
        whole = whole + rz[d]
    wn[y, x, z] = w[y, x, z] * (whole / totals)

    n_steps = gather_steps(wn)
    start(n_steps[0])
    out_templ[...] = moved(wn[y, x, z], perms[2 * flip + 1])
    acc[...] = jnp.zeros_like(acc)
    for stage in range(3):
        arrive(n_steps[stage])
        start(n_steps[stage + 1])
    arrive(n_steps[3])
    start(n_steps[4])

    def near_body(i, _):
        gain_block(wn, mid_lhs, (y + 3 + i // 3) % 4, (x + 3 + i % 3) % 4)
        return 0

    lax.fori_loop(0, 9, near_body, 0)
    arrive(n_steps[4])

    def far_body(i, _):
        gain_block(wn, mid_lhs, (y + 2) % 4, i)
        return 0

    lax.fori_loop(0, 4, far_body, 0)

    def side_body(i, _):
        gain_block(wn, mid_lhs, (y + 3 + i) % 4, (x + 2) % 4)
        return 0

    lax.fori_loop(0, 3, side_body, 0)
    gain2, last_copy = gain((sy, ry), slot())
    final = mid * gain2
    fin[...] = jnp.concatenate([final, final], 0).T
    f_copies = []
    for d in range(1, 4):
        other = (z_hi + d) % 4 * 2 + b
        rows = pl.ds(pl.multiple_of(8 * other, 8), 8)
        f_copies.append(remote(fin.at[rows], fo.at[z_hi], slot(), (other, t)))
    start(f_copies)
    fo[pl.ds(z_hi, 1)] = fin[pl.ds(pl.multiple_of(8 * f, 8), 8), :][None]
    arrive(f_copies)
    near = lax.broadcasted_iota(jnp.int32, (8, 128), 1) < 64
    out_act[:, :128] = jnp.where(near, fo[0], fo[1])
    out_act[:, 128:] = jnp.where(near, fo[2], fo[3])

    sent([halo] + h_copies)
    for stage in w_steps + n_steps:
        sent(stage)
    for g in range(4):
        s_copy(g, s_slots[g]).wait_send()
    sent([mid_copy, last_copy] + tx_copies + ty_copies + tz_copies)
    sent(a1 + b1 + a2 + b2 + c1 + d1 + c2 + d2 + z_copies + f_copies)


COPIES = 120


def on_device(signal, templates, activations):
    tables = build_tables()
    vmem = pl.BlockSpec(memory_space=pltpu.VMEM)
    f32 = lambda *shape: pltpu.VMEM(shape, F32)
    return pl.pallas_call(
        kernel,
        out_shape=(jax.ShapeDtypeStruct((8, 256), F32), jax.ShapeDtypeStruct((64, 128), F32)),
        in_specs=[pl.BlockSpec(memory_space=pl.ANY)] + [vmem] * 9,
        out_specs=(vmem, vmem),
        scratch_shapes=[
            f32(33, 256, 128),
            f32(8, 8, 256),
            f32(256, 128),
            f32(8, 256, 128),
            f32(16, 256),
            f32(16, 128),
            f32(8, 1024, 128),
            f32(4, 1024, 128),
            f32(4, 4, 8, 64, 128),
            f32(4, 4, 8, 64, 128),
            f32(4, 4, 8, 64, 128),
            f32(2, 2, 8, 32, 128),
            f32(2, 2, 8, 32, 128),
            f32(2, 4, 8, 32, 128),
            f32(2, 4, 8, 32, 128),
            f32(2, 4, 32, 128),
            f32(2, 4, 32, 128),
            f32(2, 8, 32, 128),
            f32(2, 8, 32, 128),
            f32(7, 64, 128),
            f32(144, 128),
            f32(72, 128), f32(72, 128), f32(72, 128), f32(72, 128),
            f32(8, 128),
            f32(3, 8, 128), f32(3, 8, 128), f32(7, 8, 128),
            f32(8, 128), f32(8, 128),
            f32(128, 128),
            f32(4, 8, 128),
            pltpu.SemaphoreType.DMA((4,)),
            pltpu.SemaphoreType.DMA((COPIES,)),
            pltpu.SemaphoreType.DMA((COPIES,)),
        ],
        compiler_params=pltpu.CompilerParams(
            collective_id=0, has_side_effects=True, vmem_limit_bytes=60 * 1024 * 1024
        ),
    )(signal.reshape(32, 256, 128), templates, activations, *tables)


def solution(mesh):
    return jax.shard_map(
        on_device,
        mesh=mesh,
        in_specs=(P("frames", "freq", None), P(None, ("freq", "frames")), P("freq", "frames")),
        out_specs=(P("freq", "frames"), P(None, ("freq", "frames"))),
        check_vma=False,
    )
```

```python
import math

import jax
import jax.numpy as jnp
import ml_dtypes
import numpy as np
from jax import lax
from jax.experimental import pallas as pl
from jax.experimental.pallas import tpu as pltpu
from jax.sharding import PartitionSpec as P

MESH = pl.DeviceIdType.MESH
F32 = jnp.float32
BF16 = jnp.bfloat16


def halves(table):
    high = table.astype(ml_dtypes.bfloat16)
    low = (table - high.astype(np.float64)).astype(ml_dtypes.bfloat16)
    return high, low


def build_tables():
    rows = np.arange(256)
    lanes = np.arange(128)
    m = (rows[:, None] * 128 + lanes[None, :]).astype(np.float64)
    window = (0.5 - 0.5 * np.cos(2 * math.pi / 65536 * m)).astype(np.float32)
    first = []
    twiddle = []
    for odd in (0, 1):
        k1 = 2 * np.arange(128) + odd
        angle = 2 * math.pi / 512 * (k1[:, None] * rows[None, :] % 512)
        real, imag = np.cos(angle), -np.sin(angle)
        if not odd:
            imag[0] = 1.0 - 2.0 * (rows % 2)
        first.append(np.concatenate([real, imag], 0))
        twiddle.append(2 * math.pi / 65536 * (k1[:, None] * lanes[None, :]))
    twiddle = np.concatenate(twiddle, 0)
    first = np.stack([np.stack(halves(part)) for part in first])
    second = []
    special = []
    lam = np.arange(128)
    z, x, rev, other = lam % 8, lam // 8 % 4, lam // 32 % 2, lam // 64
    for core in (0, 1):
        base = 8 * (2 * (z // 2) + (core ^ other)) + 4 * (z % 2) + x
        k2 = np.where(rev == 1, 127 - base, base)
        angle = 2 * math.pi / 128 * (lanes[:, None] * k2[None, :] % 128)
        cos, sin = np.cos(angle) / 32, np.sin(angle) / 32
        second.append(np.stack(halves(np.concatenate([np.concatenate([cos, -sin], 1), np.concatenate([sin, cos], 1)], 0))))
        angle = 2 * math.pi / 128 * (lanes[:, None] * (base + 0.5 * rev)[None, :])
        cos, sin = np.cos(angle) / 32, np.sin(angle) / 32
        keep, turn = (1 - rev)[None, :], rev[None, :]
        special.append(
            np.stack(
                halves(
                    np.concatenate(
                        [np.concatenate([cos * keep, -sin * keep], 1), np.concatenate([cos * turn, -sin * turn], 1)], 0
                    )
                )
            )
        )
    sigma = np.where(lanes < 64, 2 * lanes, 2 * (lanes - 64) + 1)
    perms = []
    for order in (sigma, (128 - sigma) % 128):
        perm = np.zeros((128, 128))
        perm[order, lanes] = 1.0
        perms += [perm, perm.T]
    perms = np.stack(perms).astype(ml_dtypes.bfloat16)
    return (
        window,
        np.cos(twiddle).astype(np.float32),
        np.sin(twiddle).astype(np.float32),
        first,
        np.stack(second),
        np.stack(special),
        perms,
    )


def split(value):
    high = value.astype(BF16)
    return high, (value - high.astype(F32)).astype(BF16)


def dot(a, b):
    return jnp.dot(a, b, preferred_element_type=F32)


def dot_t(a, b):
    return lax.dot_general(a, b, (((1,), (1,)), ((), ())), preferred_element_type=F32)


def moved(value, perm):
    high = value.astype(BF16)
    rest = value - high.astype(F32)
    middle = rest.astype(BF16)
    low = (rest - middle.astype(F32)).astype(BF16)
    return dot(high, perm) + dot(middle, perm) + dot(low, perm)


def doubled(value):
    high, low = split(value)
    lane = lax.broadcasted_iota(jnp.int32, value.shape, 1)
    both = jnp.where(lane < 64, high.astype(F32), low.astype(F32)).astype(BF16)
    return jnp.concatenate([both, both], 1)


def kernel(
    sig_hbm, templ, act, window, tcos, tsin, first, second, special, perms,
    out_act, out_templ,
    sigv, hg, ht, mag, zrow, mag0, sg, tsend, w, wn, num,
    ha1, ha2, hb1, hb2, ma1, ma2, mb1, mb2, c1, c2, c3, c4, cyb, cxb, rz,
    acc, sx, rx, sy, ry, tsx, trx, try_, trz, tsy, tsz, fin, fo,
    lsem, ssem, rsem,
):
    f = lax.axis_index("freq")
    t = lax.axis_index("frames")
    b = f % 2
    z_hi = f // 2
    z_lo = t // 16
    x = t // 4 % 4
    y = t % 4
    z = z_hi * 2 + z_lo
    partner = (f + 1 - 2 * b, t)

    def at_x(d):
        return (f, z_lo * 16 + (x + d) % 4 * 4 + y)

    def at_y(d):
        return (f, z_lo * 16 + x * 4 + (y + d) % 4)

    def at_z(d):
        other = (z + d) % 8
        return (other // 2 * 2 + b, other % 2 * 16 + x * 4 + y)

    def at_f(d):
        return ((f + d) % 8, t)

    def at_line(d):
        place = (t * 8 + f + d + 256) % 256
        return (place % 8, place // 8)

    greet = [partner] + [at_x(d) for d in (1, 2, 3)] + [at_y(d) for d in (1, 2, 3)]
    greet += [at_z(d) for d in range(1, 8)] + [at_f(d) for d in range(1, 8)] + [at_line(-1), at_line(1)]
    barrier = pltpu.get_barrier_semaphore()
    for device in greet:
        pl.semaphore_signal(barrier, inc=1, device_id=device, device_id_type=MESH)
    pl.semaphore_wait(barrier, len(greet))

    used = [0]

    def slot():
        used[0] += 1
        return used[0] - 1

    def remote(src, dst, index, device):
        return pltpu.make_async_remote_copy(
            src_ref=src, dst_ref=dst, send_sem=ssem.at[index], recv_sem=rsem.at[index],
            device_id=device, device_id_type=MESH,
        )

    loads = [
        pltpu.make_async_copy(sig_hbm.at[pl.ds(8 * i, 8)], sigv.at[pl.ds(8 * i, 8)], lsem.at[i]) for i in range(4)
    ]
    for load in loads:
        load.start()
    halo = remote(sig_hbm.at[0], sigv.at[32], slot(), at_line(-1))
    halo.start()
    h_copies = [remote(act, hg.at[f], slot(), at_f(d)) for d in range(1, 8)]
    for copy in h_copies:
        copy.start()
    hg[pl.ds(f, 1)] = act[...][None]

    flip = y // 2
    w[y, x, z] = moved(templ[...], perms[2 * flip])

    lo, hi, low_rows = pl.ds(0, 24), pl.ds(24, 24), pl.ds(0, 48)
    end = pl.ds(48, 16)
    half = (pl.ds(0, 2), pl.ds(2, 2))
    quad = (pl.ds(0, 4), pl.ds(4, 4))
    every = slice(None)
    yl, yr, yo = (y + 3) % 4, (y + 1) % 4, (y + 2) % 4
    xl, xr, xo = (x + 3) % 4, (x + 1) % 4, (x + 2) % 4

    def same(region, device):
        return remote(region, region, slot(), device)

    class Gather:
        def __init__(self, buf):
            self.zc = [same(buf.at[y, x, z, low_rows], at_z(d)) for d in range(1, 8)]
            self.cx = [same(buf.at[y, x, z, end], at_x(d)) for d in (1, 2, 3)]
            self.cy = [same(buf.at[y, every, z, end], at_y(d)) for d in (1, 2, 3)]
            self.cz = []
            for k in range(4):
                right, left = (z + 8 - k) % 8, (z + k) % 8
                parts = ((0, 1), (1, 0)) if k < 3 else ((0,), (1,))
                ring = []
                for i in range(len(parts[0])):
                    ring.append(same(buf.at[half[parts[0][i]], every, right, end], at_z(1)))
                    ring.append(same(buf.at[half[parts[1][i]], every, left, end], at_z(7)))
                self.cz.append(ring)
            a_own, b_own = buf.at[y, x, every, lo], buf.at[y, x, every, hi]
            self.m1 = [same(a_own, at_x(1)), same(a_own, at_x(3)), same(b_own, at_y(1)), same(b_own, at_y(3))]
            self.m2 = [
                same(buf.at[y, xl, quad[0], lo], at_x(1)), same(buf.at[y, xr, quad[1], lo], at_x(3)),
                same(buf.at[yl, x, quad[0], hi], at_y(1)), same(buf.at[yr, x, quad[1], hi], at_y(3)),
            ]

            def heavy(first_half):
                right, left = (0, 1) if first_half else (1, 0)
                return [
                    same(buf.at[y, half[right], every, lo], at_y(1)), same(buf.at[y, half[left], every, lo], at_y(3)),
                    same(buf.at[half[right], x, every, hi], at_x(1)), same(buf.at[half[left], x, every, hi], at_x(3)),
                ]

            self.h1, self.h1b = heavy(True), heavy(False)
            self.h2 = [
                same(buf.at[yl, half[0], every, lo], at_y(1)), same(buf.at[yr, half[1], every, lo], at_y(3)),
                same(buf.at[half[0], xl, every, hi], at_x(1)), same(buf.at[half[1], xr, every, hi], at_x(3)),
            ]

        def event(self, k):
            if k == 0:
                start(self.cx)
                start(self.zc)
            elif k == 1:
                arrive(self.cx)
                start(self.cy)
            elif k == 2:
                arrive(self.zc)
                start(self.m1)
            elif k == 3:
                arrive(self.cy)
                start(self.cz[0])
            elif k == 4:
                arrive(self.m1)
                start(self.m2)
            elif k == 5:
                self.ring(1)
            elif k == 6:
                arrive(self.m2)
                start(self.h1)
                start(self.h1b)
            elif k == 7:
                self.ring(2)
            elif k == 8:
                arrive(self.h1)
                start(self.h2)
            elif k == 9:
                self.ring(3)
            elif k == 10:
                arrive(self.cz[3])
                arrive(self.h1b)
            else:
                arrive(self.h2)

        def ring(self, k):
            for i in range(0, 4, 2):
                arrive(self.cz[k - 1][i:i + 2])
                start(self.cz[k][i:i + 2])

        def all_sent(self):
            for copies in [self.zc, self.cx, self.cy] + self.cz + [self.m1, self.m2, self.h1, self.h1b, self.h2]:
                sent(copies)

    def start(copies):
        for copy in copies:
            copy.start()

    def arrive(copies):
        for copy in copies:
            copy.wait_recv()

    def sent(copies):
        for copy in copies:
            copy.wait_send()

    w_gather = Gather(w)
    w_gather.event(0)
    s_slots = [slot() for _ in range(4)]

    def s_copy(group, index):
        return remote(tsend.at[group], sg.at[4 * b + group], index, partner)

    zrow[...] = jnp.zeros_like(zrow)

    def pair_step(group, p):
        n = group * 8 + 2 * p
        step = group * 4 + p
        for when, event in ((3, 1), (6, 2), (7, 3), (10, 4), (12, 5), (14, 6)):
            @pl.when(step == when)
            def _(event=event):
                w_gather.event(event)

        win = window[...]
        h0, h1, h2 = sigv[n], sigv[n + 1], sigv[n + 2]
        a0, a1 = h0 * win, h1 * win
        b1, b2 = h1 - a1, h2 - h2 * win
        ev, ov = [], []
        for parity, block in ((0, jnp.concatenate([a0 + b1, a1 + b2], 1)), (1, jnp.concatenate([a0 - b1, a1 - b2], 1))):
            high, low = split(block)
            d_high, d_low = first[parity, 0], first[parity, 1]
            part = dot(d_high, high) + dot(d_high, low) + dot(d_low, high)
            (ev if parity == 0 else ov).append(part)
        pieces = []
        for frame in range(2):
            for parity, part in ((0, ev[0]), (1, ov[0])):
                real = part[:128, 128 * frame:128 * frame + 128]
                imag = part[128:, 128 * frame:128 * frame + 128]
                tc = tcos[128 * parity:128 * parity + 128, :]
                ts = tsin[128 * parity:128 * parity + 128, :]
                piece = jnp.concatenate([real * tc + imag * ts, imag * tc - real * ts], 1)
                if parity == 0:
                    zrow[pl.ds(2 * p + frame, 1), :] = piece[:1]
                pieces.append(piece)
        m_high, m_low = second[b, 0], second[b, 1]
        for frame in range(2):
            high, low = split(jnp.concatenate(pieces[2 * frame:2 * frame + 2], 0))
            out = dot(high, m_high) + dot(low, m_high) + dot(high, m_low)
            real, imag = out[:, :128], out[:, 128:]
            mag[2 * p + frame] = jnp.sqrt(real * real + imag * imag)

    lane = lax.broadcasted_iota(jnp.int32, (128, 128), 1)
    row = lax.broadcasted_iota(jnp.int32, (128, 128), 0)
    mirrored = lane // 32 % 2 == 1
    top = row == 0

    def turn(group, j):
        m = mag[j]
        low = jnp.concatenate([m[:64], m[128:192]], 0)
        high = jnp.concatenate([m[64:128], m[192:]], 0)
        extra = jnp.broadcast_to(mag0[pl.ds(j, 1), :], (128, 128))
        high_row = jnp.broadcast_to(high[:1], (128, 128))
        low = jnp.where(top, jnp.where(mirrored, high_row, extra), low)
        high = jnp.where(top & mirrored, extra, high)
        low, high = low.T, high.T
        for ref, index, off in ((sg, 4 * b + group, 0), (tsend, group, 64)):
            for value, place, part in ((low, 0, 0), (high, 1, 0), (high, 2, 1), (low, 3, 1)):
                ref[index, pl.ds(256 * place + j, 32, stride=8), :] = value[off + 32 * part:off + 32 * part + 32]

    def group_step(group, _):
        @pl.when(group == 0)
        def _():
            loads[0].wait()
            loads[1].wait()

        @pl.when(group == 1)
        def _():
            loads[2].wait()

        @pl.when(group == 2)
        def _():
            loads[3].wait()

        @pl.when(group == 3)
        def _():
            halo.wait_recv()
            sigv[32] = sigv[32] * jnp.where(t * 8 + f == 255, 0.0, 1.0)

        def body(p, _):
            pair_step(group, p)
            return 0

        lax.fori_loop(0, 4, body, 0)
        high, low = split(zrow[...])
        out = dot(high, special[b, 0]) + dot(low, special[b, 0]) + dot(high, special[b, 1])
        mag0[...] = jnp.sqrt(out[:, :128] * out[:, :128] + out[:, 128:] * out[:, 128:])

        def turn_body(j, _):
            turn(group, 2 * j)
            turn(group, 2 * j + 1)
            return 0

        lax.fori_loop(0, 4, turn_body, 0)
        for g in range(4):
            @pl.when(group == g)
            def _(g=g):
                s_copy(g, s_slots[g]).start()
        return 0

    lax.fori_loop(0, 4, group_step, 0)

    arrive(h_copies)
    rows64 = hg[...].reshape(64, 256)
    ht[...] = jnp.concatenate([rows64, rows64], 0).T
    h2 = ht[pl.ds(pl.multiple_of(64 * z_hi, 64), 64), :]
    for g in range(4):
        s_copy(g, s_slots[g]).wait_recv()

    def frames_block(yy, xx):
        cols = []
        for k in range(8):
            place = pl.multiple_of(((yy * 4 + xx) * 8 + k) * 8, 8)
            cols.append(jnp.concatenate([sg[g, pl.ds(place, 8), :] for g in range(8)], 0))
        return jnp.concatenate(cols, 1)

    def ratio_of(buf, lhs, yy, xx):
        wide = jnp.concatenate([buf[yy, xx, k] for k in range(8)], 1)
        high, low = split(wide)
        approx = dot(lhs, jnp.concatenate([high, high, low, low], 0))
        return frames_block(yy, xx) / approx, high, low

    def gain_block(buf, lhs, yy, xx):
        ratio, high, low = ratio_of(buf, lhs, yy, xx)
        r_high, r_low = split(ratio)
        left = jnp.concatenate([r_high, r_low, jnp.ones((16, 1024), BF16)], 0)
        acc[...] += dot_t(left, jnp.concatenate([high, low], 0))

    def gain(stage, index):
        total = acc[...]
        part = jnp.concatenate([total[:64] + total[64:128], total[128:136]], 0)
        stage_send, stage_recv = stage
        stage_send[...] = part + pltpu.roll(part, 64, 1)
        copy = remote(stage_send, stage_recv, index, partner)
        copy.start()
        copy.wait_recv()
        both = stage_send[...] + stage_recv[...]
        return both[:64] / both[64:65], copy

    lhs1 = doubled(h2)
    acc[...] = jnp.zeros_like(acc)

    def gain_all(buf, lhs, gather):
        def near_body(i, _):
            gain_block(buf, lhs, (y + 3 + i // 3) % 4, (x + 3 + i % 3) % 4)
            return 0

        def far_body(i, _):
            gain_block(buf, lhs, (y + 2) % 4, i)
            return 0

        def side_body(i, _):
            gain_block(buf, lhs, (y + 3 + i) % 4, (x + 2) % 4)
            return 0

        gather.event(10)
        lax.fori_loop(0, 9, near_body, 0)
        gather.event(11)
        lax.fori_loop(0, 4, far_body, 0)
        lax.fori_loop(0, 3, side_body, 0)

    for event in (7, 8, 9):
        w_gather.event(event)
    gain_all(w, lhs1, w_gather)
    gain1, mid_copy = gain((sx, rx), slot())
    mid = h2 * gain1
    mid_lhs = doubled(mid)
    mid_t = jnp.concatenate([mid, mid], 0).T
    mid_left = doubled(mid_t[:64])

    tsx[...] = jnp.broadcast_to(jnp.sum(mid, axis=0, keepdims=True), (8, 128))
    tx_copies = [remote(tsx, trx.at[d - 1], slot(), at_x(d)) for d in (1, 2, 3)]
    start(tx_copies)

    def num_block(yy, xx):
        ratio, _, _ = ratio_of(w, mid_lhs, yy, xx)
        high, low = split(ratio)
        out = dot(mid_left, jnp.concatenate([high, high, low, low], 0))
        for k in range(8):
            num[yy, xx, k] = out[:, 128 * k:128 * k + 128]

    def num_run(blocks):
        def body(i, _):
            dy, dx = blocks(i)
            num_block((y + dy) % 4, (x + dx) % 4)
            return 0
        return body

    def run(count, blocks):
        lax.fori_loop(0, count, num_run(blocks), 0)

    class Reduce4:
        def __init__(self, get, once, twice, places, right, left):
            own, right_place, left_place, far = places
            self.get, self.once, self.twice, self.places = get, once, twice, places

            def to(buf, side, part):
                return buf.at[side] if part is None else buf.at[side, part]

            self.first = [
                remote(get(far, 0), once.at[0], slot(), right), remote(get(far, 1), once.at[1], slot(), left),
            ]
            size = once.shape[1]
            parts = (pl.ds(0, size), pl.ds(size, size))
            self.early = [
                remote(get(right_place, 1), to(twice, 0, parts[1]), slot(), right),
                remote(get(left_place, 0), to(twice, 1, parts[0]), slot(), left),
            ]
            self.late = [
                remote(get(right_place, 0), to(twice, 0, parts[0]), slot(), right),
                remote(get(left_place, 1), to(twice, 1, parts[1]), slot(), left),
            ]

        def pass_on(self):
            own, right_place, left_place, far = self.places
            arrive(self.first)
            target = self.get(right_place, 0)
            target[...] = target[...] + self.once[0]
            target = self.get(left_place, 1)
            target[...] = target[...] + self.once[1]
            start(self.late)

        def finish(self):
            arrive(self.early)
            arrive(self.late)
            target = self.get(self.places[0], None)
            target[...] = target[...] + (self.twice[0] + self.twice[1])

        def all_sent(self):
            sent(self.first + self.early + self.late)

    def pick(parts, part):
        return every if part is None else parts[part]

    y_places, x_places = (y, yr, yl, yo), (x, xr, xl, xo)
    ra = Reduce4(lambda i, p: num.at[i, pick(half, p), every, lo], ha1, ha2, y_places, at_y(1), at_y(3))
    rb = Reduce4(lambda i, p: num.at[pick(half, p), i, every, hi], hb1, hb2, x_places, at_x(1), at_x(3))
    na = Reduce4(lambda i, p: num.at[y, i, pick(quad, p), lo], ma1, ma2, x_places, at_x(1), at_x(3))
    nb = Reduce4(lambda i, p: num.at[i, x, pick(quad, p), hi], mb1, mb2, y_places, at_y(1), at_y(3))

    run(4, lambda i: (2, i))
    start(ra.first)
    run(3, lambda i: ((i + 3) % 4, 2))
    start(rb.first)
    run(3, lambda i: (1, (i + 3) % 4))
    run(3, lambda i: (3, (i + 3) % 4))
    start(ra.early)
    run(2, lambda i: (0, 1 + 2 * i))
    start(rb.early)
    run(1, lambda i: (0, 0))

    def zz(d):
        return (z + 8 + d) % 8

    ring1 = [
        remote(num.at[half[0], every, zz(4), end], c1.at[0], slot(), at_z(1)),
        remote(num.at[half[1], every, zz(4), end], c1.at[1], slot(), at_z(7)),
    ]
    start(ring1)

    def ring_send(buf, d):
        copies = [
            remote(num.at[every, every, zz(d), end], buf.at[0], slot(), at_z(1)),
            remote(num.at[every, every, zz(-d), end], buf.at[1], slot(), at_z(7)),
        ]
        start(copies)
        return copies

    def ring_add(buf, d):
        for side, place in ((0, zz(d)), (1, zz(-d))):
            target = num.at[every, every, place, end]
            target[...] = target[...] + buf[side]

    arrive(tx_copies)
    tsy[...] = tsx[...] + trx[0] + trx[1] + trx[2]
    ty_copies = [remote(tsy, try_.at[d - 1], slot(), at_y(d)) for d in (1, 2, 3)]
    start(ty_copies)
    arrive(ring1)
    for side, place in ((0, zz(3)), (1, zz(-3))):
        target = num.at[half[side], every, place, end]
        target[...] = target[...] + c1[side]
    ring2 = ring_send(c2, 3)
    ra.pass_on()
    rb.pass_on()
    arrive(ty_copies)
    tsz[...] = tsy[...] + try_[0] + try_[1] + try_[2]
    tz_copies = [remote(tsz, trz.at[d - 1], slot(), at_z(d)) for d in range(1, 8)]
    start(tz_copies)
    arrive(ring2)
    ring_add(c2, 2)
    ring3 = ring_send(c3, 2)
    arrive(ring3)
    ring_add(c3, 1)
    ring4 = ring_send(c4, 1)
    ra.finish()
    start(na.first + na.early)
    rb.finish()
    start(nb.first + nb.early)
    arrive(ring4)
    target = num.at[every, every, z, end]
    target[...] = target[...] + (c4[0] + c4[1])
    cy_copies = [remote(num.at[(y + d) % 4, every, z, end], cyb.at[d - 1], slot(), at_y(d)) for d in (1, 2, 3)]
    start(cy_copies)
    na.pass_on()
    nb.pass_on()
    arrive(tz_copies)
    totals = tsz[...]
    for d in range(7):
        totals = totals + trz[d]
    totals = jnp.broadcast_to(totals[:1], (128, 128)).T[:64]
    arrive(cy_copies)
    target = num.at[y, every, z, end]
    target[...] = target[...] + (cyb[0] + cyb[1] + cyb[2])
    cx_copies = [remote(num.at[y, (x + d) % 4, z, end], cxb.at[d - 1], slot(), at_x(d)) for d in (1, 2, 3)]
    start(cx_copies)
    na.finish()
    nb.finish()
    z_copies = [remote(num.at[y, x, zz(d), low_rows], rz.at[d - 1], slot(), at_z(d)) for d in range(1, 8)]
    start(z_copies)
    arrive(cx_copies)
    whole = num[y, x, z, end] + (cxb[0] + cxb[1] + cxb[2])
    wn[y, x, z, end] = w[y, x, z, end] * (whole / totals[48:])
    n_gather = Gather(wn)
    start(n_gather.cx)
    arrive(z_copies)
    whole = num[y, x, z, low_rows]
    for d in range(7):
        whole = whole + rz[d]
    wn[y, x, z, low_rows] = w[y, x, z, low_rows] * (whole / totals[:48])
    start(n_gather.zc)

    out_templ[...] = moved(wn[y, x, z], perms[2 * flip + 1])
    acc[...] = jnp.zeros_like(acc)
    for event in (1, 3, 2, 5, 4, 6, 7, 8, 9):
        n_gather.event(event)
    gain_all(wn, mid_lhs, n_gather)
    gain2, last_copy = gain((sy, ry), slot())
    final = mid * gain2
    fin[...] = jnp.concatenate([final, final], 0).T
    f_copies = []
    for d in range(1, 4):
        other = (z_hi + d) % 4 * 2 + b
        rows = pl.ds(pl.multiple_of(8 * other, 8), 8)
        f_copies.append(remote(fin.at[rows], fo.at[z_hi], slot(), (other, t)))
    start(f_copies)
    fo[pl.ds(z_hi, 1)] = fin[pl.ds(pl.multiple_of(8 * f, 8), 8), :][None]
    arrive(f_copies)
    near = lax.broadcasted_iota(jnp.int32, (8, 128), 1) < 64
    out_act[:, :128] = jnp.where(near, fo[0], fo[1])
    out_act[:, 128:] = jnp.where(near, fo[2], fo[3])

    sent([halo] + h_copies)
    w_gather.all_sent()
    n_gather.all_sent()
    for g in range(4):
        s_copy(g, s_slots[g]).wait_send()
    sent([mid_copy, last_copy] + tx_copies + ty_copies + tz_copies)
    for part in (ra, rb, na, nb):
        part.all_sent()
    sent(ring1 + ring2 + ring3 + ring4 + cy_copies + cx_copies + z_copies + f_copies)


COPIES = 180


def on_device(signal, templates, activations):
    tables = build_tables()
    vmem = pl.BlockSpec(memory_space=pltpu.VMEM)
    f32 = lambda *shape: pltpu.VMEM(shape, F32)
    return pl.pallas_call(
        kernel,
        out_shape=(jax.ShapeDtypeStruct((8, 256), F32), jax.ShapeDtypeStruct((64, 128), F32)),
        in_specs=[pl.BlockSpec(memory_space=pl.ANY)] + [vmem] * 9,
        out_specs=(vmem, vmem),
        scratch_shapes=[
            f32(33, 256, 128),
            f32(8, 8, 256),
            f32(256, 128),
            f32(8, 256, 128),
            f32(16, 256),
            f32(16, 128),
            f32(8, 1024, 128),
            f32(4, 1024, 128),
            f32(4, 4, 8, 64, 128),
            f32(4, 4, 8, 64, 128),
            f32(4, 4, 8, 64, 128),
            f32(2, 2, 8, 24, 128),
            f32(2, 4, 8, 24, 128),
            f32(2, 2, 8, 24, 128),
            f32(2, 4, 8, 24, 128),
            f32(2, 4, 24, 128),
            f32(2, 8, 24, 128),
            f32(2, 4, 24, 128),
            f32(2, 8, 24, 128),
            f32(2, 2, 4, 16, 128),
            f32(2, 4, 4, 16, 128),
            f32(2, 4, 4, 16, 128),
            f32(2, 4, 4, 16, 128),
            f32(3, 4, 16, 128),
            f32(3, 16, 128),
            f32(7, 48, 128),
            f32(144, 128),
            f32(72, 128), f32(72, 128), f32(72, 128), f32(72, 128),
            f32(8, 128),
            f32(3, 8, 128), f32(3, 8, 128), f32(7, 8, 128),
            f32(8, 128), f32(8, 128),
            f32(128, 128),
            f32(4, 8, 128),
            pltpu.SemaphoreType.DMA((4,)),
            pltpu.SemaphoreType.DMA((COPIES,)),
            pltpu.SemaphoreType.DMA((COPIES,)),
        ],
        compiler_params=pltpu.CompilerParams(
            collective_id=0, has_side_effects=True, vmem_limit_bytes=60 * 1024 * 1024
        ),
    )(signal.reshape(32, 256, 128), templates, activations, *tables)


def solution(mesh):
    return jax.shard_map(
        on_device,
        mesh=mesh,
        in_specs=(P("frames", "freq", None), P(None, ("freq", "frames")), P("freq", "frames")),
        out_specs=(P("freq", "frames"), P(None, ("freq", "frames"))),
        check_vma=False,
    )
```

```python
import math

import jax
import jax.numpy as jnp
import ml_dtypes
import numpy as np
from jax import lax
from jax.experimental import pallas as pl
from jax.experimental.pallas import tpu as pltpu
from jax.sharding import PartitionSpec as P

MESH = pl.DeviceIdType.MESH
F32 = jnp.float32
BF16 = jnp.bfloat16


def halves(table):
    high = table.astype(ml_dtypes.bfloat16)
    low = (table - high.astype(np.float64)).astype(ml_dtypes.bfloat16)
    return high, low


def build_tables():
    rows = np.arange(256)
    lanes = np.arange(128)
    m = (rows[:, None] * 128 + lanes[None, :]).astype(np.float64)
    window = (0.5 - 0.5 * np.cos(2 * math.pi / 65536 * m)).astype(np.float32)
    first = []
    twiddle = []
    for odd in (0, 1):
        k1 = 2 * np.arange(128) + odd
        angle = 2 * math.pi / 512 * (k1[:, None] * rows[None, :] % 512)
        real, imag = np.cos(angle), -np.sin(angle)
        if not odd:
            imag[0] = 1.0 - 2.0 * (rows % 2)
        first.append(np.concatenate([real, imag], 0))
        twiddle.append(2 * math.pi / 65536 * (k1[:, None] * lanes[None, :]))
    twiddle = np.concatenate(twiddle, 0)
    first = np.stack([np.stack(halves(part)) for part in first])
    second = []
    special = []
    lam = np.arange(128)
    z, x, rev, other = lam % 8, lam // 8 % 4, lam // 32 % 2, lam // 64
    for core in (0, 1):
        base = 8 * (2 * (z // 2) + (core ^ other)) + 4 * (z % 2) + x
        k2 = np.where(rev == 1, 127 - base, base)
        angle = 2 * math.pi / 128 * (lanes[:, None] * k2[None, :] % 128)
        cos, sin = np.cos(angle) / 32, np.sin(angle) / 32
        second.append(np.stack(halves(np.concatenate([np.concatenate([cos, -sin], 1), np.concatenate([sin, cos], 1)], 0))))
        angle = 2 * math.pi / 128 * (lanes[:, None] * (base + 0.5 * rev)[None, :])
        cos, sin = np.cos(angle) / 32, np.sin(angle) / 32
        keep, turn = (1 - rev)[None, :], rev[None, :]
        special.append(
            np.stack(
                halves(
                    np.concatenate(
                        [np.concatenate([cos * keep, -sin * keep], 1), np.concatenate([cos * turn, -sin * turn], 1)], 0
                    )
                )
            )
        )
    sigma = np.where(lanes < 64, 2 * lanes, 2 * (lanes - 64) + 1)
    perms = []
    for order in (sigma, (128 - sigma) % 128):
        perm = np.zeros((128, 128))
        perm[order, lanes] = 1.0
        perms += [perm, perm.T]
    perms = np.stack(perms).astype(ml_dtypes.bfloat16)
    return (
        window,
        np.cos(twiddle).astype(np.float32),
        np.sin(twiddle).astype(np.float32),
        first,
        np.stack(second),
        np.stack(special),
        perms,
    )


def split(value):
    high = value.astype(BF16)
    return high, (value - high.astype(F32)).astype(BF16)


def dot(a, b):
    return jnp.dot(a, b, preferred_element_type=F32)


def dot_t(a, b):
    return lax.dot_general(a, b, (((1,), (1,)), ((), ())), preferred_element_type=F32)


def moved(value, perm):
    high = value.astype(BF16)
    rest = value - high.astype(F32)
    middle = rest.astype(BF16)
    low = (rest - middle.astype(F32)).astype(BF16)
    return dot(high, perm) + dot(middle, perm) + dot(low, perm)


def doubled(value):
    high, low = split(value)
    lane = lax.broadcasted_iota(jnp.int32, value.shape, 1)
    both = jnp.where(lane < 64, high.astype(F32), low.astype(F32)).astype(BF16)
    return jnp.concatenate([both, both], 1)


def kernel(
    sig_hbm, templ, act, window, tcos, tsin, first, second, special, perms,
    out_act, out_templ,
    sigv, hg, ht, mag, zrow, mag0, sg, tsend, w, wn, num,
    ha1, ha2, hb1, hb2, ma1, ma2, mb1, mb2, c1, c2, c3, c4, cyb, cxb, rz,
    acc, sx, rx, sy, ry, tsx, trx, try_, trz, tsy, tsz, fin, fo,
    lsem, ssem, rsem,
):
    f = lax.axis_index("freq")
    t = lax.axis_index("frames")
    b = f % 2
    z_hi = f // 2
    z_lo = t // 16
    x = t // 4 % 4
    y = t % 4
    z = z_hi * 2 + z_lo
    partner = (f + 1 - 2 * b, t)

    def at_x(d):
        return (f, z_lo * 16 + (x + d) % 4 * 4 + y)

    def at_y(d):
        return (f, z_lo * 16 + x * 4 + (y + d) % 4)

    def at_z(d):
        other = (z + d) % 8
        return (other // 2 * 2 + b, other % 2 * 16 + x * 4 + y)

    def at_line(d):
        place = (t * 8 + f + d + 256) % 256
        return (place % 8, place // 8)

    greet = [partner] + [at_x(d) for d in (1, 2, 3)] + [at_y(d) for d in (1, 2, 3)]
    greet += [at_z(d) for d in range(1, 8)] + [at_line(-1), at_line(1)]
    barrier = pltpu.get_barrier_semaphore()
    for device in greet:
        pl.semaphore_signal(barrier, inc=1, device_id=device, device_id_type=MESH)
    loads = [
        pltpu.make_async_copy(sig_hbm.at[pl.ds(8 * i, 8)], sigv.at[pl.ds(8 * i, 8)], lsem.at[i]) for i in range(4)
    ]
    for load in loads:
        load.start()
    flip = y // 2
    w[y, x, z] = moved(templ[...], perms[2 * flip])
    hg[pl.ds(f, 1)] = act[...][None]
    zrow[...] = jnp.zeros_like(zrow)
    pl.semaphore_wait(barrier, len(greet))

    used = [0]

    def slot():
        used[0] += 1
        return used[0] - 1

    def remote(src, dst, index, device):
        return pltpu.make_async_remote_copy(
            src_ref=src, dst_ref=dst, send_sem=ssem.at[index], recv_sem=rsem.at[index],
            device_id=device, device_id_type=MESH,
        )

    class Group:
        def __init__(self, index, like, *copies):
            self.index, self.like = index, like
            self.copies = [remote(src, dst, index, device) for src, dst, device in copies]

        def start(self, *which):
            for i in which or range(len(self.copies)):
                self.copies[i].start()

        def arrive(self):
            pltpu.make_async_copy(self.like, self.like, rsem.at[self.index]).wait()

        def sent(self):
            pltpu.make_async_copy(self.like, self.like, ssem.at[self.index]).wait()

    groups = []

    def group(like, *copies):
        groups.append(Group(slot(), like, *copies))
        return groups[-1]

    halo = remote(sig_hbm.at[0], sigv.at[32], slot(), at_line(-1))
    halo.start()
    h_far = group(hg.at[pl.ds(0, 3)], *[(act, hg.at[f], at_z(d)) for d in (2, 4, 6)])
    h_near = group(hg.at[0], (act, hg.at[f], partner))
    h_pass = group(hg.at[pl.ds(0, 3)], *[(hg.at[(f + d) % 8], hg.at[(f + d) % 8], partner) for d in (2, 4, 6)])
    h_far.start()
    h_near.start()

    lo, hi, low_rows = pl.ds(0, 24), pl.ds(24, 24), pl.ds(0, 48)
    end = pl.ds(48, 16)
    half = (pl.ds(0, 2), pl.ds(2, 2))
    quad = (pl.ds(0, 4), pl.ds(4, 4))
    every = slice(None)
    yl, yr, yo = (y + 3) % 4, (y + 1) % 4, (y + 2) % 4
    xl, xr, xo = (x + 3) % 4, (x + 1) % 4, (x + 2) % 4

    def start(copies):
        for copy in copies:
            copy.start()

    def arrive(copies):
        for copy in copies:
            copy.wait_recv()

    def sent(copies):
        for copy in copies:
            copy.wait_send()

    gather_slots = [slot() for _ in range(18)]

    class Gather:
        def __init__(self, buf):
            count = [0]

            def stage(like, *moves):
                count[0] += 1
                return Group(gather_slots[count[0] - 1], like, *[(region, region, device) for region, device in moves])

            up, down, right, left = at_y(1), at_y(3), at_x(1), at_x(3)
            self.zc = stage(rz, *[(buf.at[y, x, z, low_rows], at_z(d)) for d in range(1, 8)])
            self.cx = stage(cxb, *[(buf.at[y, x, z, end], at_x(d)) for d in (1, 2, 3)])
            self.cy = stage(cyb, *[(buf.at[y, every, z, end], at_y(d)) for d in (1, 2, 3)])
            self.cz = []
            for k in range(4):
                after, before = (z + 8 - k) % 8, (z + k) % 8
                ring = []
                for p, q in ((0, 1), (1, 0)) if k < 3 else ((0, 1),):
                    ring.append(stage(
                        c1, (buf.at[half[p], every, after, end], at_z(1)), (buf.at[half[q], every, before, end], at_z(7)),
                    ))
                self.cz.append(ring)
            two, four = buf.at[0, pl.ds(0, 2), every, lo], buf.at[0, every, every, lo]
            eight = buf.at[pl.ds(0, 2), every, every, lo]
            a_own, b_own = buf.at[y, x, every, lo], buf.at[y, x, every, hi]
            self.m1 = stage(four, (a_own, right), (a_own, left), (b_own, up), (b_own, down))
            self.m2 = stage(
                two,
                (buf.at[y, xl, quad[0], lo], right), (buf.at[y, xr, quad[1], lo], left),
                (buf.at[yl, x, quad[0], hi], up), (buf.at[yr, x, quad[1], hi], down),
            )
            self.hp = stage(four, (a_own, up), (a_own, down), (b_own, right), (b_own, left))

            def bulk(xx, yy):
                a_part, b_part = buf.at[y, xx, every, lo], buf.at[yy, x, every, hi]
                return [(a_part, up), (a_part, down), (b_part, right), (b_part, left)]

            self.hs = stage(eight, *(bulk(xl, yl) + bulk(xr, yr)))
            self.ho = stage(four, *bulk(xo, yo))
            self.f1 = stage(two, (buf.at[yl, x, every, lo], up), (buf.at[y, xl, every, hi], right))
            self.f2 = stage(
                four,
                (buf.at[yl, xl, every, lo], up), (buf.at[yr, xr, every, lo], down),
                (buf.at[yl, xl, every, hi], right), (buf.at[yr, xr, every, hi], left),
            )
            self.f3 = stage(two, (buf.at[yr, xo, every, lo], down), (buf.at[yo, xr, every, hi], left))
            self.stages = [self.zc, self.cx, self.cy] + sum(self.cz, [])
            self.stages += [self.m1, self.m2, self.hp, self.hs, self.ho, self.f1, self.f2, self.f3]

        def event(self, k):
            after = {
                1: (self.cx, self.cy), 2: (self.zc, self.m1, self.hp), 3: (self.cy, *self.cz[0]),
                4: (self.m1, self.m2, self.hs), 5: (self.hp, self.f1), 7: (self.m2, self.ho),
                9: (self.hs, self.f2), 11: (self.ho, self.f3),
            }
            if k in after:
                after[k][0].arrive()
                for stage in after[k][1:]:
                    stage.start()
            elif k in (6, 8, 10):
                ring = k // 2 - 2
                for i in range(2):
                    self.cz[ring - 1][i].arrive()
                    if i < len(self.cz[ring]):
                        self.cz[ring][i].start()
            elif k == 12:
                self.cz[3][0].arrive()
            else:
                self.f1.arrive()
                self.f2.arrive()
                self.f3.arrive()

        def all_sent(self):
            for stage in self.stages:
                stage.sent()

    w_gather = Gather(w)
    w_gather.cx.start()
    w_gather.zc.start()
    s_slots = [slot() for _ in range(4)]

    def s_copy(group, index):
        return remote(tsend.at[group], sg.at[4 * b + group], index, partner)

    def pair_step(group, p):
        n = group * 8 + 2 * p
        step = group * 4 + p
        for when, event in ((3, 1), (5, 2), (6, 3), (8, 4), (10, 5), (11, 6), (12, 7), (14, 8)):
            @pl.when(step == when)
            def _(event=event):
                w_gather.event(event)

        @pl.when(step == 7)
        def _():
            h_far.arrive()
            h_pass.start()

        win = window[...]
        h0, h1, h2 = sigv[n], sigv[n + 1], sigv[n + 2]
        a0, a1 = h0 * win, h1 * win
        b1, b2 = h1 - a1, h2 - h2 * win
        ev, ov = [], []
        for parity, block in ((0, jnp.concatenate([a0 + b1, a1 + b2], 1)), (1, jnp.concatenate([a0 - b1, a1 - b2], 1))):
            high, low = split(block)
            d_high, d_low = first[parity, 0], first[parity, 1]
            part = dot(d_high, high) + dot(d_high, low) + dot(d_low, high)
            (ev if parity == 0 else ov).append(part)
        pieces = []
        for frame in range(2):
            for parity, part in ((0, ev[0]), (1, ov[0])):
                real = part[:128, 128 * frame:128 * frame + 128]
                imag = part[128:, 128 * frame:128 * frame + 128]
                tc = tcos[128 * parity:128 * parity + 128, :]
                ts = tsin[128 * parity:128 * parity + 128, :]
                piece = jnp.concatenate([real * tc + imag * ts, imag * tc - real * ts], 1)
                if parity == 0:
                    zrow[pl.ds(2 * p + frame, 1), :] = piece[:1]
                pieces.append(piece)
        m_high, m_low = second[b, 0], second[b, 1]
        for frame in range(2):
            high, low = split(jnp.concatenate(pieces[2 * frame:2 * frame + 2], 0))
            out = dot(high, m_high) + dot(low, m_high) + dot(high, m_low)
            real, imag = out[:, :128], out[:, 128:]
            mag[2 * p + frame] = jnp.sqrt(real * real + imag * imag)

    lane = lax.broadcasted_iota(jnp.int32, (128, 128), 1)
    row = lax.broadcasted_iota(jnp.int32, (128, 128), 0)
    mirrored = lane // 32 % 2 == 1
    top = row == 0

    def turn(group, j):
        m = mag[j]
        low = jnp.concatenate([m[:64], m[128:192]], 0)
        high = jnp.concatenate([m[64:128], m[192:]], 0)
        extra = jnp.broadcast_to(mag0[pl.ds(j, 1), :], (128, 128))
        high_row = jnp.broadcast_to(high[:1], (128, 128))
        low = jnp.where(top, jnp.where(mirrored, high_row, extra), low)
        high = jnp.where(top & mirrored, extra, high)
        low, high = low.T, high.T
        for ref, index, off in ((sg, 4 * b + group, 0), (tsend, group, 64)):
            for value, place, part in ((low, 0, 0), (high, 1, 0), (high, 2, 1), (low, 3, 1)):
                ref[index, pl.ds(256 * place + j, 32, stride=8), :] = value[off + 32 * part:off + 32 * part + 32]

    def group_step(group, _):
        @pl.when(group == 0)
        def _():
            loads[0].wait()
            loads[1].wait()

        @pl.when(group == 1)
        def _():
            loads[2].wait()

        @pl.when(group == 2)
        def _():
            loads[3].wait()

        @pl.when(group == 3)
        def _():
            halo.wait_recv()
            sigv[32] = sigv[32] * jnp.where(t * 8 + f == 255, 0.0, 1.0)

        def body(p, _):
            pair_step(group, p)
            return 0

        lax.fori_loop(0, 4, body, 0)
        high, low = split(zrow[...])
        out = dot(high, special[b, 0]) + dot(low, special[b, 0]) + dot(high, special[b, 1])
        mag0[...] = jnp.sqrt(out[:, :128] * out[:, :128] + out[:, 128:] * out[:, 128:])

        def turn_body(j, _):
            turn(group, 2 * j)
            turn(group, 2 * j + 1)
            return 0

        lax.fori_loop(0, 4, turn_body, 0)
        for g in range(4):
            @pl.when(group == g)
            def _(g=g):
                s_copy(g, s_slots[g]).start()
        return 0

    lax.fori_loop(0, 4, group_step, 0)

    h_near.arrive()
    h_pass.arrive()
    rows64 = hg[...].reshape(64, 256)
    ht[...] = jnp.concatenate([rows64, rows64], 0).T
    h2 = ht[pl.ds(pl.multiple_of(64 * z_hi, 64), 64), :]
    for g in range(4):
        s_copy(g, s_slots[g]).wait_recv()

    def frames_block(yy, xx):
        cols = []
        for k in range(8):
            place = pl.multiple_of(((yy * 4 + xx) * 8 + k) * 8, 8)
            cols.append(jnp.concatenate([sg[g, pl.ds(place, 8), :] for g in range(8)], 0))
        return jnp.concatenate(cols, 1)

    def ratio_of(buf, lhs, yy, xx):
        wide = jnp.concatenate([buf[yy, xx, k] for k in range(8)], 1)
        high, low = split(wide)
        approx = dot(lhs, jnp.concatenate([high, high, low, low], 0))
        return frames_block(yy, xx) / approx, high, low

    def gain_block(buf, lhs, yy, xx):
        ratio, high, low = ratio_of(buf, lhs, yy, xx)
        r_high, r_low = split(ratio)
        left = jnp.concatenate([r_high, r_low, jnp.ones((16, 1024), BF16)], 0)
        acc[...] += dot_t(left, jnp.concatenate([high, low], 0))

    def gain(stage, index):
        total = acc[...]
        part = jnp.concatenate([total[:64] + total[64:128], total[128:136]], 0)
        stage_send, stage_recv = stage
        stage_send[...] = part + pltpu.roll(part, 64, 1)
        copy = remote(stage_send, stage_recv, index, partner)
        copy.start()
        copy.wait_recv()
        both = stage_send[...] + stage_recv[...]
        return both[:64] / both[64:65], copy

    lhs1 = doubled(h2)
    acc[...] = jnp.zeros_like(acc)

    def gain_all(buf, lhs, gather):
        def near_body(i, _):
            gain_block(buf, lhs, (y + 3 + i // 3) % 4, (x + 3 + i % 3) % 4)
            return 0

        def far_body(i, _):
            gain_block(buf, lhs, (y + 2) % 4, i)
            return 0

        def side_body(i, _):
            gain_block(buf, lhs, (y + 3 + i) % 4, (x + 2) % 4)
            return 0

        gather.event(12)
        lax.fori_loop(0, 9, near_body, 0)
        gather.event(13)
        lax.fori_loop(0, 4, far_body, 0)
        lax.fori_loop(0, 3, side_body, 0)

    for event in (9, 10, 11):
        w_gather.event(event)
    gain_all(w, lhs1, w_gather)
    gain1, mid_copy = gain((sx, rx), slot())
    mid = h2 * gain1
    mid_lhs = doubled(mid)
    mid_t = jnp.concatenate([mid, mid], 0).T
    mid_left = doubled(mid_t[:64])

    tsx[...] = jnp.broadcast_to(jnp.sum(mid, axis=0, keepdims=True), (8, 128))
    tx_copies = group(trx, *[(tsx, trx.at[d - 1], at_x(d)) for d in (1, 2, 3)])
    tx_copies.start()

    def num_block(yy, xx):
        ratio, _, _ = ratio_of(w, mid_lhs, yy, xx)
        high, low = split(ratio)
        out = dot(mid_left, jnp.concatenate([high, high, low, low], 0))
        for k in range(8):
            num[yy, xx, k] = out[:, 128 * k:128 * k + 128]

    def num_run(blocks):
        def body(i, _):
            dy, dx = blocks(i)
            num_block((y + dy) % 4, (x + dx) % 4)
            return 0
        return body

    def run(count, blocks):
        lax.fori_loop(0, count, num_run(blocks), 0)

    def part_a(place, part, rows=every):
        return num.at[place, part, rows, lo]

    def part_b(place, part, rows=every):
        return num.at[part, place, rows, hi]

    two, four = num.at[0, pl.ds(0, 2), every, lo], num.at[0, every, every, lo]
    colours = (
        (part_a, (y, yr, yl, yo), (x, xr, xl, xo), ha1, ha2, at_y(1), at_y(3)),
        (part_b, (x, xr, xl, xo), (y, yr, yl, yo), hb1, hb2, at_x(1), at_x(3)),
    )
    travels = {3: 0, 2: 0, 1: 1, 0: 1}

    def wave(like, moves):
        copies = []
        for get, places, parts, once, twice, right, left in colours:
            for place, part, side in moves:
                target = once.at[part] if place == 3 else twice.at[side, part]
                copies.append((get(places[place], parts[part]), target, right if side == 0 else left))
        return group(like, *copies)

    w1 = wave(four, ((3, 3, 0), (3, 1, 1)))
    w2 = wave(four, ((3, 2, 0), (3, 0, 1)))
    e1 = wave(four, ((1, 1, 0), (2, 3, 1)))
    e2 = wave(four, ((1, 0, 0), (2, 2, 1)))
    l1 = wave(four, ((1, 3, 0), (2, 1, 1)))
    l2 = wave(four, ((1, 2, 0), (2, 0, 1)))

    def pass_on(parts_now):
        for get, places, parts, once, twice, right, left in colours:
            for part in parts_now:
                target = get(places[1 + travels[part]], parts[part])
                target[...] = target[...] + once[part]

    def settle(parts_now):
        for get, places, parts, once, twice, right, left in colours:
            for part in parts_now:
                target = get(places[0], parts[part])
                target[...] = target[...] + (twice[0, part] + twice[1, part])

    def mid_moves(like, moves):
        copies = []
        for (get, places, parts, _, _, _, _), (once, twice), right, left in (
            (colours[0], (ma1, ma2), at_x(1), at_x(3)), (colours[1], (mb1, mb2), at_y(1), at_y(3)),
        ):
            for part, h, side in moves:
                target = once.at[side] if part == 3 else twice.at[side, quad[h]]
                copies.append((get(places[0], parts[part], quad[h]), target, right if side == 0 else left))
        return group(like, *copies)

    mf = mid_moves(two, ((3, 0, 0), (3, 1, 1)))
    me1 = mid_moves(num.at[0, 0, every, lo], ((1, 1, 0),))
    me2 = mid_moves(num.at[0, 0, every, lo], ((2, 0, 1),))
    ml = mid_moves(two, ((1, 0, 0), (2, 1, 1)))

    def chosen(order):
        def blocks(i):
            dy = sum(jnp.where(i == k, v[0], 0) for k, v in enumerate(order))
            dx = sum(jnp.where(i == k, v[1], 0) for k, v in enumerate(order))
            return dy, dx
        run(len(order), blocks)

    run(4, lambda i: (2, i))
    w1.start(0, 1)
    w2.start(0, 1)
    run(3, lambda i: ((i + 3) % 4, 2))
    w1.start(2, 3)
    w2.start(2, 3)
    chosen([(1, 1), (1, 0), (3, 3), (0, 1)])
    e1.start()
    e2.start()
    chosen([(1, 3), (3, 1), (3, 0), (0, 3), (0, 0)])

    def zz(d):
        return (z + 8 + d) % 8

    ring1 = group(
        c1,
        (num.at[half[0], every, zz(4), end], c1.at[0], at_z(1)), (num.at[half[1], every, zz(4), end], c1.at[1], at_z(7)),
    )
    ring1.start()

    def ring_send(buf, d):
        copies = group(
            buf,
            (num.at[every, every, zz(d), end], buf.at[0], at_z(1)), (num.at[every, every, zz(-d), end], buf.at[1], at_z(7)),
        )
        copies.start()
        return copies

    def ring_add(buf, d):
        for side, place in ((0, zz(d)), (1, zz(-d))):
            target = num.at[every, every, place, end]
            target[...] = target[...] + buf[side]

    tx_copies.arrive()
    tsy[...] = tsx[...] + trx[0] + trx[1] + trx[2]
    ty_copies = group(try_, *[(tsy, try_.at[d - 1], at_y(d)) for d in (1, 2, 3)])
    ty_copies.start()
    w1.arrive()
    pass_on((3, 1))
    l1.start()
    ring1.arrive()
    for side, place in ((0, zz(3)), (1, zz(-3))):
        target = num.at[half[side], every, place, end]
        target[...] = target[...] + c1[side]
    ring2 = ring_send(c2, 3)
    w2.arrive()
    pass_on((2, 0))
    l2.start()
    ty_copies.arrive()
    tsz[...] = tsy[...] + try_[0] + try_[1] + try_[2]
    tz_copies = group(trz, *[(tsz, trz.at[d - 1], at_z(d)) for d in range(1, 8)])
    tz_copies.start()
    ring2.arrive()
    ring_add(c2, 2)
    ring3 = ring_send(c3, 2)
    e1.arrive()
    ring3.arrive()
    ring_add(c3, 1)
    ring4 = ring_send(c4, 1)
    l1.arrive()
    settle((3, 1))
    mf.start()
    me1.start()
    e2.arrive()
    l2.arrive()
    settle((2, 0))
    me2.start()
    ring4.arrive()
    target = num.at[every, every, z, end]
    target[...] = target[...] + (c4[0] + c4[1])
    cy_copies = group(cyb, *[(num.at[(y + d) % 4, every, z, end], cyb.at[d - 1], at_y(d)) for d in (1, 2, 3)])
    cy_copies.start()
    mf.arrive()
    for get, places, parts, once in ((part_a, (y,), (x, xr, xl), ma1), (part_b, (x,), (y, yr, yl), mb1)):
        for side in (0, 1):
            target = get(places[0], parts[1 + side], quad[side])
            target[...] = target[...] + once[side]
    ml.start()
    tz_copies.arrive()
    totals = tsz[...]
    for d in range(7):
        totals = totals + trz[d]
    totals = jnp.broadcast_to(totals[:1], (128, 128)).T[:64]
    cy_copies.arrive()
    target = num.at[y, every, z, end]
    target[...] = target[...] + (cyb[0] + cyb[1] + cyb[2])
    cx_copies = group(cxb, *[(num.at[y, (x + d) % 4, z, end], cxb.at[d - 1], at_x(d)) for d in (1, 2, 3)])
    cx_copies.start()
    me1.arrive()
    me2.arrive()
    ml.arrive()
    for get, place, part, twice in ((part_a, y, x, ma2), (part_b, x, y, mb2)):
        target = get(place, part)
        target[...] = target[...] + (twice[0] + twice[1])
    z_copies = group(rz, *[(num.at[y, x, zz(d), low_rows], rz.at[d - 1], at_z(d)) for d in range(1, 8)])
    z_copies.start()
    cx_copies.arrive()
    whole = num[y, x, z, end] + (cxb[0] + cxb[1] + cxb[2])
    wn[y, x, z, end] = w[y, x, z, end] * (whole / totals[48:])
    w_gather.all_sent()
    n_gather = Gather(wn)
    n_gather.cx.start()
    z_copies.arrive()
    whole = num[y, x, z, low_rows]
    for d in range(7):
        whole = whole + rz[d]
    wn[y, x, z, low_rows] = w[y, x, z, low_rows] * (whole / totals[:48])
    n_gather.zc.start()

    out_templ[...] = moved(wn[y, x, z], perms[2 * flip + 1])
    acc[...] = jnp.zeros_like(acc)
    for event in (1, 3, 2, 6, 4, 5, 7, 8, 9, 10, 11):
        n_gather.event(event)
    gain_all(wn, mid_lhs, n_gather)
    gain2, last_copy = gain((sy, ry), slot())
    final = mid * gain2
    fin[...] = jnp.concatenate([final, final], 0).T
    f_copies = group(
        fo.at[pl.ds(0, 3)],
        *[
            (fin.at[pl.ds(pl.multiple_of(8 * ((f + d) % 8), 8), 8)], fo.at[z_hi], at_z(d))
            for d in (2, 4, 6)
        ],
    )
    f_copies.start()
    fo[pl.ds(z_hi, 1)] = fin[pl.ds(pl.multiple_of(8 * f, 8), 8), :][None]
    halo.wait_send()
    n_gather.all_sent()
    for g in range(4):
        s_copy(g, s_slots[g]).wait_send()
    sent([mid_copy, last_copy])
    for part in groups:
        part.sent()
    f_copies.arrive()
    out_act[...] = fo[...]


def finish(parts, templ, out_act, out_templ):
    near = lax.broadcasted_iota(jnp.int32, (8, 128), 1) < 64
    out_act[:, :128] = jnp.where(near, parts[0], parts[1])
    out_act[:, 128:] = jnp.where(near, parts[2], parts[3])
    out_templ[...] = templ[...]


COPIES = 64


def on_device(signal, templates, activations):
    tables = build_tables()
    vmem = pl.BlockSpec(memory_space=pltpu.VMEM)
    f32 = lambda *shape: pltpu.VMEM(shape, F32)
    parts, templ = pl.pallas_call(
        kernel,
        out_shape=(jax.ShapeDtypeStruct((4, 8, 128), F32), jax.ShapeDtypeStruct((64, 128), F32)),
        in_specs=[pl.BlockSpec(memory_space=pl.ANY)] + [vmem] * 9,
        out_specs=(vmem, vmem),
        scratch_shapes=[
            f32(33, 256, 128),
            f32(8, 8, 256),
            f32(256, 128),
            f32(8, 256, 128),
            f32(16, 256),
            f32(16, 128),
            f32(8, 1024, 128),
            f32(4, 1024, 128),
            f32(4, 4, 8, 64, 128),
            f32(4, 4, 8, 64, 128),
            f32(4, 4, 8, 64, 128),
            f32(4, 8, 24, 128),
            f32(2, 4, 8, 24, 128),
            f32(4, 8, 24, 128),
            f32(2, 4, 8, 24, 128),
            f32(2, 4, 24, 128),
            f32(2, 8, 24, 128),
            f32(2, 4, 24, 128),
            f32(2, 8, 24, 128),
            f32(2, 2, 4, 16, 128),
            f32(2, 4, 4, 16, 128),
            f32(2, 4, 4, 16, 128),
            f32(2, 4, 4, 16, 128),
            f32(3, 4, 16, 128),
            f32(3, 16, 128),
            f32(7, 48, 128),
            f32(144, 128),
            f32(72, 128), f32(72, 128), f32(72, 128), f32(72, 128),
            f32(8, 128),
            f32(3, 8, 128), f32(3, 8, 128), f32(7, 8, 128),
            f32(8, 128), f32(8, 128),
            f32(128, 128),
            f32(4, 8, 128),
            pltpu.SemaphoreType.DMA((4,)),
            pltpu.SemaphoreType.DMA((COPIES,)),
            pltpu.SemaphoreType.DMA((COPIES,)),
        ],
        compiler_params=pltpu.CompilerParams(
            collective_id=0, has_side_effects=True, vmem_limit_bytes=60 * 1024 * 1024
        ),
    )(signal.reshape(32, 256, 128), templates, activations, *tables)
    return pl.pallas_call(
        finish,
        out_shape=(jax.ShapeDtypeStruct((8, 256), F32), jax.ShapeDtypeStruct((64, 128), F32)),
        in_specs=[vmem, vmem],
        out_specs=(vmem, vmem),
    )(parts, templ)


def solution(mesh):
    return jax.shard_map(
        on_device,
        mesh=mesh,
        in_specs=(P("frames", "freq", None), P(None, ("freq", "frames")), P("freq", "frames")),
        out_specs=(P("freq", "frames"), P(None, ("freq", "frames"))),
        check_vma=False,
    )
```

```python
import math

import jax
import jax.numpy as jnp
import ml_dtypes
import numpy as np
from jax import lax
from jax.experimental import pallas as pl
from jax.experimental.pallas import tpu as pltpu
from jax.sharding import PartitionSpec as P

MESH = pl.DeviceIdType.MESH
F32 = jnp.float32
BF16 = jnp.bfloat16


def halves(table):
    high = table.astype(ml_dtypes.bfloat16)
    low = (table - high.astype(np.float64)).astype(ml_dtypes.bfloat16)
    return high, low


def build_tables():
    rows = np.arange(256)
    lanes = np.arange(128)
    m = (rows[:, None] * 128 + lanes[None, :]).astype(np.float64)
    window = (0.5 - 0.5 * np.cos(2 * math.pi / 65536 * m)).astype(np.float32)
    first = []
    twiddle = []
    for odd in (0, 1):
        k1 = 2 * np.arange(128) + odd
        angle = 2 * math.pi / 512 * (k1[:, None] * rows[None, :] % 512)
        real, imag = np.cos(angle), -np.sin(angle)
        if not odd:
            imag[0] = 1.0 - 2.0 * (rows % 2)
        first.append(np.concatenate([real, imag], 0))
        twiddle.append(2 * math.pi / 65536 * (k1[:, None] * lanes[None, :]))
    twiddle = np.concatenate(twiddle, 0)
    first = np.stack([np.stack(halves(part)) for part in first])
    second = []
    special = []
    lam = np.arange(128)
    z, x, rev, other = lam % 8, lam // 8 % 4, lam // 32 % 2, lam // 64
    for core in (0, 1):
        base = 8 * (2 * (z // 2) + (core ^ other)) + 4 * (z % 2) + x
        k2 = np.where(rev == 1, 127 - base, base)
        angle = 2 * math.pi / 128 * (lanes[:, None] * k2[None, :] % 128)
        cos, sin = np.cos(angle) / 32, np.sin(angle) / 32
        second.append(np.stack(halves(np.concatenate([np.concatenate([cos, -sin], 1), np.concatenate([sin, cos], 1)], 0))))
        angle = 2 * math.pi / 128 * (lanes[:, None] * (base + 0.5 * rev)[None, :])
        cos, sin = np.cos(angle) / 32, np.sin(angle) / 32
        keep, turn = (1 - rev)[None, :], rev[None, :]
        special.append(
            np.stack(
                halves(
                    np.concatenate(
                        [np.concatenate([cos * keep, -sin * keep], 1), np.concatenate([cos * turn, -sin * turn], 1)], 0
                    )
                )
            )
        )
    sigma = np.where(lanes < 64, 2 * lanes, 2 * (lanes - 64) + 1)
    perms = []
    for order in (sigma, (128 - sigma) % 128):
        perm = np.zeros((128, 128))
        perm[order, lanes] = 1.0
        perms += [perm, perm.T]
    perms = np.stack(perms).astype(ml_dtypes.bfloat16)
    return (
        window,
        np.cos(twiddle).astype(np.float32),
        np.sin(twiddle).astype(np.float32),
        first,
        np.stack(second),
        np.stack(special),
        perms,
    )


def split(value):
    high = value.astype(BF16)
    return high, (value - high.astype(F32)).astype(BF16)


def dot(a, b):
    return jnp.dot(a, b, preferred_element_type=F32)


def dot_t(a, b):
    return lax.dot_general(a, b, (((1,), (1,)), ((), ())), preferred_element_type=F32)


def moved(value, perm):
    high = value.astype(BF16)
    rest = value - high.astype(F32)
    middle = rest.astype(BF16)
    low = (rest - middle.astype(F32)).astype(BF16)
    return dot(high, perm) + dot(middle, perm) + dot(low, perm)


def doubled(value):
    high, low = split(value)
    lane = lax.broadcasted_iota(jnp.int32, value.shape, 1)
    both = jnp.where(lane < 64, high.astype(F32), low.astype(F32)).astype(BF16)
    return jnp.concatenate([both, both], 1)


def kernel(
    sig_hbm, templ, act, window, tcos, tsin, first, second, special, perms,
    out_act, out_templ,
    sigv, hg, ht, mag, zrow, mag0, sg, tsend, w, wn, num,
    ha1, ha2, hb1, hb2, ma1, ma2, mb1, mb2, c1, c2, c3, c4, cyb, cxb, rz,
    hop, acc, sx, rx, sy, ry, tsx, trx, try_, trz, tsy, tsz, fin, fo,
    lsem, ssem, rsem,
):
    f = lax.axis_index("freq")
    t = lax.axis_index("frames")
    b = f % 2
    z_hi = f // 2
    z_lo = t // 16
    x = t // 4 % 4
    y = t % 4
    z = z_hi * 2 + z_lo
    partner = (f + 1 - 2 * b, t)

    def at_x(d):
        return (f, z_lo * 16 + (x + d) % 4 * 4 + y)

    def at_y(d):
        return (f, z_lo * 16 + x * 4 + (y + d) % 4)

    def at_z(d):
        other = (z + d) % 8
        return (other // 2 * 2 + b, other % 2 * 16 + x * 4 + y)

    greet = [partner] + [at_x(d) for d in (1, 2, 3)] + [at_y(d) for d in (1, 2, 3)]
    greet += [at_z(d) for d in range(1, 8)]
    barrier = pltpu.get_barrier_semaphore()
    for device in greet:
        pl.semaphore_signal(barrier, inc=1, device_id=device, device_id_type=MESH)
    loads = [
        pltpu.make_async_copy(sig_hbm.at[pl.ds(8 * i, 8)], sigv.at[pl.ds(8 * i, 8)], lsem.at[i]) for i in range(4)
    ]
    for load in loads:
        load.start()
    flip = y // 2
    w[y, x, z] = moved(templ[...], perms[2 * flip])
    hg[pl.ds(f, 1)] = act[...][None]
    zrow[...] = jnp.zeros_like(zrow)
    pl.semaphore_wait(barrier, len(greet))

    used = [0]

    def slot():
        used[0] += 1
        return used[0] - 1

    def remote(src, dst, index, device):
        return pltpu.make_async_remote_copy(
            src_ref=src, dst_ref=dst, send_sem=ssem.at[index], recv_sem=rsem.at[index],
            device_id=device, device_id_type=MESH,
        )

    class Group:
        def __init__(self, index, like, *copies):
            self.index, self.like = index, like
            self.copies = [remote(src, dst, index, device) for src, dst, device in copies]

        def start(self, *which):
            for i in which or range(len(self.copies)):
                self.copies[i].start()

        def arrive(self):
            pltpu.make_async_copy(self.like, self.like, rsem.at[self.index]).wait()

        def sent(self):
            pltpu.make_async_copy(self.like, self.like, ssem.at[self.index]).wait()

    groups = []

    def group(like, *copies):
        groups.append(Group(slot(), like, *copies))
        return groups[-1]

    halos = [
        group(hop.at[0], (sig_hbm.at[0], hop.at[0], partner)),
        group(hop.at[5], (sig_hbm.at[0], hop.at[5], at_z(6))),
        group(hop.at[1], (hop.at[5], hop.at[1], partner)),
        group(hop.at[2], (hop.at[1], hop.at[2], at_y(3))),
        group(hop.at[3], (hop.at[2], hop.at[3], at_x(3))),
        group(hop.at[4], (hop.at[3], hop.at[4], at_z(7))),
    ]
    halos[0].start()
    halos[1].start()
    h_far = group(hg.at[pl.ds(0, 3)], *[(act, hg.at[f], at_z(d)) for d in (2, 4, 6)])
    h_near = group(hg.at[0], (act, hg.at[f], partner))
    h_pass = group(hg.at[pl.ds(0, 3)], *[(hg.at[(f + d) % 8], hg.at[(f + d) % 8], partner) for d in (2, 4, 6)])
    h_far.start()
    h_near.start()

    subs = ((0, 8), (16, 16))
    end = pl.ds(48, 16)
    half = (pl.ds(0, 2), pl.ds(2, 2))
    quad = (pl.ds(0, 4), pl.ds(4, 4))
    every = slice(None)
    yl, yr, yo = (y + 3) % 4, (y + 1) % 4, (y + 2) % 4
    xl, xr, xo = (x + 3) % 4, (x + 1) % 4, (x + 2) % 4

    def start(copies):
        for copy in copies:
            copy.start()

    def arrive(copies):
        for copy in copies:
            copy.wait_recv()

    def sent(copies):
        for copy in copies:
            copy.wait_send()

    gather_slots = [slot() for _ in range(27)]
    up, down, right, left = at_y(1), at_y(3), at_x(1), at_x(3)

    class Stages:
        def __init__(self, slots):
            self.slots, self.stages = list(slots), []

        def stage(self, like, *moves):
            self.stages.append(Group(self.slots.pop(0), like, *[(region, region, device) for region, device in moves]))
            return self.stages[-1]

        def all_sent(self):
            for stage in self.stages:
                stage.sent()

    class Ring(Stages):
        def __init__(self, buf, slots):
            super().__init__(slots)
            self.cx = self.stage(cxb, *[(buf.at[y, x, z, end], at_x(d)) for d in (1, 2, 3)])
            self.cy = self.stage(cyb, *[(buf.at[y, every, z, end], at_y(d)) for d in (1, 2, 3)])
            self.cz = []
            for k in range(4):
                after, before = (z + 8 - k) % 8, (z + k) % 8
                self.cz.append([
                    self.stage(
                        c1, (buf.at[half[p], every, after, end], at_z(1)), (buf.at[half[q], every, before, end], at_z(7)),
                    )
                    for p, q in (((0, 1), (1, 0)) if k < 3 else ((0, 1),))
                ])

        def event(self, k):
            if k == 0:
                self.cx.start()
            elif k == 1:
                self.cx.arrive()
                self.cy.start()
            elif k == 2:
                self.cy.arrive()
                self.cz[0][0].start()
                self.cz[0][1].start()
            elif k < 6:
                for i in range(2):
                    self.cz[k - 3][i].arrive()
                    if i < len(self.cz[k - 2]):
                        self.cz[k - 2][i].start()
            else:
                self.cz[3][0].arrive()

    class Bulk(Stages):
        def __init__(self, buf, sub, slots):
            super().__init__(slots)
            row, rows = sub
            lo, hi, both = pl.ds(row, rows), pl.ds(row + rows, rows), pl.ds(row, 2 * rows)
            two, four = buf.at[0, pl.ds(0, 2), every, lo], buf.at[0, every, every, lo]
            eight = buf.at[pl.ds(0, 2), every, every, lo]

            def bulk(xx, yy):
                a_part, b_part = buf.at[y, xx, every, lo], buf.at[yy, x, every, hi]
                return [(a_part, up), (a_part, down), (b_part, right), (b_part, left)]

            a_own, b_own = buf.at[y, x, every, lo], buf.at[y, x, every, hi]
            zc = self.stage(rz.at[every, both], *[(buf.at[y, x, z, both], at_z(d)) for d in range(1, 8)])
            m1 = self.stage(four, (a_own, right), (a_own, left), (b_own, up), (b_own, down))
            hp = self.stage(four, *bulk(x, y))
            m2 = self.stage(
                two,
                (buf.at[y, xl, quad[0], lo], right), (buf.at[y, xr, quad[1], lo], left),
                (buf.at[yl, x, quad[0], hi], up), (buf.at[yr, x, quad[1], hi], down),
            )
            hs = self.stage(eight, *(bulk(xl, yl) + bulk(xr, yr)))
            ho = self.stage(four, *bulk(xo, yo))
            f1 = self.stage(two, (buf.at[yl, x, every, lo], up), (buf.at[y, xl, every, hi], right))
            f2 = self.stage(
                four,
                (buf.at[yl, xl, every, lo], up), (buf.at[yr, xr, every, lo], down),
                (buf.at[yl, xl, every, hi], right), (buf.at[yr, xr, every, hi], left),
            )
            f3 = self.stage(two, (buf.at[yr, xo, every, lo], down), (buf.at[yo, xr, every, hi], left))
            self.steps = [
                ((), (zc,)), ((zc,), (m1, hp)), ((m1,), (m2, hs)), ((hp,), (f1,)), ((m2,), (ho,)), ((hs,), (f2,)),
                ((ho,), (f3,)), ((f1, f2, f3), ()),
            ]

        def event(self, k):
            for stage in self.steps[k][0]:
                stage.arrive()
            for stage in self.steps[k][1]:
                stage.start()

    class Gather:
        def __init__(self, buf):
            self.parts = [
                Ring(buf, gather_slots[:9]), Bulk(buf, subs[0], gather_slots[9:18]), Bulk(buf, subs[1], gather_slots[18:]),
            ]

        def event(self, part, k):
            self.parts[part].event(k)

        def all_sent(self):
            for part in self.parts:
                part.all_sent()

    w_gather = Gather(w)
    for part in range(3):
        w_gather.event(part, 0)
    s_slots = [slot() for _ in range(4)]

    def s_copy(group, index):
        return remote(tsend.at[group], sg.at[4 * b + group], index, partner)

    def pair_step(group, p):
        n = group * 8 + 2 * p
        step = group * 4 + p
        for when, events in (
            (2, ((0, 1),)), (3, ((1, 1),)), (5, ((0, 2), (1, 2))), (6, ((1, 3),)), (7, ((2, 1), (1, 4))),
            (9, ((0, 3), (2, 2))), (10, ((1, 5), (2, 3))), (12, ((1, 6), (2, 4))), (14, ((0, 4), (2, 5))),
        ):
            @pl.when(step == when)
            def _(events=events):
                for event in events:
                    w_gather.event(*event)

        @pl.when(step == 4)
        def _():
            h_far.arrive()
            h_pass.start()

        for when, stage in ((2, 1), (4, 2), (7, 3), (9, 4)):
            @pl.when(step == when)
            def _(stage=stage):
                halos[stage].arrive()
                halos[stage + 1].start()

        win = window[...]
        h0, h1, h2 = sigv[n], sigv[n + 1], sigv[n + 2]
        a0, a1 = h0 * win, h1 * win
        b1, b2 = h1 - a1, h2 - h2 * win
        ev, ov = [], []
        for parity, block in ((0, jnp.concatenate([a0 + b1, a1 + b2], 1)), (1, jnp.concatenate([a0 - b1, a1 - b2], 1))):
            high, low = split(block)
            d_high, d_low = first[parity, 0], first[parity, 1]
            part = dot(d_high, high) + dot(d_high, low) + dot(d_low, high)
            (ev if parity == 0 else ov).append(part)
        pieces = []
        for frame in range(2):
            for parity, part in ((0, ev[0]), (1, ov[0])):
                real = part[:128, 128 * frame:128 * frame + 128]
                imag = part[128:, 128 * frame:128 * frame + 128]
                tc = tcos[128 * parity:128 * parity + 128, :]
                ts = tsin[128 * parity:128 * parity + 128, :]
                piece = jnp.concatenate([real * tc + imag * ts, imag * tc - real * ts], 1)
                if parity == 0:
                    zrow[pl.ds(2 * p + frame, 1), :] = piece[:1]
                pieces.append(piece)
        m_high, m_low = second[b, 0], second[b, 1]
        for frame in range(2):
            high, low = split(jnp.concatenate(pieces[2 * frame:2 * frame + 2], 0))
            out = dot(high, m_high) + dot(low, m_high) + dot(high, m_low)
            real, imag = out[:, :128], out[:, 128:]
            mag[2 * p + frame] = jnp.sqrt(real * real + imag * imag)

    lane = lax.broadcasted_iota(jnp.int32, (128, 128), 1)
    row = lax.broadcasted_iota(jnp.int32, (128, 128), 0)
    mirrored = lane // 32 % 2 == 1
    top = row == 0

    def turn(group, j):
        m = mag[j]
        low = jnp.concatenate([m[:64], m[128:192]], 0)
        high = jnp.concatenate([m[64:128], m[192:]], 0)
        extra = jnp.broadcast_to(mag0[pl.ds(j, 1), :], (128, 128))
        high_row = jnp.broadcast_to(high[:1], (128, 128))
        low = jnp.where(top, jnp.where(mirrored, high_row, extra), low)
        high = jnp.where(top & mirrored, extra, high)
        low, high = low.T, high.T
        for ref, index, off in ((sg, 4 * b + group, 0), (tsend, group, 64)):
            for value, place, part in ((low, 0, 0), (high, 1, 0), (high, 2, 1), (low, 3, 1)):
                ref[index, pl.ds(256 * place + j, 32, stride=8), :] = value[off + 32 * part:off + 32 * part + 32]

    def group_step(group, _):
        @pl.when(group == 0)
        def _():
            loads[0].wait()
            loads[1].wait()

        @pl.when(group == 1)
        def _():
            loads[2].wait()

        @pl.when(group == 2)
        def _():
            loads[3].wait()

        @pl.when(group == 3)
        def _():
            halos[0].arrive()
            halos[5].arrive()
            line = jnp.where(y < 3, 2, jnp.where(x < 3, 3, 4))
            source = jnp.where(b == 0, 0, jnp.where(z_hi < 3, 1, line))
            sigv[32] = hop[source] * jnp.where(t * 8 + f == 255, 0.0, 1.0)

        def body(p, _):
            pair_step(group, p)
            return 0

        lax.fori_loop(0, 4, body, 0)
        high, low = split(zrow[...])
        out = dot(high, special[b, 0]) + dot(low, special[b, 0]) + dot(high, special[b, 1])
        mag0[...] = jnp.sqrt(out[:, :128] * out[:, :128] + out[:, 128:] * out[:, 128:])

        def turn_body(j, _):
            turn(group, 2 * j)
            turn(group, 2 * j + 1)
            return 0

        lax.fori_loop(0, 4, turn_body, 0)
        for g in range(4):
            @pl.when(group == g)
            def _(g=g):
                s_copy(g, s_slots[g]).start()
        return 0

    lax.fori_loop(0, 4, group_step, 0)

    h_near.arrive()
    h_pass.arrive()
    rows64 = hg[...].reshape(64, 256)
    ht[...] = jnp.concatenate([rows64, rows64], 0).T
    h2 = ht[pl.ds(pl.multiple_of(64 * z_hi, 64), 64), :]
    for g in range(4):
        s_copy(g, s_slots[g]).wait_recv()

    def frames_block(yy, xx):
        cols = []
        for k in range(8):
            place = pl.multiple_of(((yy * 4 + xx) * 8 + k) * 8, 8)
            cols.append(jnp.concatenate([sg[g, pl.ds(place, 8), :] for g in range(8)], 0))
        return jnp.concatenate(cols, 1)

    def ratio_of(buf, lhs, yy, xx):
        wide = jnp.concatenate([buf[yy, xx, k] for k in range(8)], 1)
        high, low = split(wide)
        approx = dot(lhs, jnp.concatenate([high, high, low, low], 0))
        return frames_block(yy, xx) / approx, high, low

    def gain_block(buf, lhs, yy, xx):
        ratio, high, low = ratio_of(buf, lhs, yy, xx)
        r_high, r_low = split(ratio)
        left = jnp.concatenate([r_high, r_low, jnp.ones((16, 1024), BF16)], 0)
        acc[...] += dot_t(left, jnp.concatenate([high, low], 0))

    def gain(stage, index):
        total = acc[...]
        part = jnp.concatenate([total[:64] + total[64:128], total[128:136]], 0)
        stage_send, stage_recv = stage
        stage_send[...] = part + pltpu.roll(part, 64, 1)
        copy = remote(stage_send, stage_recv, index, partner)
        copy.start()
        copy.wait_recv()
        both = stage_send[...] + stage_recv[...]
        return both[:64] / both[64:65], copy

    lhs1 = doubled(h2)
    acc[...] = jnp.zeros_like(acc)

    def gain_all(buf, lhs, gather):
        def near_body(i, _):
            gain_block(buf, lhs, (y + 3 + i // 3) % 4, (x + 3 + i % 3) % 4)
            return 0

        def far_body(i, _):
            gain_block(buf, lhs, (y + 2) % 4, i)
            return 0

        def side_body(i, _):
            gain_block(buf, lhs, (y + 3 + i) % 4, (x + 2) % 4)
            return 0

        gather.event(0, 6)
        lax.fori_loop(0, 9, near_body, 0)
        gather.event(1, 7)
        gather.event(2, 7)
        lax.fori_loop(0, 4, far_body, 0)
        lax.fori_loop(0, 3, side_body, 0)

    w_gather.event(0, 5)
    w_gather.event(2, 6)
    gain_all(w, lhs1, w_gather)
    gain1, mid_copy = gain((sx, rx), slot())
    mid = h2 * gain1
    mid_lhs = doubled(mid)
    mid_t = jnp.concatenate([mid, mid], 0).T
    mid_left = doubled(mid_t[:64])

    tsx[...] = jnp.broadcast_to(jnp.sum(mid, axis=0, keepdims=True), (8, 128))
    tx_copies = group(trx, *[(tsx, trx.at[d - 1], at_x(d)) for d in (1, 2, 3)])
    tx_copies.start()

    def num_block(yy, xx):
        ratio, _, _ = ratio_of(w, mid_lhs, yy, xx)
        high, low = split(ratio)
        out = dot(mid_left, jnp.concatenate([high, high, low, low], 0))
        for k in range(8):
            num[yy, xx, k] = out[:, 128 * k:128 * k + 128]

    def num_run(blocks):
        def body(i, _):
            dy, dx = blocks(i)
            num_block((y + dy) % 4, (x + dx) % 4)
            return 0
        return body

    def run(count, blocks):
        lax.fori_loop(0, count, num_run(blocks), 0)

    travels = {3: 0, 2: 0, 1: 1, 0: 1}

    class Reduce:
        def __init__(self, sub):
            row, rows = sub
            lo, hi = pl.ds(row, rows), pl.ds(row + rows, rows)
            self.both = pl.ds(row, 2 * rows)
            here = pl.ds(row // 2, rows)
            one, two, four = num.at[0, 0, every, lo], num.at[0, pl.ds(0, 2), every, lo], num.at[0, every, every, lo]

            def part_a(place, part, z_rows=every):
                return num.at[place, part, z_rows, lo]

            def part_b(place, part, z_rows=every):
                return num.at[part, place, z_rows, hi]

            self.colours = (
                (part_a, (y, yr, yl, yo), (x, xr, xl, xo), ha1, ha2, ma1, ma2, up, down, right, left),
                (part_b, (x, xr, xl, xo), (y, yr, yl, yo), hb1, hb2, mb1, mb2, right, left, up, down),
            )
            self.here = here

            def wave(*moves):
                copies = []
                for get, places, parts, once, twice, _, _, ahead, behind, _, _ in self.colours:
                    for place, part, side in moves:
                        target = once.at[part, every, here] if place == 3 else twice.at[side, part, every, here]
                        copies.append((get(places[place], parts[part]), target, ahead if side == 0 else behind))
                return group(four, *copies)

            self.w1, self.w2 = wave((3, 3, 0), (3, 1, 1)), wave((3, 2, 0), (3, 0, 1))
            self.e1, self.e2 = wave((1, 1, 0), (2, 3, 1)), wave((1, 0, 0), (2, 2, 1))
            self.l1, self.l2 = wave((1, 3, 0), (2, 1, 1)), wave((1, 2, 0), (2, 0, 1))

            def mid_moves(like, *moves):
                copies = []
                for get, places, parts, _, _, once, twice, _, _, ahead, behind in self.colours:
                    for part, h, side in moves:
                        target = once.at[side, every, here] if part == 3 else twice.at[side, quad[h], here]
                        copies.append((get(places[0], parts[part], quad[h]), target, ahead if side == 0 else behind))
                return group(like, *copies)

            self.mf = mid_moves(two, (3, 0, 0), (3, 1, 1))
            self.me1, self.me2 = mid_moves(one, (1, 1, 0)), mid_moves(one, (2, 0, 1))
            self.ml = mid_moves(two, (1, 0, 0), (2, 1, 1))
            self.zs = group(
                rz.at[every, self.both],
                *[(num.at[y, x, zz(d), self.both], rz.at[d - 1, self.both], at_z(d)) for d in range(1, 8)],
            )

        def pass_on(self, parts_now):
            for get, places, parts, once, *_ in self.colours:
                for part in parts_now:
                    target = get(places[1 + travels[part]], parts[part])
                    target[...] = target[...] + once[part, :, self.here]

        def settle(self, parts_now):
            for get, places, parts, _, twice, *_ in self.colours:
                for part in parts_now:
                    target = get(places[0], parts[part])
                    target[...] = target[...] + (twice[0, part, :, self.here] + twice[1, part, :, self.here])

        def event(self, k):
            if k == 1:
                self.w1.arrive()
                self.pass_on((3, 1))
                self.l1.start()
            elif k == 2:
                self.w2.arrive()
                self.pass_on((2, 0))
                self.l2.start()
            elif k == 3:
                self.e1.arrive()
                self.l1.arrive()
                self.settle((3, 1))
                self.mf.start()
                self.me1.start()
            elif k == 4:
                self.e2.arrive()
                self.l2.arrive()
                self.settle((2, 0))
                self.me2.start()
            elif k == 5:
                self.mf.arrive()
                for get, places, parts, _, _, once, *_ in self.colours:
                    for side in (0, 1):
                        target = get(places[0], parts[1 + side], quad[side])
                        target[...] = target[...] + once[side, :, self.here]
                self.ml.start()
            elif k == 6:
                self.me1.arrive()
                self.me2.arrive()
                self.ml.arrive()
                for get, places, parts, _, _, _, twice, *_ in self.colours:
                    target = get(places[0], parts[0])
                    target[...] = target[...] + (twice[0, :, self.here] + twice[1, :, self.here])
                self.zs.start()
            else:
                self.zs.arrive()
                whole = num[y, x, z, self.both]
                for d in range(7):
                    whole = whole + rz[d, self.both]
                row, rows = self.both.start, self.both.size
                wn[y, x, z, self.both] = w[y, x, z, self.both] * (whole / totals[row:row + rows])

    def zz(d):
        return (z + 8 + d) % 8

    w_gather.all_sent()
    n_gather = Gather(wn)
    r1, r2 = Reduce(subs[0]), Reduce(subs[1])

    def chosen(order):
        def blocks(i):
            dy = sum(jnp.where(i == k, v[0], 0) for k, v in enumerate(order))
            dx = sum(jnp.where(i == k, v[1], 0) for k, v in enumerate(order))
            return dy, dx
        run(len(order), blocks)

    run(4, lambda i: (2, i))
    r1.w1.start(0, 1)
    r1.w2.start(0, 1)
    run(3, lambda i: ((i + 3) % 4, 2))
    r1.w1.start(2, 3)
    r1.w2.start(2, 3)
    chosen([(1, 1), (1, 0), (3, 3), (0, 1)])
    r1.e1.start()
    r1.e2.start()
    r2.w1.start()
    chosen([(1, 3), (3, 1), (3, 0), (0, 3), (0, 0)])

    ring1 = group(
        c1,
        (num.at[half[0], every, zz(4), end], c1.at[0], at_z(1)), (num.at[half[1], every, zz(4), end], c1.at[1], at_z(7)),
    )
    ring1.start()

    def ring_send(buf, d):
        copies = group(
            buf,
            (num.at[every, every, zz(d), end], buf.at[0], at_z(1)), (num.at[every, every, zz(-d), end], buf.at[1], at_z(7)),
        )
        copies.start()
        return copies

    def ring_add(buf, d):
        for side, place in ((0, zz(d)), (1, zz(-d))):
            target = num.at[every, every, place, end]
            target[...] = target[...] + buf[side]

    tx_copies.arrive()
    tsy[...] = tsx[...] + trx[0] + trx[1] + trx[2]
    ty_copies = group(try_, *[(tsy, try_.at[d - 1], at_y(d)) for d in (1, 2, 3)])
    ty_copies.start()
    r1.event(1)
    r2.w2.start()
    ring1.arrive()
    for side, place in ((0, zz(3)), (1, zz(-3))):
        target = num.at[half[side], every, place, end]
        target[...] = target[...] + c1[side]
    ring2 = ring_send(c2, 3)
    r1.event(2)
    r2.e1.start()
    ty_copies.arrive()
    tsz[...] = tsy[...] + try_[0] + try_[1] + try_[2]
    tz_copies = group(trz, *[(tsz, trz.at[d - 1], at_z(d)) for d in range(1, 8)])
    tz_copies.start()
    r1.event(3)
    r2.event(1)
    r2.e2.start()
    ring2.arrive()
    ring_add(c2, 2)
    ring3 = ring_send(c3, 2)
    r1.event(4)
    r2.event(2)
    r1.event(5)
    tz_copies.arrive()
    totals = tsz[...]
    for d in range(7):
        totals = totals + trz[d]
    totals = jnp.broadcast_to(totals[:1], (128, 128)).T[:64]
    ring3.arrive()
    ring_add(c3, 1)
    ring4 = ring_send(c4, 1)
    r1.event(6)
    r2.event(3)
    ring4.arrive()
    target = num.at[every, every, z, end]
    target[...] = target[...] + (c4[0] + c4[1])
    cy_copies = group(cyb, *[(num.at[(y + d) % 4, every, z, end], cyb.at[d - 1], at_y(d)) for d in (1, 2, 3)])
    cy_copies.start()
    r1.event(7)
    n_gather.event(1, 0)
    r2.event(4)
    cy_copies.arrive()
    target = num.at[y, every, z, end]
    target[...] = target[...] + (cyb[0] + cyb[1] + cyb[2])
    cx_copies = group(cxb, *[(num.at[y, (x + d) % 4, z, end], cxb.at[d - 1], at_x(d)) for d in (1, 2, 3)])
    cx_copies.start()
    r2.event(5)
    n_gather.event(1, 1)
    cx_copies.arrive()
    whole = num[y, x, z, end] + (cxb[0] + cxb[1] + cxb[2])
    wn[y, x, z, end] = w[y, x, z, end] * (whole / totals[48:])
    n_gather.event(0, 0)
    r2.event(6)
    n_gather.event(1, 2)
    n_gather.event(1, 3)
    n_gather.event(0, 1)
    r2.event(7)
    n_gather.event(2, 0)

    out_templ[...] = moved(wn[y, x, z], perms[2 * flip + 1])
    acc[...] = jnp.zeros_like(acc)
    for event in (
        (1, 4), (0, 2), (1, 5), (1, 6), (2, 1), (0, 3), (2, 2), (2, 3), (0, 4), (2, 4), (2, 5), (0, 5), (2, 6),
    ):
        n_gather.event(*event)
    gain_all(wn, mid_lhs, n_gather)
    gain2, last_copy = gain((sy, ry), slot())
    final = mid * gain2
    fin[...] = jnp.concatenate([final, final], 0).T
    f_copies = group(
        fo.at[pl.ds(0, 3)],
        *[
            (fin.at[pl.ds(pl.multiple_of(8 * ((f + d) % 8), 8), 8)], fo.at[z_hi], at_z(d))
            for d in (2, 4, 6)
        ],
    )
    f_copies.start()
    fo[pl.ds(z_hi, 1)] = fin[pl.ds(pl.multiple_of(8 * f, 8), 8), :][None]
    n_gather.all_sent()
    for g in range(4):
        s_copy(g, s_slots[g]).wait_send()
    sent([mid_copy, last_copy])
    for part in groups:
        part.sent()
    f_copies.arrive()
    out_act[...] = fo[...]


def finish(parts, templ, out_act, out_templ):
    near = lax.broadcasted_iota(jnp.int32, (8, 128), 1) < 64
    out_act[:, :128] = jnp.where(near, parts[0], parts[1])
    out_act[:, 128:] = jnp.where(near, parts[2], parts[3])
    out_templ[...] = templ[...]


COPIES = 96


def on_device(signal, templates, activations):
    tables = build_tables()
    vmem = pl.BlockSpec(memory_space=pltpu.VMEM)
    f32 = lambda *shape: pltpu.VMEM(shape, F32)
    parts, templ = pl.pallas_call(
        kernel,
        out_shape=(jax.ShapeDtypeStruct((4, 8, 128), F32), jax.ShapeDtypeStruct((64, 128), F32)),
        in_specs=[pl.BlockSpec(memory_space=pl.ANY)] + [vmem] * 9,
        out_specs=(vmem, vmem),
        scratch_shapes=[
            f32(33, 256, 128),
            f32(8, 8, 256),
            f32(256, 128),
            f32(8, 256, 128),
            f32(16, 256),
            f32(16, 128),
            f32(8, 1024, 128),
            f32(4, 1024, 128),
            f32(4, 4, 8, 64, 128),
            f32(4, 4, 8, 64, 128),
            f32(4, 4, 8, 64, 128),
            f32(4, 8, 24, 128),
            f32(2, 4, 8, 24, 128),
            f32(4, 8, 24, 128),
            f32(2, 4, 8, 24, 128),
            f32(2, 4, 24, 128),
            f32(2, 8, 24, 128),
            f32(2, 4, 24, 128),
            f32(2, 8, 24, 128),
            f32(2, 2, 4, 16, 128),
            f32(2, 4, 4, 16, 128),
            f32(2, 4, 4, 16, 128),
            f32(2, 4, 4, 16, 128),
            f32(3, 4, 16, 128),
            f32(3, 16, 128),
            f32(7, 48, 128),
            f32(6, 256, 128),
            f32(144, 128),
            f32(72, 128), f32(72, 128), f32(72, 128), f32(72, 128),
            f32(8, 128),
            f32(3, 8, 128), f32(3, 8, 128), f32(7, 8, 128),
            f32(8, 128), f32(8, 128),
            f32(128, 128),
            f32(4, 8, 128),
            pltpu.SemaphoreType.DMA((4,)),
            pltpu.SemaphoreType.DMA((COPIES,)),
            pltpu.SemaphoreType.DMA((COPIES,)),
        ],
        compiler_params=pltpu.CompilerParams(
            collective_id=0, has_side_effects=True, vmem_limit_bytes=60 * 1024 * 1024
        ),
    )(signal.reshape(32, 256, 128), templates, activations, *tables)
    return pl.pallas_call(
        finish,
        out_shape=(jax.ShapeDtypeStruct((8, 256), F32), jax.ShapeDtypeStruct((64, 128), F32)),
        in_specs=[vmem, vmem],
        out_specs=(vmem, vmem),
    )(parts, templ)


def solution(mesh):
    return jax.shard_map(
        on_device,
        mesh=mesh,
        in_specs=(P("frames", "freq", None), P(None, ("freq", "frames")), P("freq", "frames")),
        out_specs=(P("freq", "frames"), P(None, ("freq", "frames"))),
        check_vma=False,
    )
```

```python
import math

import jax
import jax.numpy as jnp
import ml_dtypes
import numpy as np
from jax import lax
from jax.experimental import pallas as pl
from jax.experimental.pallas import tpu as pltpu
from jax.sharding import PartitionSpec as P

MESH = pl.DeviceIdType.MESH
F32 = jnp.float32
BF16 = jnp.bfloat16


def halves(table):
    high = table.astype(ml_dtypes.bfloat16)
    low = (table - high.astype(np.float64)).astype(ml_dtypes.bfloat16)
    return high, low


def build_tables():
    rows = np.arange(256)
    lanes = np.arange(128)
    m = (rows[:, None] * 128 + lanes[None, :]).astype(np.float64)
    window = (0.5 - 0.5 * np.cos(2 * math.pi / 65536 * m)).astype(np.float32)
    first = []
    twiddle = []
    for odd in (0, 1):
        k1 = 2 * np.arange(128) + odd
        angle = 2 * math.pi / 512 * (k1[:, None] * rows[None, :] % 512)
        real, imag = np.cos(angle), -np.sin(angle)
        if not odd:
            imag[0] = 1.0 - 2.0 * (rows % 2)
        first.append(np.concatenate([real, imag], 0))
        twiddle.append(2 * math.pi / 65536 * (k1[:, None] * lanes[None, :]))
    twiddle = np.concatenate(twiddle, 0)
    first = np.stack([np.stack(halves(part)) for part in first])
    second = []
    special = []
    lam = np.arange(128)
    z, x, rev, other = lam % 8, lam // 8 % 4, lam // 32 % 2, lam // 64
    for core in (0, 1):
        base = 8 * (2 * (z // 2) + (core ^ other)) + 4 * (z % 2) + x
        k2 = np.where(rev == 1, 127 - base, base)
        angle = 2 * math.pi / 128 * (lanes[:, None] * k2[None, :] % 128)
        cos, sin = np.cos(angle) / 32, np.sin(angle) / 32
        second.append(np.stack(halves(np.concatenate([np.concatenate([cos, -sin], 1), np.concatenate([sin, cos], 1)], 0))))
        angle = 2 * math.pi / 128 * (lanes[:, None] * (base + 0.5 * rev)[None, :])
        cos, sin = np.cos(angle) / 32, np.sin(angle) / 32
        keep, turn = (1 - rev)[None, :], rev[None, :]
        special.append(
            np.stack(
                halves(
                    np.concatenate(
                        [np.concatenate([cos * keep, -sin * keep], 1), np.concatenate([cos * turn, -sin * turn], 1)], 0
                    )
                )
            )
        )
    sigma = np.where(lanes < 64, 2 * lanes, 2 * (lanes - 64) + 1)
    perms = []
    for order in (sigma, (128 - sigma) % 128):
        perm = np.zeros((128, 128))
        perm[order, lanes] = 1.0
        perms += [perm, perm.T]
    perms = np.stack(perms).astype(ml_dtypes.bfloat16)
    return (
        window,
        np.cos(twiddle).astype(np.float32),
        np.sin(twiddle).astype(np.float32),
        first,
        np.stack(second),
        np.stack(special),
        perms,
    )


def split(value):
    high = value.astype(BF16)
    return high, (value - high.astype(F32)).astype(BF16)


def dot(a, b):
    return jnp.dot(a, b, preferred_element_type=F32)


def dot_t(a, b):
    return lax.dot_general(a, b, (((1,), (1,)), ((), ())), preferred_element_type=F32)


def moved(value, perm):
    high = value.astype(BF16)
    rest = value - high.astype(F32)
    middle = rest.astype(BF16)
    low = (rest - middle.astype(F32)).astype(BF16)
    return dot(high, perm) + dot(middle, perm) + dot(low, perm)


def doubled(value):
    high, low = split(value)
    lane = lax.broadcasted_iota(jnp.int32, value.shape, 1)
    both = jnp.where(lane < 64, high.astype(F32), low.astype(F32)).astype(BF16)
    return jnp.concatenate([both, both], 1)


def kernel(
    sig_hbm, templ, act, window, tcos, tsin, first, second, special, perms,
    out_act, out_templ,
    sigv, hg, ht, mag, zrow, mag0, sg, tsend, w, wn, num,
    ha1, ha2, hb1, hb2, ma1, ma2, mb1, mb2, c1, c2, c3, c4, cyb, cxb, rz,
    hop, acc, sx, rx, sy, ry, tsx, trx, try_, trz, tsy, tsz, fin, fo,
    lsem, ssem, rsem,
):
    f = lax.axis_index("freq")
    t = lax.axis_index("frames")
    b = f % 2
    z_hi = f // 2
    z_lo = t // 16
    x = t // 4 % 4
    y = t % 4
    z = z_hi * 2 + z_lo
    partner = (f + 1 - 2 * b, t)

    def at_x(d):
        return (f, z_lo * 16 + (x + d) % 4 * 4 + y)

    def at_y(d):
        return (f, z_lo * 16 + x * 4 + (y + d) % 4)

    def at_z(d):
        other = (z + d) % 8
        return (other // 2 * 2 + b, other % 2 * 16 + x * 4 + y)

    greet = [partner] + [at_x(d) for d in (1, 2, 3)] + [at_y(d) for d in (1, 2, 3)]
    greet += [at_z(d) for d in range(1, 8)]
    barrier = pltpu.get_barrier_semaphore()
    for device in greet:
        pl.semaphore_signal(barrier, inc=1, device_id=device, device_id_type=MESH)
    loads = [
        pltpu.make_async_copy(sig_hbm.at[pl.ds(8 * i, 8)], sigv.at[pl.ds(8 * i, 8)], lsem.at[i]) for i in range(4)
    ]
    for load in loads:
        load.start()
    flip = y // 2
    w[y, x, z] = moved(templ[...], perms[2 * flip])
    hg[pl.ds(f, 1)] = act[...][None]
    zrow[...] = jnp.zeros_like(zrow)
    pl.semaphore_wait(barrier, len(greet))

    used = [0]

    def slot():
        used[0] += 1
        return used[0] - 1

    def remote(src, dst, index, device):
        return pltpu.make_async_remote_copy(
            src_ref=src, dst_ref=dst, send_sem=ssem.at[index], recv_sem=rsem.at[index],
            device_id=device, device_id_type=MESH,
        )

    class Group:
        def __init__(self, index, like, *copies):
            self.index, self.like = index, like
            self.copies = [remote(src, dst, index, device) for src, dst, device in copies]

        def start(self, *which):
            for i in which or range(len(self.copies)):
                self.copies[i].start()

        def arrive(self):
            pltpu.make_async_copy(self.like, self.like, rsem.at[self.index]).wait()

        def sent(self):
            pltpu.make_async_copy(self.like, self.like, ssem.at[self.index]).wait()

    groups = []

    def group(like, *copies):
        groups.append(Group(slot(), like, *copies))
        return groups[-1]

    turn_y = (b == 1) & (z_hi == 3)
    turn_x = turn_y & (y == 3)
    turn_z = turn_x & (x == 3)
    halos = [
        (sig_hbm.at[0], hop.at[0], partner, b == 1, b == 0),
        (sig_hbm.at[0], hop.at[5], at_z(6), b == 0, b == 0),
        (hop.at[5], hop.at[1], partner, b == 0, b == 1),
        (hop.at[1], hop.at[2], at_y(3), turn_y, turn_y),
        (hop.at[2], hop.at[3], at_x(3), turn_x, turn_x),
        (hop.at[3], hop.at[4], at_z(7), turn_z & (z_lo == 1), turn_z & (z_lo == 0)),
    ]
    halos = [(remote(src, dst, slot(), device), sends, receives) for src, dst, device, sends, receives in halos]

    def halo_start(k):
        @pl.when(halos[k][1])
        def _():
            halos[k][0].start()

    def halo_arrive(k):
        @pl.when(halos[k][2])
        def _():
            halos[k][0].wait_recv()

    halo_start(0)
    halo_start(1)
    h_far = group(hg.at[pl.ds(0, 3)], *[(act, hg.at[f], at_z(d)) for d in (2, 4, 6)])
    h_near = group(hg.at[0], (act, hg.at[f], partner))
    h_pass = group(hg.at[pl.ds(0, 3)], *[(hg.at[(f + d) % 8], hg.at[(f + d) % 8], partner) for d in (2, 4, 6)])
    h_far.start()
    h_near.start()

    lo, hi, low_rows = pl.ds(0, 24), pl.ds(24, 24), pl.ds(0, 48)
    end = pl.ds(48, 16)
    half = (pl.ds(0, 2), pl.ds(2, 2))
    quad = (pl.ds(0, 4), pl.ds(4, 4))
    every = slice(None)
    yl, yr, yo = (y + 3) % 4, (y + 1) % 4, (y + 2) % 4
    xl, xr, xo = (x + 3) % 4, (x + 1) % 4, (x + 2) % 4

    def start(copies):
        for copy in copies:
            copy.start()

    def arrive(copies):
        for copy in copies:
            copy.wait_recv()

    def sent(copies):
        for copy in copies:
            copy.wait_send()

    gather_slots = [slot() for _ in range(21)]

    class Gather:
        def __init__(self, buf):
            count = [0]

            def stage(like, *moves):
                count[0] += 1
                return Group(gather_slots[count[0] - 1], like, *[(region, region, device) for region, device in moves])

            up, down, right, left = at_y(1), at_y(3), at_x(1), at_x(3)
            own = buf.at[y, x, z, low_rows]
            flips = (1 - 2 * (z % 2), 2 - 4 * (z // 2 % 2), 4)

            def across(k):
                return at_z(8 + k % 2 * flips[0] + k // 2 % 2 * flips[1] + k // 4 * flips[2])

            self.zc = stage(rz.at[pl.ds(0, 3)], *[(own, across(k)) for k in (2, 3, 1)])
            self.zd = stage(rz.at[pl.ds(0, 4)], *[(own, across(k)) for k in (4, 5, 6, 7)])
            self.cx = stage(cxb, *[(buf.at[y, x, z, end], at_x(d)) for d in (1, 2, 3)])
            self.cy = stage(cyb, *[(buf.at[y, every, z, end], at_y(d)) for d in (1, 2, 3)])
            self.cz = []
            for k in range(4):
                after, before = (z + 8 - k) % 8, (z + k) % 8
                ring = []
                for p, q in ((0, 1), (1, 0)) if k < 3 else ((0, 1),):
                    ring.append(stage(
                        c1, (buf.at[half[p], every, after, end], at_z(1)), (buf.at[half[q], every, before, end], at_z(7)),
                    ))
                self.cz.append(ring)
            two, four = buf.at[0, pl.ds(0, 2), every, lo], buf.at[0, every, every, lo]
            eight = buf.at[pl.ds(0, 2), every, every, lo]
            near, away = pl.ds(z // 4 * 4, 4), pl.ds(4 - z // 4 * 4, 4)

            def sides(part, one, other):
                return [(part, one), (part, other)]

            a_near, b_near = buf.at[y, x, near, lo], buf.at[y, x, near, hi]
            a_away, b_away = buf.at[y, x, away, lo], buf.at[y, x, away, hi]
            self.m1 = stage(two, *(sides(a_near, right, left) + sides(b_near, up, down)))
            self.n1 = stage(two, *(sides(a_away, right, left) + sides(b_away, up, down)))
            self.m2 = stage(
                two,
                (buf.at[y, xl, quad[0], lo], right), (buf.at[y, xr, quad[1], lo], left),
                (buf.at[yl, x, quad[0], hi], up), (buf.at[yr, x, quad[1], hi], down),
            )
            self.hp = stage(two, *(sides(a_near, up, down) + sides(b_near, right, left)))
            self.hq = stage(two, *(sides(a_away, up, down) + sides(b_away, right, left)))

            def bulk(xx, yy):
                a_part, b_part = buf.at[y, xx, every, lo], buf.at[yy, x, every, hi]
                return [(a_part, up), (a_part, down), (b_part, right), (b_part, left)]

            self.hs = stage(eight, *(bulk(xl, yl) + bulk(xr, yr)))
            self.ho = stage(four, *bulk(xo, yo))
            self.f1 = stage(two, (buf.at[yl, x, every, lo], up), (buf.at[y, xl, every, hi], right))
            self.f2 = stage(
                four,
                (buf.at[yl, xl, every, lo], up), (buf.at[yr, xr, every, lo], down),
                (buf.at[yl, xl, every, hi], right), (buf.at[yr, xr, every, hi], left),
            )
            self.f3 = stage(two, (buf.at[yr, xo, every, lo], down), (buf.at[yo, xr, every, hi], left))
            self.stages = [self.zc, self.zd, self.n1, self.hq, self.cx, self.cy] + sum(self.cz, [])
            self.stages += [self.m1, self.m2, self.hp, self.hs, self.ho, self.f1, self.f2, self.f3]

        def event(self, k):
            after = {
                1: ((self.cx,), (self.cy,)), 2: ((self.zc,), (self.m1, self.hp)), 3: ((self.cy,), self.cz[0]),
                4: ((self.m1, self.n1), (self.m2, self.hs)), 5: ((self.hp, self.hq), (self.f1,)), 7: ((self.m2,), (self.ho,)),
                9: ((self.hs,), (self.f2,)), 11: ((self.ho,), (self.f3,)), 14: ((self.zd,), (self.n1, self.hq)),
            }
            if k in after:
                for stage in after[k][0]:
                    stage.arrive()
                for stage in after[k][1]:
                    stage.start()
            elif k in (6, 8, 10):
                ring = k // 2 - 2
                for i in range(2):
                    self.cz[ring - 1][i].arrive()
                    if i < len(self.cz[ring]):
                        self.cz[ring][i].start()
            elif k == 12:
                self.cz[3][0].arrive()
            else:
                self.f1.arrive()
                self.f2.arrive()
                self.f3.arrive()

        def all_sent(self):
            for stage in self.stages:
                stage.sent()

    w_gather = Gather(w)
    w_gather.cx.start()
    w_gather.zc.start()
    w_gather.zd.start()
    s_slots = [slot() for _ in range(4)]

    def s_copy(group, index):
        return remote(tsend.at[group], sg.at[4 * b + group], index, partner)

    def pair_step(group, p):
        n = group * 8 + 2 * p
        step = group * 4 + p
        for when, event in ((2, 1), (3, 2), (5, 3), (6, 14), (8, 4), (9, 5), (10, 6), (11, 7), (13, 8)):
            @pl.when(step == when)
            def _(event=event):
                w_gather.event(event)

        @pl.when(step == 4)
        def _():
            h_far.arrive()
            h_pass.start()

        for when, stage in ((2, 1), (4, 2), (6, 3), (8, 4)):
            @pl.when(step == when)
            def _(stage=stage):
                halo_arrive(stage)
                halo_start(stage + 1)

        win = window[...]
        h0, h1, h2 = sigv[n], sigv[n + 1], sigv[n + 2]
        a0, a1 = h0 * win, h1 * win
        b1, b2 = h1 - a1, h2 - h2 * win
        ev, ov = [], []
        for parity, block in ((0, jnp.concatenate([a0 + b1, a1 + b2], 1)), (1, jnp.concatenate([a0 - b1, a1 - b2], 1))):
            high, low = split(block)
            d_high, d_low = first[parity, 0], first[parity, 1]
            part = dot(d_high, high) + dot(d_high, low) + dot(d_low, high)
            (ev if parity == 0 else ov).append(part)
        pieces = []
        for frame in range(2):
            for parity, part in ((0, ev[0]), (1, ov[0])):
                real = part[:128, 128 * frame:128 * frame + 128]
                imag = part[128:, 128 * frame:128 * frame + 128]
                tc = tcos[128 * parity:128 * parity + 128, :]
                ts = tsin[128 * parity:128 * parity + 128, :]
                piece = jnp.concatenate([real * tc + imag * ts, imag * tc - real * ts], 1)
                if parity == 0:
                    zrow[pl.ds(2 * p + frame, 1), :] = piece[:1]
                pieces.append(piece)
        m_high, m_low = second[b, 0], second[b, 1]
        for frame in range(2):
            high, low = split(jnp.concatenate(pieces[2 * frame:2 * frame + 2], 0))
            out = dot(high, m_high) + dot(low, m_high) + dot(high, m_low)
            real, imag = out[:, :128], out[:, 128:]
            mag[2 * p + frame] = jnp.sqrt(real * real + imag * imag)

    lane = lax.broadcasted_iota(jnp.int32, (128, 128), 1)
    row = lax.broadcasted_iota(jnp.int32, (128, 128), 0)
    mirrored = lane // 32 % 2 == 1
    top = row == 0

    def turn(group, j):
        m = mag[j]
        low = jnp.concatenate([m[:64], m[128:192]], 0)
        high = jnp.concatenate([m[64:128], m[192:]], 0)
        extra = jnp.broadcast_to(mag0[pl.ds(j, 1), :], (128, 128))
        high_row = jnp.broadcast_to(high[:1], (128, 128))
        low = jnp.where(top, jnp.where(mirrored, high_row, extra), low)
        high = jnp.where(top & mirrored, extra, high)
        low, high = low.T, high.T
        for ref, index, off in ((sg, 4 * b + group, 0), (tsend, group, 64)):
            for value, place, part in ((low, 0, 0), (high, 1, 0), (high, 2, 1), (low, 3, 1)):
                ref[index, pl.ds(256 * place + j, 32, stride=8), :] = value[off + 32 * part:off + 32 * part + 32]

    def group_step(group, _):
        @pl.when(group == 0)
        def _():
            loads[0].wait()
            loads[1].wait()

        @pl.when(group == 1)
        def _():
            loads[2].wait()

        @pl.when(group == 2)
        def _():
            loads[3].wait()

        @pl.when(group == 3)
        def _():
            halo_arrive(0)
            halo_arrive(5)
            line = jnp.where(y < 3, 2, jnp.where(x < 3, 3, 4))
            source = jnp.where(b == 0, 0, jnp.where(z_hi < 3, 1, line))
            keep = jnp.where(t * 8 + f == 255, 0, 1)

            @pl.when(keep == 1)
            def _():
                sigv[32] = hop[source]

            @pl.when(keep == 0)
            def _():
                sigv[32] = jnp.zeros((256, 128), F32)

        def body(p, _):
            pair_step(group, p)
            return 0

        lax.fori_loop(0, 4, body, 0)
        high, low = split(zrow[...])
        out = dot(high, special[b, 0]) + dot(low, special[b, 0]) + dot(high, special[b, 1])
        mag0[...] = jnp.sqrt(out[:, :128] * out[:, :128] + out[:, 128:] * out[:, 128:])

        def turn_body(j, _):
            turn(group, 2 * j)
            turn(group, 2 * j + 1)
            return 0

        lax.fori_loop(0, 4, turn_body, 0)
        for g in range(4):
            @pl.when(group == g)
            def _(g=g):
                s_copy(g, s_slots[g]).start()
        return 0

    lax.fori_loop(0, 4, group_step, 0)

    h_near.arrive()
    h_pass.arrive()
    rows64 = hg[...].reshape(64, 256)
    ht[...] = jnp.concatenate([rows64, rows64], 0).T
    h2 = ht[pl.ds(pl.multiple_of(64 * z_hi, 64), 64), :]
    for g in range(4):
        s_copy(g, s_slots[g]).wait_recv()

    def frames_block(yy, xx):
        cols = []
        for k in range(8):
            place = pl.multiple_of(((yy * 4 + xx) * 8 + k) * 8, 8)
            cols.append(jnp.concatenate([sg[g, pl.ds(place, 8), :] for g in range(8)], 0))
        return jnp.concatenate(cols, 1)

    def ratio_of(buf, lhs, yy, xx):
        wide = jnp.concatenate([buf[yy, xx, k] for k in range(8)], 1)
        high, low = split(wide)
        approx = dot(lhs, jnp.concatenate([high, high, low, low], 0))
        return frames_block(yy, xx) / approx, high, low

    def gain_block(buf, lhs, yy, xx):
        ratio, high, low = ratio_of(buf, lhs, yy, xx)
        r_high, r_low = split(ratio)
        left = jnp.concatenate([r_high, r_low, jnp.ones((16, 1024), BF16)], 0)
        acc[...] += dot_t(left, jnp.concatenate([high, low], 0))

    def gain(stage, index):
        total = acc[...]
        part = jnp.concatenate([total[:64] + total[64:128], total[128:136]], 0)
        stage_send, stage_recv = stage
        stage_send[...] = part + pltpu.roll(part, 64, 1)
        copy = remote(stage_send, stage_recv, index, partner)
        copy.start()
        copy.wait_recv()
        both = stage_send[...] + stage_recv[...]
        return both[:64] / both[64:65], copy

    lhs1 = doubled(h2)
    acc[...] = jnp.zeros_like(acc)

    def gain_all(buf, lhs, gather):
        def near_body(i, _):
            gain_block(buf, lhs, (y + 3 + i // 3) % 4, (x + 3 + i % 3) % 4)
            return 0

        def far_body(i, _):
            gain_block(buf, lhs, (y + 2) % 4, i)
            return 0

        def side_body(i, _):
            gain_block(buf, lhs, (y + 3 + i) % 4, (x + 2) % 4)
            return 0

        gather.event(12)
        lax.fori_loop(0, 4, near_body, 0)
        gather.event(11)
        lax.fori_loop(4, 9, near_body, 0)
        gather.event(13)
        lax.fori_loop(0, 4, far_body, 0)
        lax.fori_loop(0, 3, side_body, 0)

    for event in (9, 10):
        w_gather.event(event)
    gain_all(w, lhs1, w_gather)
    gain1, mid_copy = gain((sx, rx), slot())
    mid = h2 * gain1
    mid_lhs = doubled(mid)
    mid_t = jnp.concatenate([mid, mid], 0).T
    mid_left = doubled(mid_t[:64])

    tsx[...] = jnp.broadcast_to(jnp.sum(mid, axis=0, keepdims=True), (8, 128))
    tx_copies = group(trx, *[(tsx, trx.at[d - 1], at_x(d)) for d in (1, 2, 3)])
    tx_copies.start()

    def num_block(yy, xx):
        ratio, _, _ = ratio_of(w, mid_lhs, yy, xx)
        high, low = split(ratio)
        out = dot(mid_left, jnp.concatenate([high, high, low, low], 0))
        for k in range(8):
            num[yy, xx, k] = out[:, 128 * k:128 * k + 128]

    def num_run(blocks):
        def body(i, _):
            dy, dx = blocks(i)
            num_block((y + dy) % 4, (x + dx) % 4)
            return 0
        return body

    def run(count, blocks):
        lax.fori_loop(0, count, num_run(blocks), 0)

    def part_a(place, part, rows=every):
        return num.at[place, part, rows, lo]

    def part_b(place, part, rows=every):
        return num.at[part, place, rows, hi]

    two, four = num.at[0, pl.ds(0, 2), every, lo], num.at[0, every, every, lo]
    colours = (
        (part_a, (y, yr, yl, yo), (x, xr, xl, xo), ha1, ha2, at_y(1), at_y(3)),
        (part_b, (x, xr, xl, xo), (y, yr, yl, yo), hb1, hb2, at_x(1), at_x(3)),
    )
    travels = {3: 0, 2: 0, 1: 1, 0: 1}

    def wave(like, moves):
        copies = []
        for get, places, parts, once, twice, right, left in colours:
            for place, part, side in moves:
                target = once.at[part] if place == 3 else twice.at[side, part]
                copies.append((get(places[place], parts[part]), target, right if side == 0 else left))
        return group(like, *copies)

    w1 = wave(four, ((3, 3, 0), (3, 1, 1)))
    w2 = wave(four, ((3, 2, 0), (3, 0, 1)))
    e1 = wave(four, ((1, 1, 0), (2, 3, 1)))
    e2 = wave(four, ((1, 0, 0), (2, 2, 1)))
    l1 = wave(four, ((1, 3, 0), (2, 1, 1)))
    l2 = wave(four, ((1, 2, 0), (2, 0, 1)))

    def pass_on(parts_now):
        for get, places, parts, once, twice, right, left in colours:
            for part in parts_now:
                target = get(places[1 + travels[part]], parts[part])
                target[...] = target[...] + once[part]

    def settle(parts_now):
        for get, places, parts, once, twice, right, left in colours:
            for part in parts_now:
                target = get(places[0], parts[part])
                target[...] = target[...] + (twice[0, part] + twice[1, part])

    def mid_moves(like, moves):
        copies = []
        for (get, places, parts, _, _, _, _), (once, twice), right, left in (
            (colours[0], (ma1, ma2), at_x(1), at_x(3)), (colours[1], (mb1, mb2), at_y(1), at_y(3)),
        ):
            for part, h, side in moves:
                target = once.at[side] if part == 3 else twice.at[side, quad[h]]
                copies.append((get(places[0], parts[part], quad[h]), target, right if side == 0 else left))
        return group(like, *copies)

    mf = mid_moves(two, ((3, 0, 0), (3, 1, 1)))
    me1 = mid_moves(num.at[0, 0, every, lo], ((1, 1, 0),))
    me2 = mid_moves(num.at[0, 0, every, lo], ((2, 0, 1),))
    ml = mid_moves(two, ((1, 0, 0), (2, 1, 1)))

    def chosen(order):
        def blocks(i):
            dy = sum(jnp.where(i == k, v[0], 0) for k, v in enumerate(order))
            dx = sum(jnp.where(i == k, v[1], 0) for k, v in enumerate(order))
            return dy, dx
        run(len(order), blocks)

    run(4, lambda i: (2, i))
    w1.start(0, 1)
    w2.start(0, 1)
    run(3, lambda i: ((i + 3) % 4, 2))
    w1.start(2, 3)
    w2.start(2, 3)
    chosen([(1, 1), (1, 0), (3, 3), (0, 1)])
    e1.start()
    chosen([(1, 3), (3, 1), (3, 0), (0, 3), (0, 0)])

    def zz(d):
        return (z + 8 + d) % 8

    ring1 = group(
        c1,
        (num.at[half[0], every, zz(4), end], c1.at[0], at_z(1)), (num.at[half[1], every, zz(4), end], c1.at[1], at_z(7)),
    )
    ring1.start()

    def ring_send(buf, d):
        copies = group(
            buf,
            (num.at[every, every, zz(d), end], buf.at[0], at_z(1)), (num.at[every, every, zz(-d), end], buf.at[1], at_z(7)),
        )
        copies.start()
        return copies

    def ring_add(buf, d):
        for side, place in ((0, zz(d)), (1, zz(-d))):
            target = num.at[every, every, place, end]
            target[...] = target[...] + buf[side]

    tx_copies.arrive()
    tsy[...] = tsx[...] + trx[0] + trx[1] + trx[2]
    ty_copies = group(try_, *[(tsy, try_.at[d - 1], at_y(d)) for d in (1, 2, 3)])
    ty_copies.start()
    w1.arrive()
    pass_on((3, 1))
    l1.start()
    e2.start()
    ring1.arrive()
    for side, place in ((0, zz(3)), (1, zz(-3))):
        target = num.at[half[side], every, place, end]
        target[...] = target[...] + c1[side]
    ring2 = ring_send(c2, 3)
    w2.arrive()
    pass_on((2, 0))
    l2.start()
    ty_copies.arrive()
    tsz[...] = tsy[...] + try_[0] + try_[1] + try_[2]
    tz_copies = group(trz, *[(tsz, trz.at[d - 1], at_z(d)) for d in range(1, 8)])
    tz_copies.start()
    ring2.arrive()
    ring_add(c2, 2)
    ring3 = ring_send(c3, 2)
    e1.arrive()
    l1.arrive()
    settle((3, 1))
    mf.start()
    me1.start()
    ring3.arrive()
    ring_add(c3, 1)
    ring4 = ring_send(c4, 1)
    e2.arrive()
    l2.arrive()
    settle((2, 0))
    me2.start()
    ring4.arrive()
    target = num.at[every, every, z, end]
    target[...] = target[...] + (c4[0] + c4[1])
    cy_copies = group(cyb, *[(num.at[(y + d) % 4, every, z, end], cyb.at[d - 1], at_y(d)) for d in (1, 2, 3)])
    cy_copies.start()
    mf.arrive()
    for get, places, parts, once in ((part_a, (y,), (x, xr, xl), ma1), (part_b, (x,), (y, yr, yl), mb1)):
        for side in (0, 1):
            target = get(places[0], parts[1 + side], quad[side])
            target[...] = target[...] + once[side]
    ml.start()
    tz_copies.arrive()
    totals = tsz[...]
    for d in range(7):
        totals = totals + trz[d]
    totals = jnp.broadcast_to(totals[:1], (128, 128)).T[:64]
    cy_copies.arrive()
    target = num.at[y, every, z, end]
    target[...] = target[...] + (cyb[0] + cyb[1] + cyb[2])
    cx_copies = group(cxb, *[(num.at[y, (x + d) % 4, z, end], cxb.at[d - 1], at_x(d)) for d in (1, 2, 3)])
    cx_copies.start()
    me1.arrive()
    me2.arrive()
    ml.arrive()
    for get, place, part, twice in ((part_a, y, x, ma2), (part_b, x, y, mb2)):
        target = get(place, part)
        target[...] = target[...] + (twice[0] + twice[1])
    z_copies = group(rz, *[(num.at[y, x, zz(d), low_rows], rz.at[d - 1], at_z(d)) for d in range(1, 8)])
    z_copies.start()
    cx_copies.arrive()
    whole = num[y, x, z, end] + (cxb[0] + cxb[1] + cxb[2])
    wn[y, x, z, end] = w[y, x, z, end] * (whole / totals[48:])
    w_gather.all_sent()
    n_gather = Gather(wn)
    n_gather.cx.start()
    z_copies.arrive()
    whole = num[y, x, z, low_rows]
    for d in range(7):
        whole = whole + rz[d]
    wn[y, x, z, low_rows] = w[y, x, z, low_rows] * (whole / totals[:48])
    n_gather.zc.start()
    n_gather.zd.start()

    out_templ[...] = moved(wn[y, x, z], perms[2 * flip + 1])
    acc[...] = jnp.zeros_like(acc)
    for event in (1, 2, 3, 14, 6, 4, 5, 7, 8, 9, 10):
        n_gather.event(event)
    gain_all(wn, mid_lhs, n_gather)
    gain2, last_copy = gain((sy, ry), slot())
    final = mid * gain2
    fin[...] = jnp.concatenate([final, final], 0).T
    f_copies = group(
        fo.at[pl.ds(0, 3)],
        *[
            (fin.at[pl.ds(pl.multiple_of(8 * ((f + d) % 8), 8), 8)], fo.at[z_hi], at_z(d))
            for d in (2, 4, 6)
        ],
    )
    f_copies.start()
    fo[pl.ds(z_hi, 1)] = fin[pl.ds(pl.multiple_of(8 * f, 8), 8), :][None]
    for copy, sends, _ in halos:
        @pl.when(sends)
        def _(copy=copy):
            copy.wait_send()

    n_gather.all_sent()
    for g in range(4):
        s_copy(g, s_slots[g]).wait_send()
    sent([mid_copy, last_copy])
    for part in groups:
        part.sent()
    f_copies.arrive()
    assert used[0] <= COPIES, used[0]
    out_act[...] = fo[...]


def finish(parts, templ, out_act, out_templ):
    near = lax.broadcasted_iota(jnp.int32, (8, 128), 1) < 64
    out_act[:, :128] = jnp.where(near, parts[0], parts[1])
    out_act[:, 128:] = jnp.where(near, parts[2], parts[3])
    out_templ[...] = templ[...]


COPIES = 57


def on_device(signal, templates, activations):
    tables = build_tables()
    vmem = pl.BlockSpec(memory_space=pltpu.VMEM)
    f32 = lambda *shape: pltpu.VMEM(shape, F32)
    parts, templ = pl.pallas_call(
        kernel,
        out_shape=(jax.ShapeDtypeStruct((4, 8, 128), F32), jax.ShapeDtypeStruct((64, 128), F32)),
        in_specs=[pl.BlockSpec(memory_space=pl.ANY)] + [vmem] * 9,
        out_specs=(vmem, vmem),
        scratch_shapes=[
            f32(33, 256, 128),
            f32(8, 8, 256),
            f32(256, 128),
            f32(8, 256, 128),
            f32(16, 256),
            f32(16, 128),
            f32(8, 1024, 128),
            f32(4, 1024, 128),
            f32(4, 4, 8, 64, 128),
            f32(4, 4, 8, 64, 128),
            f32(4, 4, 8, 64, 128),
            f32(4, 8, 24, 128),
            f32(2, 4, 8, 24, 128),
            f32(4, 8, 24, 128),
            f32(2, 4, 8, 24, 128),
            f32(2, 4, 24, 128),
            f32(2, 8, 24, 128),
            f32(2, 4, 24, 128),
            f32(2, 8, 24, 128),
            f32(2, 2, 4, 16, 128),
            f32(2, 4, 4, 16, 128),
            f32(2, 4, 4, 16, 128),
            f32(2, 4, 4, 16, 128),
            f32(3, 4, 16, 128),
            f32(3, 16, 128),
            f32(7, 48, 128),
            f32(6, 256, 128),
            f32(144, 128),
            f32(72, 128), f32(72, 128), f32(72, 128), f32(72, 128),
            f32(8, 128),
            f32(3, 8, 128), f32(3, 8, 128), f32(7, 8, 128),
            f32(8, 128), f32(8, 128),
            f32(128, 128),
            f32(4, 8, 128),
            pltpu.SemaphoreType.DMA((4,)),
            pltpu.SemaphoreType.DMA((COPIES,)),
            pltpu.SemaphoreType.DMA((COPIES,)),
        ],
        compiler_params=pltpu.CompilerParams(
            collective_id=0, has_side_effects=True, vmem_limit_bytes=60 * 1024 * 1024
        ),
    )(signal.reshape(32, 256, 128), templates, activations, *tables)
    return pl.pallas_call(
        finish,
        out_shape=(jax.ShapeDtypeStruct((8, 256), F32), jax.ShapeDtypeStruct((64, 128), F32)),
        in_specs=[vmem, vmem],
        out_specs=(vmem, vmem),
    )(parts, templ)


def solution(mesh):
    return jax.shard_map(
        on_device,
        mesh=mesh,
        in_specs=(P("frames", "freq", None), P(None, ("freq", "frames")), P("freq", "frames")),
        out_specs=(P("freq", "frames"), P(None, ("freq", "frames"))),
        check_vma=False,
    )
```

```python
import math

import jax
import jax.numpy as jnp
import ml_dtypes
import numpy as np
from jax import lax
from jax.experimental import pallas as pl
from jax.experimental.pallas import tpu as pltpu
from jax.sharding import PartitionSpec as P

MESH = pl.DeviceIdType.MESH
F32 = jnp.float32
BF16 = jnp.bfloat16


def halves(table):
    high = table.astype(ml_dtypes.bfloat16)
    low = (table - high.astype(np.float64)).astype(ml_dtypes.bfloat16)
    return high, low


def build_tables():
    rows = np.arange(256)
    lanes = np.arange(128)
    m = (rows[:, None] * 128 + lanes[None, :]).astype(np.float64)
    window = (0.5 - 0.5 * np.cos(2 * math.pi / 65536 * m)).astype(np.float32)
    first = []
    twiddle = []
    for odd in (0, 1):
        k1 = 2 * np.arange(128) + odd
        angle = 2 * math.pi / 512 * (k1[:, None] * rows[None, :] % 512)
        real, imag = np.cos(angle), -np.sin(angle)
        if not odd:
            imag[0] = 1.0 - 2.0 * (rows % 2)
        first.append(np.concatenate([real, imag], 0))
        twiddle.append(2 * math.pi / 65536 * (k1[:, None] * lanes[None, :]))
    twiddle = np.concatenate(twiddle, 0)
    first = np.stack([np.stack(halves(part)) for part in first])
    second = []
    special = []
    lam = np.arange(128)
    z, x, rev, other = lam % 8, lam // 8 % 4, lam // 32 % 2, lam // 64
    for core in (0, 1):
        base = 8 * (2 * (z // 2) + (core ^ other)) + 4 * (z % 2) + x
        k2 = np.where(rev == 1, 127 - base, base)
        angle = 2 * math.pi / 128 * (lanes[:, None] * k2[None, :] % 128)
        cos, sin = np.cos(angle) / 32, np.sin(angle) / 32
        second.append(np.stack(halves(np.concatenate([np.concatenate([cos, -sin], 1), np.concatenate([sin, cos], 1)], 0))))
        angle = 2 * math.pi / 128 * (lanes[:, None] * (base + 0.5 * rev)[None, :])
        cos, sin = np.cos(angle) / 32, np.sin(angle) / 32
        keep, turn = (1 - rev)[None, :], rev[None, :]
        special.append(
            np.stack(
                halves(
                    np.concatenate(
                        [np.concatenate([cos * keep, -sin * keep], 1), np.concatenate([cos * turn, -sin * turn], 1)], 0
                    )
                )
            )
        )
    sigma = np.where(lanes < 64, 2 * lanes, 2 * (lanes - 64) + 1)
    perms = []
    for order in (sigma, (128 - sigma) % 128):
        perm = np.zeros((128, 128))
        perm[order, lanes] = 1.0
        perms += [perm, perm.T]
    perms = np.stack(perms).astype(ml_dtypes.bfloat16)
    return (
        window,
        np.cos(twiddle).astype(np.float32),
        np.sin(twiddle).astype(np.float32),
        first,
        np.stack(second),
        np.stack(special),
        perms,
    )


def split(value):
    high = value.astype(BF16)
    return high, (value - high.astype(F32)).astype(BF16)


def dot(a, b):
    return jnp.dot(a, b, preferred_element_type=F32)


def dot_t(a, b):
    return lax.dot_general(a, b, (((1,), (1,)), ((), ())), preferred_element_type=F32)


def moved(value, perm):
    high = value.astype(BF16)
    rest = value - high.astype(F32)
    middle = rest.astype(BF16)
    low = (rest - middle.astype(F32)).astype(BF16)
    return dot(high, perm) + dot(middle, perm) + dot(low, perm)


def doubled(value):
    high, low = split(value)
    lane = lax.broadcasted_iota(jnp.int32, value.shape, 1)
    both = jnp.where(lane < 64, high.astype(F32), low.astype(F32)).astype(BF16)
    return jnp.concatenate([both, both], 1)


def kernel(
    sig_hbm, templ, act, window, tcos, tsin, first, second, special, perms,
    out_act, out_templ,
    sigv, hg, ht, mag, zrow, mag0, sg, tsend, w, wn, num,
    ha1, ha2, hb1, hb2, ma1, ma2, mb1, mb2, c1, c2, c3, c4, cyb, cxb, rz,
    hop, acc, sx, rx, sy, ry, tsx, trx, try_, trz, tsy, tsz, fin, fo,
    lsem, ssem, rsem,
):
    f = lax.axis_index("freq")
    t = lax.axis_index("frames")
    b = f % 2
    z_hi = f // 2
    z_lo = t // 16
    x = t // 4 % 4
    y = t % 4
    z = z_hi * 2 + z_lo
    partner = (f + 1 - 2 * b, t)

    def at_x(d):
        return (f, z_lo * 16 + (x + d) % 4 * 4 + y)

    def at_y(d):
        return (f, z_lo * 16 + x * 4 + (y + d) % 4)

    def at_z(d):
        other = (z + d) % 8
        return (other // 2 * 2 + b, other % 2 * 16 + x * 4 + y)

    greet = [partner] + [at_x(d) for d in (1, 2, 3)] + [at_y(d) for d in (1, 2, 3)]
    greet += [at_z(d) for d in range(1, 8)]
    barrier = pltpu.get_barrier_semaphore()
    for device in greet:
        pl.semaphore_signal(barrier, inc=1, device_id=device, device_id_type=MESH)
    loads = [
        pltpu.make_async_copy(sig_hbm.at[pl.ds(8 * i, 8)], sigv.at[pl.ds(8 * i, 8)], lsem.at[i]) for i in range(4)
    ]
    for load in loads:
        load.start()
    flip = y // 2
    w[y, x, z] = moved(templ[...], perms[2 * flip])
    hg[pl.ds(f, 1)] = act[...][None]
    zrow[...] = jnp.zeros_like(zrow)

    used = [0]

    def slot():
        used[0] += 1
        return used[0] - 1

    def remote(src, dst, index, device):
        return pltpu.make_async_remote_copy(
            src_ref=src, dst_ref=dst, send_sem=ssem.at[index], recv_sem=rsem.at[index],
            device_id=device, device_id_type=MESH,
        )

    class Group:
        def __init__(self, index, like, *copies):
            self.index, self.like = index, like
            self.copies = [remote(src, dst, index, device) for src, dst, device in copies]

        def start(self, *which):
            for i in which or range(len(self.copies)):
                self.copies[i].start()

        def arrive(self):
            pltpu.make_async_copy(self.like, self.like, rsem.at[self.index]).wait()

        def sent(self):
            pltpu.make_async_copy(self.like, self.like, ssem.at[self.index]).wait()

    groups = []

    def group(like, *copies):
        groups.append(Group(slot(), like, *copies))
        return groups[-1]

    turn_y = (b == 1) & (z_hi == 3)
    turn_x = turn_y & (y == 3)
    turn_z = turn_x & (x == 3)
    halos = [
        (sig_hbm.at[0], hop.at[0], partner, b == 1, b == 0),
        (sig_hbm.at[0], hop.at[5], at_z(6), b == 0, b == 0),
        (hop.at[5], hop.at[1], partner, b == 0, b == 1),
        (hop.at[1], hop.at[2], at_y(3), turn_y, turn_y),
        (hop.at[2], hop.at[3], at_x(3), turn_x, turn_x),
        (hop.at[3], hop.at[4], at_z(7), turn_z & (z_lo == 1), turn_z & (z_lo == 0)),
    ]
    halos = [(remote(src, dst, slot(), device), sends, receives) for src, dst, device, sends, receives in halos]

    def halo_start(k):
        @pl.when(halos[k][1])
        def _():
            halos[k][0].start()

    def halo_arrive(k):
        @pl.when(halos[k][2])
        def _():
            halos[k][0].wait_recv()

    h_far = group(hg.at[pl.ds(0, 3)], *[(act, hg.at[f], at_z(d)) for d in (2, 4, 6)])
    h_near = group(hg.at[0], (act, hg.at[f], partner))
    h_pass = group(hg.at[pl.ds(0, 3)], *[(hg.at[(f + d) % 8], hg.at[(f + d) % 8], partner) for d in (2, 4, 6)])

    lo, hi, low_rows = pl.ds(0, 24), pl.ds(24, 24), pl.ds(0, 48)
    end = pl.ds(48, 16)
    half = (pl.ds(0, 2), pl.ds(2, 2))
    quad = (pl.ds(0, 4), pl.ds(4, 4))
    every = slice(None)
    yl, yr, yo = (y + 3) % 4, (y + 1) % 4, (y + 2) % 4
    xl, xr, xo = (x + 3) % 4, (x + 1) % 4, (x + 2) % 4

    def start(copies):
        for copy in copies:
            copy.start()

    def arrive(copies):
        for copy in copies:
            copy.wait_recv()

    def sent(copies):
        for copy in copies:
            copy.wait_send()

    gather_slots = [slot() for _ in range(18)]

    class Gather:
        def __init__(self, buf):
            count = [0]

            def stage(like, *moves):
                count[0] += 1
                return Group(gather_slots[count[0] - 1], like, *[(region, region, device) for region, device in moves])

            up, down, right, left = at_y(1), at_y(3), at_x(1), at_x(3)
            self.zc = stage(rz, *[(buf.at[y, x, z, low_rows], at_z(d)) for d in range(1, 8)])
            self.cx = stage(cxb, *[(buf.at[y, x, z, end], at_x(d)) for d in (1, 2, 3)])
            self.cy = stage(cyb, *[(buf.at[y, every, z, end], at_y(d)) for d in (1, 2, 3)])
            self.cz = []
            for k in range(4):
                after, before = (z + 8 - k) % 8, (z + k) % 8
                ring = []
                for p, q in ((0, 1), (1, 0)) if k < 3 else ((0, 1),):
                    ring.append(stage(
                        c1, (buf.at[half[p], every, after, end], at_z(1)), (buf.at[half[q], every, before, end], at_z(7)),
                    ))
                self.cz.append(ring)
            two, four = buf.at[0, pl.ds(0, 2), every, lo], buf.at[0, every, every, lo]
            eight = buf.at[pl.ds(0, 2), every, every, lo]
            a_own, b_own = buf.at[y, x, every, lo], buf.at[y, x, every, hi]
            self.m1 = stage(four, (a_own, right), (a_own, left), (b_own, up), (b_own, down))
            self.m2 = stage(
                two,
                (buf.at[y, xl, quad[0], lo], right), (buf.at[y, xr, quad[1], lo], left),
                (buf.at[yl, x, quad[0], hi], up), (buf.at[yr, x, quad[1], hi], down),
            )
            self.hp = stage(four, (a_own, up), (a_own, down), (b_own, right), (b_own, left))

            def bulk(xx, yy):
                a_part, b_part = buf.at[y, xx, every, lo], buf.at[yy, x, every, hi]
                return [(a_part, up), (a_part, down), (b_part, right), (b_part, left)]

            self.hs = stage(eight, *(bulk(xl, yl) + bulk(xr, yr)))
            self.ho = stage(four, *bulk(xo, yo))
            self.f1 = stage(two, (buf.at[yl, x, every, lo], up), (buf.at[y, xl, every, hi], right))
            self.f2 = stage(
                four,
                (buf.at[yl, xl, every, lo], up), (buf.at[yr, xr, every, lo], down),
                (buf.at[yl, xl, every, hi], right), (buf.at[yr, xr, every, hi], left),
            )
            self.f3 = stage(two, (buf.at[yr, xo, every, lo], down), (buf.at[yo, xr, every, hi], left))
            self.stages = [self.zc, self.cx, self.cy] + sum(self.cz, [])
            self.stages += [self.m1, self.m2, self.hp, self.hs, self.ho, self.f1, self.f2, self.f3]

        def event(self, k):
            after = {
                1: (self.cx, self.cy), 2: (self.zc, self.m1, self.hp), 3: (self.cy, *self.cz[0]),
                4: (self.m1, self.m2, self.hs), 5: (self.hp, self.f1), 7: (self.m2, self.ho),
                9: (self.hs, self.f2), 11: (self.ho, self.f3),
            }
            if k in after:
                after[k][0].arrive()
                for stage in after[k][1:]:
                    stage.start()
            elif k in (6, 8, 10):
                ring = k // 2 - 2
                for i in range(2):
                    self.cz[ring - 1][i].arrive()
                    if i < len(self.cz[ring]):
                        self.cz[ring][i].start()
            elif k == 12:
                self.cz[3][0].arrive()
            else:
                self.f1.arrive()
                self.f2.arrive()
                self.f3.arrive()

        def all_sent(self):
            for stage in self.stages:
                stage.sent()

    w_gather = Gather(w)
    s_slots = [slot() for _ in range(4)]

    def s_copy(group, index):
        return remote(tsend.at[group], sg.at[4 * b + group], index, partner)

    def exchange_step(step):
        for when, event in ((7, 1), (9, 2), (10, 3), (12, 4), (14, 5), (15, 6)):
            @pl.when(step == when)
            def _(event=event):
                w_gather.event(event)

        @pl.when(step == 8)
        def _():
            h_far.arrive()
            h_pass.start()

        for when, stage in ((6, 1), (8, 2), (10, 3), (11, 4)):
            @pl.when(step == when)
            def _(stage=stage):
                halo_arrive(stage)
                halo_start(stage + 1)

    def pair_step(group, p):
        n = group * 8 + 2 * p
        if not isinstance(group, int):
            exchange_step(group * 4 + p)
        win = window[...]
        h0, h1, h2 = sigv[n], sigv[n + 1], sigv[n + 2]
        a0, a1 = h0 * win, h1 * win
        b1, b2 = h1 - a1, h2 - h2 * win
        ev, ov = [], []
        for parity, block in ((0, jnp.concatenate([a0 + b1, a1 + b2], 1)), (1, jnp.concatenate([a0 - b1, a1 - b2], 1))):
            high, low = split(block)
            d_high, d_low = first[parity, 0], first[parity, 1]
            part = dot(d_high, high) + dot(d_high, low) + dot(d_low, high)
            (ev if parity == 0 else ov).append(part)
        pieces = []
        for frame in range(2):
            for parity, part in ((0, ev[0]), (1, ov[0])):
                real = part[:128, 128 * frame:128 * frame + 128]
                imag = part[128:, 128 * frame:128 * frame + 128]
                tc = tcos[128 * parity:128 * parity + 128, :]
                ts = tsin[128 * parity:128 * parity + 128, :]
                piece = jnp.concatenate([real * tc + imag * ts, imag * tc - real * ts], 1)
                if parity == 0:
                    zrow[pl.ds(2 * p + frame, 1), :] = piece[:1]
                pieces.append(piece)
        m_high, m_low = second[b, 0], second[b, 1]
        for frame in range(2):
            high, low = split(jnp.concatenate(pieces[2 * frame:2 * frame + 2], 0))
            out = dot(high, m_high) + dot(low, m_high) + dot(high, m_low)
            real, imag = out[:, :128], out[:, 128:]
            mag[2 * p + frame] = jnp.sqrt(real * real + imag * imag)

    lane = lax.broadcasted_iota(jnp.int32, (128, 128), 1)
    row = lax.broadcasted_iota(jnp.int32, (128, 128), 0)
    mirrored = lane // 32 % 2 == 1
    top = row == 0

    def turn(group, j):
        m = mag[j]
        low = jnp.concatenate([m[:64], m[128:192]], 0)
        high = jnp.concatenate([m[64:128], m[192:]], 0)
        extra = jnp.broadcast_to(mag0[pl.ds(j, 1), :], (128, 128))
        high_row = jnp.broadcast_to(high[:1], (128, 128))
        low = jnp.where(top, jnp.where(mirrored, high_row, extra), low)
        high = jnp.where(top & mirrored, extra, high)
        low, high = low.T, high.T
        for ref, index, off in ((sg, 4 * b + group, 0), (tsend, group, 64)):
            for value, place, part in ((low, 0, 0), (high, 1, 0), (high, 2, 1), (low, 3, 1)):
                ref[index, pl.ds(256 * place + j, 32, stride=8), :] = value[off + 32 * part:off + 32 * part + 32]

    def group_step(group, _):
        @pl.when(group == 1)
        def _():
            loads[2].wait()

        @pl.when(group == 2)
        def _():
            loads[3].wait()

        @pl.when(group == 3)
        def _():
            halo_arrive(0)
            halo_arrive(5)
            line = jnp.where(y < 3, 2, jnp.where(x < 3, 3, 4))
            source = jnp.where(b == 0, 0, jnp.where(z_hi < 3, 1, line))
            keep = jnp.where(t * 8 + f == 255, 0, 1)

            @pl.when(keep == 1)
            def _():
                sigv[32] = hop[source]

            @pl.when(keep == 0)
            def _():
                sigv[32] = jnp.zeros((256, 128), F32)

        transform(group)
        for g in range(1, 4):
            @pl.when(group == g)
            def _(g=g):
                s_copy(g, s_slots[g]).start()
        return 0

    def transform(group):
        def body(p, _):
            pair_step(group, p)
            return 0

        lax.fori_loop(0, 4, body, 0)
        high, low = split(zrow[...])
        out = dot(high, special[b, 0]) + dot(low, special[b, 0]) + dot(high, special[b, 1])
        mag0[...] = jnp.sqrt(out[:, :128] * out[:, :128] + out[:, 128:] * out[:, 128:])

        def turn_body(j, _):
            turn(group, 2 * j)
            turn(group, 2 * j + 1)
            return 0

        lax.fori_loop(0, 4, turn_body, 0)

    loads[0].wait()
    loads[1].wait()
    transform(0)
    pl.semaphore_wait(barrier, len(greet))
    w_gather.cx.start()
    w_gather.zc.start()
    h_far.start()
    h_near.start()
    halo_start(0)
    halo_start(1)
    s_copy(0, s_slots[0]).start()
    lax.fori_loop(1, 4, group_step, 0)

    h_near.arrive()
    h_pass.arrive()
    rows64 = hg[...].reshape(64, 256)
    ht[...] = jnp.concatenate([rows64, rows64], 0).T
    h2 = ht[pl.ds(pl.multiple_of(64 * z_hi, 64), 64), :]
    for g in range(4):
        s_copy(g, s_slots[g]).wait_recv()

    def frames_block(places):
        cols = []
        for yy, xx, k in places:
            place = pl.multiple_of(((yy * 4 + xx) * 8 + k) * 8, 8)
            cols.append(jnp.concatenate([sg[g, pl.ds(place, 8), :] for g in range(8)], 0))
        return jnp.concatenate(cols, 1)

    def ratio_of(buf, lhs, places):
        wide = jnp.concatenate([buf[place] for place in places], 1)
        high, low = split(wide)
        approx = dot(lhs, jnp.concatenate([high, high, low, low], 0))
        return frames_block(places) / approx, high, low

    def gain_block(buf, lhs, places):
        ratio, high, low = ratio_of(buf, lhs, places)
        r_high, r_low = split(ratio)
        left = jnp.concatenate([r_high, r_low, jnp.ones((16, 128 * len(places)), BF16)], 0)
        acc[...] += dot_t(left, jnp.concatenate([high, low], 0))

    def gain(stage, index):
        total = acc[...]
        part = jnp.concatenate([total[:64] + total[64:128], total[128:136]], 0)
        stage_send, stage_recv = stage
        stage_send[...] = part + pltpu.roll(part, 64, 1)
        copy = remote(stage_send, stage_recv, index, partner)
        copy.start()
        copy.wait_recv()
        both = stage_send[...] + stage_recv[...]
        return both[:64] / both[64:65], copy

    lhs1 = doubled(h2)
    acc[...] = jnp.zeros_like(acc)

    near = [(yy, xx) for yy in (yl, y, yr) for xx in (xl, x, xr)]
    far = [(yo, xx) for xx in (xl, x, xr, xo)] + [(yy, xo) for yy in (yl, y, yr)]

    def gain_all(buf, lhs, gather):
        def run_z(start, stop, which):
            def body(i, _):
                gain_block(buf, lhs, [(yy, xx, (z + i) % 8) for yy, xx in which])
                return 0

            lax.fori_loop(start, stop, body, 0)

        run_z(5, 8, near)
        gather.event(11)
        run_z(8, 12, near)
        gather.event(12)
        run_z(12, 13, near)
        gather.event(13)
        run_z(0, 8, far)

    for event in (7, 8, 9, 10):
        w_gather.event(event)
    gain_all(w, lhs1, w_gather)
    gain1, mid_copy = gain((sx, rx), slot())
    mid = h2 * gain1
    mid_lhs = doubled(mid)
    mid_t = jnp.concatenate([mid, mid], 0).T
    mid_left = doubled(mid_t[:64])

    tsx[...] = jnp.broadcast_to(jnp.sum(mid, axis=0, keepdims=True), (8, 128))
    tx_copies = group(trx, *[(tsx, trx.at[d - 1], at_x(d)) for d in (1, 2, 3)])
    tx_copies.start()

    def num_block(yy, xx):
        ratio, _, _ = ratio_of(w, mid_lhs, [(yy, xx, k) for k in range(8)])
        high, low = split(ratio)
        out = dot(mid_left, jnp.concatenate([high, high, low, low], 0))
        for k in range(8):
            num[yy, xx, k] = out[:, 128 * k:128 * k + 128]

    def num_run(blocks):
        def body(i, _):
            dy, dx = blocks(i)
            num_block((y + dy) % 4, (x + dx) % 4)
            return 0
        return body

    def run(count, blocks):
        lax.fori_loop(0, count, num_run(blocks), 0)

    def part_a(place, part, rows=every):
        return num.at[place, part, rows, lo]

    def part_b(place, part, rows=every):
        return num.at[part, place, rows, hi]

    two, four = num.at[0, pl.ds(0, 2), every, lo], num.at[0, every, every, lo]
    colours = (
        (part_a, (y, yr, yl, yo), (x, xr, xl, xo), ha1, ha2, at_y(1), at_y(3)),
        (part_b, (x, xr, xl, xo), (y, yr, yl, yo), hb1, hb2, at_x(1), at_x(3)),
    )
    travels = {3: 0, 2: 0, 1: 1, 0: 1}

    def wave(like, moves):
        copies = []
        for get, places, parts, once, twice, right, left in colours:
            for place, part, side in moves:
                target = once.at[part] if place == 3 else twice.at[side, part]
                copies.append((get(places[place], parts[part]), target, right if side == 0 else left))
        return group(like, *copies)

    w1 = wave(four, ((3, 3, 0), (3, 1, 1)))
    w2 = wave(four, ((3, 2, 0), (3, 0, 1)))
    e1 = wave(four, ((1, 1, 0), (2, 3, 1)))
    e2 = wave(four, ((1, 0, 0), (2, 2, 1)))
    l1 = wave(four, ((1, 3, 0), (2, 1, 1)))
    l2 = wave(four, ((1, 2, 0), (2, 0, 1)))

    def pass_on(parts_now):
        for get, places, parts, once, twice, right, left in colours:
            for part in parts_now:
                target = get(places[1 + travels[part]], parts[part])
                target[...] = target[...] + once[part]

    def settle(parts_now):
        for get, places, parts, once, twice, right, left in colours:
            for part in parts_now:
                target = get(places[0], parts[part])
                target[...] = target[...] + (twice[0, part] + twice[1, part])

    def mid_moves(like, moves):
        copies = []
        for (get, places, parts, _, _, _, _), (once, twice), right, left in (
            (colours[0], (ma1, ma2), at_x(1), at_x(3)), (colours[1], (mb1, mb2), at_y(1), at_y(3)),
        ):
            for part, h, side in moves:
                target = once.at[side] if part == 3 else twice.at[side, quad[h]]
                copies.append((get(places[0], parts[part], quad[h]), target, right if side == 0 else left))
        return group(like, *copies)

    mf = mid_moves(two, ((3, 0, 0), (3, 1, 1)))
    me1 = mid_moves(num.at[0, 0, every, lo], ((1, 1, 0),))
    me2 = mid_moves(num.at[0, 0, every, lo], ((2, 0, 1),))
    ml = mid_moves(two, ((1, 0, 0), (2, 1, 1)))

    def chosen(order):
        def blocks(i):
            dy = sum(jnp.where(i == k, v[0], 0) for k, v in enumerate(order))
            dx = sum(jnp.where(i == k, v[1], 0) for k, v in enumerate(order))
            return dy, dx
        run(len(order), blocks)

    run(4, lambda i: (2, i))
    w1.start(0, 1)
    w2.start(0, 1)
    run(3, lambda i: ((i + 3) % 4, 2))
    w1.start(2, 3)
    w2.start(2, 3)
    chosen([(1, 1), (1, 0), (3, 3), (0, 1)])
    e1.start()
    chosen([(1, 3), (3, 1), (3, 0), (0, 3), (0, 0)])

    def zz(d):
        return (z + 8 + d) % 8

    ring1 = group(
        c1,
        (num.at[half[0], every, zz(4), end], c1.at[0], at_z(1)), (num.at[half[1], every, zz(4), end], c1.at[1], at_z(7)),
    )
    ring1.start()

    def ring_send(buf, d):
        copies = group(
            buf,
            (num.at[every, every, zz(d), end], buf.at[0], at_z(1)), (num.at[every, every, zz(-d), end], buf.at[1], at_z(7)),
        )
        copies.start()
        return copies

    def ring_add(buf, d):
        for side, place in ((0, zz(d)), (1, zz(-d))):
            target = num.at[every, every, place, end]
            target[...] = target[...] + buf[side]

    tx_copies.arrive()
    tsy[...] = tsx[...] + trx[0] + trx[1] + trx[2]
    ty_copies = group(try_, *[(tsy, try_.at[d - 1], at_y(d)) for d in (1, 2, 3)])
    ty_copies.start()
    w1.arrive()
    pass_on((3, 1))
    l1.start()
    e2.start()
    ring1.arrive()
    for side, place in ((0, zz(3)), (1, zz(-3))):
        target = num.at[half[side], every, place, end]
        target[...] = target[...] + c1[side]
    ring2 = ring_send(c2, 3)
    w2.arrive()
    pass_on((2, 0))
    l2.start()
    ty_copies.arrive()
    tsz[...] = tsy[...] + try_[0] + try_[1] + try_[2]
    tz_copies = group(trz, *[(tsz, trz.at[d - 1], at_z(d)) for d in range(1, 8)])
    tz_copies.start()
    ring2.arrive()
    ring_add(c2, 2)
    ring3 = ring_send(c3, 2)
    e1.arrive()
    l1.arrive()
    settle((3, 1))
    mf.start()
    me1.start()
    ring3.arrive()
    ring_add(c3, 1)
    ring4 = ring_send(c4, 1)
    e2.arrive()
    l2.arrive()
    settle((2, 0))
    me2.start()
    ring4.arrive()
    target = num.at[every, every, z, end]
    target[...] = target[...] + (c4[0] + c4[1])
    cy_copies = group(cyb, *[(num.at[(y + d) % 4, every, z, end], cyb.at[d - 1], at_y(d)) for d in (1, 2, 3)])
    cy_copies.start()
    mf.arrive()
    for get, places, parts, once in ((part_a, (y,), (x, xr, xl), ma1), (part_b, (x,), (y, yr, yl), mb1)):
        for side in (0, 1):
            target = get(places[0], parts[1 + side], quad[side])
            target[...] = target[...] + once[side]
    ml.start()
    tz_copies.arrive()
    totals = tsz[...]
    for d in range(7):
        totals = totals + trz[d]
    totals = jnp.broadcast_to(totals[:1], (128, 128)).T[:64]
    cy_copies.arrive()
    target = num.at[y, every, z, end]
    target[...] = target[...] + (cyb[0] + cyb[1] + cyb[2])
    cx_copies = group(cxb, *[(num.at[y, (x + d) % 4, z, end], cxb.at[d - 1], at_x(d)) for d in (1, 2, 3)])
    cx_copies.start()
    me1.arrive()
    me2.arrive()
    ml.arrive()
    for get, place, part, twice in ((part_a, y, x, ma2), (part_b, x, y, mb2)):
        target = get(place, part)
        target[...] = target[...] + (twice[0] + twice[1])
    z_copies = group(rz, *[(num.at[y, x, zz(d), low_rows], rz.at[d - 1], at_z(d)) for d in range(1, 8)])
    z_copies.start()
    cx_copies.arrive()
    whole = num[y, x, z, end] + (cxb[0] + cxb[1] + cxb[2])
    wn[y, x, z, end] = w[y, x, z, end] * (whole / totals[48:])
    w_gather.all_sent()
    n_gather = Gather(wn)
    n_gather.cx.start()
    z_copies.arrive()
    whole = num[y, x, z, low_rows]
    for d in range(7):
        whole = whole + rz[d]
    wn[y, x, z, low_rows] = w[y, x, z, low_rows] * (whole / totals[:48])
    n_gather.zc.start()

    out_templ[...] = moved(wn[y, x, z], perms[2 * flip + 1])
    acc[...] = jnp.zeros_like(acc)
    for event in (1, 3, 2, 6, 4, 5, 7, 8, 9, 10):
        n_gather.event(event)
    gain_all(wn, mid_lhs, n_gather)
    gain2, last_copy = gain((sy, ry), slot())
    final = mid * gain2
    fin[...] = jnp.concatenate([final, final], 0).T
    f_copies = group(
        fo.at[pl.ds(0, 3)],
        *[
            (fin.at[pl.ds(pl.multiple_of(8 * ((f + d) % 8), 8), 8)], fo.at[z_hi], at_z(d))
            for d in (2, 4, 6)
        ],
    )
    f_copies.start()
    fo[pl.ds(z_hi, 1)] = fin[pl.ds(pl.multiple_of(8 * f, 8), 8), :][None]
    for copy, sends, _ in halos:
        @pl.when(sends)
        def _(copy=copy):
            copy.wait_send()

    n_gather.all_sent()
    for g in range(4):
        s_copy(g, s_slots[g]).wait_send()
    sent([mid_copy, last_copy])
    for part in groups:
        part.sent()
    f_copies.arrive()
    assert used[0] <= COPIES, used[0]
    out_act[...] = fo[...]


def finish(parts, templ, out_act, out_templ):
    near = lax.broadcasted_iota(jnp.int32, (8, 128), 1) < 64
    out_act[:, :128] = jnp.where(near, parts[0], parts[1])
    out_act[:, 128:] = jnp.where(near, parts[2], parts[3])
    out_templ[...] = templ[...]


COPIES = 54


def on_device(signal, templates, activations):
    tables = build_tables()
    vmem = pl.BlockSpec(memory_space=pltpu.VMEM)
    f32 = lambda *shape: pltpu.VMEM(shape, F32)
    parts, templ = pl.pallas_call(
        kernel,
        out_shape=(jax.ShapeDtypeStruct((4, 8, 128), F32), jax.ShapeDtypeStruct((64, 128), F32)),
        in_specs=[pl.BlockSpec(memory_space=pl.ANY)] + [vmem] * 9,
        out_specs=(vmem, vmem),
        scratch_shapes=[
            f32(33, 256, 128),
            f32(8, 8, 256),
            f32(256, 128),
            f32(8, 256, 128),
            f32(16, 256),
            f32(16, 128),
            f32(8, 1024, 128),
            f32(4, 1024, 128),
            f32(4, 4, 8, 64, 128),
            f32(4, 4, 8, 64, 128),
            f32(4, 4, 8, 64, 128),
            f32(4, 8, 24, 128),
            f32(2, 4, 8, 24, 128),
            f32(4, 8, 24, 128),
            f32(2, 4, 8, 24, 128),
            f32(2, 4, 24, 128),
            f32(2, 8, 24, 128),
            f32(2, 4, 24, 128),
            f32(2, 8, 24, 128),
            f32(2, 2, 4, 16, 128),
            f32(2, 4, 4, 16, 128),
            f32(2, 4, 4, 16, 128),
            f32(2, 4, 4, 16, 128),
            f32(3, 4, 16, 128),
            f32(3, 16, 128),
            f32(7, 48, 128),
            f32(6, 256, 128),
            f32(144, 128),
            f32(72, 128), f32(72, 128), f32(72, 128), f32(72, 128),
            f32(8, 128),
            f32(3, 8, 128), f32(3, 8, 128), f32(7, 8, 128),
            f32(8, 128), f32(8, 128),
            f32(128, 128),
            f32(4, 8, 128),
            pltpu.SemaphoreType.DMA((4,)),
            pltpu.SemaphoreType.DMA((COPIES,)),
            pltpu.SemaphoreType.DMA((COPIES,)),
        ],
        compiler_params=pltpu.CompilerParams(
            collective_id=0, has_side_effects=True, vmem_limit_bytes=60 * 1024 * 1024
        ),
    )(signal.reshape(32, 256, 128), templates, activations, *tables)
    return pl.pallas_call(
        finish,
        out_shape=(jax.ShapeDtypeStruct((8, 256), F32), jax.ShapeDtypeStruct((64, 128), F32)),
        in_specs=[vmem, vmem],
        out_specs=(vmem, vmem),
    )(parts, templ)


def solution(mesh):
    return jax.shard_map(
        on_device,
        mesh=mesh,
        in_specs=(P("frames", "freq", None), P(None, ("freq", "frames")), P("freq", "frames")),
        out_specs=(P("freq", "frames"), P(None, ("freq", "frames"))),
        check_vma=False,
    )
```

```python
import math

import jax
import jax.numpy as jnp
import ml_dtypes
import numpy as np
from jax import lax
from jax.experimental import pallas as pl
from jax.experimental.pallas import tpu as pltpu
from jax.sharding import PartitionSpec as P

MESH = pl.DeviceIdType.MESH
F32 = jnp.float32
BF16 = jnp.bfloat16


def halves(table):
    high = table.astype(ml_dtypes.bfloat16)
    low = (table - high.astype(np.float64)).astype(ml_dtypes.bfloat16)
    return high, low


def build_tables():
    rows = np.arange(256)
    lanes = np.arange(128)
    m = (rows[:, None] * 128 + lanes[None, :]).astype(np.float64)
    window = (0.5 - 0.5 * np.cos(2 * math.pi / 65536 * m)).astype(np.float32)
    first = []
    twiddle = []
    for odd in (0, 1):
        k1 = 2 * np.arange(128) + odd
        angle = 2 * math.pi / 512 * (k1[:, None] * rows[None, :] % 512)
        real, imag = np.cos(angle), -np.sin(angle)
        if not odd:
            imag[0] = 1.0 - 2.0 * (rows % 2)
        first.append(np.concatenate([real, imag], 0))
        twiddle.append(2 * math.pi / 65536 * (k1[:, None] * lanes[None, :]))
    twiddle = np.concatenate(twiddle, 0)
    first = np.stack([np.stack(halves(part)) for part in first])
    second = []
    special = []
    lam = np.arange(128)
    z, x, rev, other = lam % 8, lam // 8 % 4, lam // 32 % 2, lam // 64
    for core in (0, 1):
        base = 8 * (2 * (z // 2) + (core ^ other)) + 4 * (z % 2) + x
        k2 = np.where(rev == 1, 127 - base, base)
        angle = 2 * math.pi / 128 * (lanes[:, None] * k2[None, :] % 128)
        cos, sin = np.cos(angle) / 32, np.sin(angle) / 32
        second.append(np.stack(halves(np.concatenate([np.concatenate([cos, -sin], 1), np.concatenate([sin, cos], 1)], 0))))
        angle = 2 * math.pi / 128 * (lanes[:, None] * (base + 0.5 * rev)[None, :])
        cos, sin = np.cos(angle) / 32, np.sin(angle) / 32
        keep, turn = (1 - rev)[None, :], rev[None, :]
        special.append(
            np.stack(
                halves(
                    np.concatenate(
                        [np.concatenate([cos * keep, -sin * keep], 1), np.concatenate([cos * turn, -sin * turn], 1)], 0
                    )
                )
            )
        )
    sigma = np.where(lanes < 64, 2 * lanes, 2 * (lanes - 64) + 1)
    perms = []
    for order in (sigma, (128 - sigma) % 128):
        perm = np.zeros((128, 128))
        perm[order, lanes] = 1.0
        perms += [perm, perm.T]
    perms = np.stack(perms).astype(ml_dtypes.bfloat16)
    return (
        window,
        np.cos(twiddle).astype(np.float32),
        np.sin(twiddle).astype(np.float32),
        first,
        np.stack(second),
        np.stack(special),
        perms,
    )


def split(value):
    high = value.astype(BF16)
    return high, (value - high.astype(F32)).astype(BF16)


def dot(a, b):
    return jnp.dot(a, b, preferred_element_type=F32)


def dot_t(a, b):
    return lax.dot_general(a, b, (((1,), (1,)), ((), ())), preferred_element_type=F32)


def moved(value, perm):
    high = value.astype(BF16)
    rest = value - high.astype(F32)
    middle = rest.astype(BF16)
    low = (rest - middle.astype(F32)).astype(BF16)
    return dot(high, perm) + dot(middle, perm) + dot(low, perm)


def doubled(value):
    high, low = split(value)
    lane = lax.broadcasted_iota(jnp.int32, value.shape, 1)
    both = jnp.where(lane < 64, high.astype(F32), low.astype(F32)).astype(BF16)
    return jnp.concatenate([both, both], 1)


def kernel(
    sig_hbm, templ, act, window, tcos, tsin, first, second, special, perms,
    out_act, out_templ,
    sigv, hg, ht, mag, zrow, mag0, sg, tsend, w, wn, num,
    ha1, ha2, hb1, hb2, ma1, ma2, mb1, mb2, c1, c2, c3, c4, cyb, cxb, rz,
    acc, sx, rx, sy, ry, tsx, trx, try_, trz, tsy, tsz, fin, fo,
    lsem, ssem, rsem,
):
    f = lax.axis_index("freq")
    t = lax.axis_index("frames")
    b = f % 2
    z_hi = f // 2
    z_lo = t // 16
    x = t // 4 % 4
    y = t % 4
    z = z_hi * 2 + z_lo
    partner = (f + 1 - 2 * b, t)

    def at_x(d):
        return (f, z_lo * 16 + (x + d) % 4 * 4 + y)

    def at_y(d):
        return (f, z_lo * 16 + x * 4 + (y + d) % 4)

    def at_z(d):
        other = (z + d) % 8
        return (other // 2 * 2 + b, other % 2 * 16 + x * 4 + y)

    def at_line(d):
        place = (t * 8 + f + d + 256) % 256
        return (place % 8, place // 8)

    greet = [partner] + [at_x(d) for d in (1, 2, 3)] + [at_y(d) for d in (1, 2, 3)]
    greet += [at_z(d) for d in range(1, 8)] + [at_line(-1), at_line(1)]
    barrier = pltpu.get_barrier_semaphore()
    for device in greet:
        pl.semaphore_signal(barrier, inc=1, device_id=device, device_id_type=MESH)
    loads = [
        pltpu.make_async_copy(sig_hbm.at[pl.ds(8 * i, 8)], sigv.at[pl.ds(8 * i, 8)], lsem.at[i]) for i in range(4)
    ]
    for load in loads:
        load.start()
    flip = y // 2
    w[y, x, z] = moved(templ[...], perms[2 * flip])
    hg[pl.ds(f, 1)] = act[...][None]
    zrow[...] = jnp.zeros_like(zrow)
    pl.semaphore_wait(barrier, len(greet))

    used = [0]

    def slot():
        used[0] += 1
        return used[0] - 1

    def remote(src, dst, index, device):
        return pltpu.make_async_remote_copy(
            src_ref=src, dst_ref=dst, send_sem=ssem.at[index], recv_sem=rsem.at[index],
            device_id=device, device_id_type=MESH,
        )

    class Group:
        def __init__(self, index, like, *copies):
            self.index, self.like = index, like
            self.copies = [remote(src, dst, index, device) for src, dst, device in copies]

        def start(self, *which):
            for i in which or range(len(self.copies)):
                self.copies[i].start()

        def arrive(self):
            pltpu.make_async_copy(self.like, self.like, rsem.at[self.index]).wait()

        def sent(self):
            pltpu.make_async_copy(self.like, self.like, ssem.at[self.index]).wait()

    groups = []

    def group(like, *copies):
        groups.append(Group(slot(), like, *copies))
        return groups[-1]

    halo = remote(sig_hbm.at[0], sigv.at[32], slot(), at_line(-1))
    h_far = group(hg.at[pl.ds(0, 3)], *[(act, hg.at[f], at_z(d)) for d in (2, 4, 6)])
    h_near = group(hg.at[0], (act, hg.at[f], partner))
    h_pass = group(hg.at[pl.ds(0, 3)], *[(hg.at[(f + d) % 8], hg.at[(f + d) % 8], partner) for d in (2, 4, 6)])

    lo, hi, low_rows = pl.ds(0, 24), pl.ds(24, 24), pl.ds(0, 48)
    end = pl.ds(48, 16)
    half = (pl.ds(0, 2), pl.ds(2, 2))
    quad = (pl.ds(0, 4), pl.ds(4, 4))
    every = slice(None)
    yl, yr, yo = (y + 3) % 4, (y + 1) % 4, (y + 2) % 4
    xl, xr, xo = (x + 3) % 4, (x + 1) % 4, (x + 2) % 4

    def start(copies):
        for copy in copies:
            copy.start()

    def arrive(copies):
        for copy in copies:
            copy.wait_recv()

    def sent(copies):
        for copy in copies:
            copy.wait_send()

    gather_slots = [slot() for _ in range(18)]

    class Gather:
        def __init__(self, buf):
            count = [0]

            def stage(like, *moves):
                count[0] += 1
                return Group(gather_slots[count[0] - 1], like, *[(region, region, device) for region, device in moves])

            up, down, right, left = at_y(1), at_y(3), at_x(1), at_x(3)
            self.zc = stage(rz, *[(buf.at[y, x, z, low_rows], at_z(d)) for d in range(1, 8)])
            self.cx = stage(cxb, *[(buf.at[y, x, z, end], at_x(d)) for d in (1, 2, 3)])
            self.cy = stage(cyb, *[(buf.at[y, every, z, end], at_y(d)) for d in (1, 2, 3)])
            self.cz = []
            for k in range(4):
                after, before = (z + 8 - k) % 8, (z + k) % 8
                ring = []
                for p, q in ((0, 1), (1, 0)) if k < 3 else ((0, 1),):
                    ring.append(stage(
                        c1, (buf.at[half[p], every, after, end], at_z(1)), (buf.at[half[q], every, before, end], at_z(7)),
                    ))
                self.cz.append(ring)
            two, four = buf.at[0, pl.ds(0, 2), every, lo], buf.at[0, every, every, lo]
            eight = buf.at[pl.ds(0, 2), every, every, lo]
            a_own, b_own = buf.at[y, x, every, lo], buf.at[y, x, every, hi]
            self.m1 = stage(four, (a_own, right), (a_own, left), (b_own, up), (b_own, down))
            self.m2 = stage(
                two,
                (buf.at[y, xl, quad[0], lo], right), (buf.at[y, xr, quad[1], lo], left),
                (buf.at[yl, x, quad[0], hi], up), (buf.at[yr, x, quad[1], hi], down),
            )
            self.hp = stage(four, (a_own, up), (a_own, down), (b_own, right), (b_own, left))

            def bulk(xx, yy):
                a_part, b_part = buf.at[y, xx, every, lo], buf.at[yy, x, every, hi]
                return [(a_part, up), (a_part, down), (b_part, right), (b_part, left)]

            self.hs = stage(eight, *(bulk(xl, yl) + bulk(xr, yr)))
            self.ho = stage(four, *bulk(xo, yo))
            self.f1 = stage(two, (buf.at[yl, x, every, lo], up), (buf.at[y, xl, every, hi], right))
            self.f2 = stage(
                four,
                (buf.at[yl, xl, every, lo], up), (buf.at[yr, xr, every, lo], down),
                (buf.at[yl, xl, every, hi], right), (buf.at[yr, xr, every, hi], left),
            )
            self.f3 = stage(two, (buf.at[yr, xo, every, lo], down), (buf.at[yo, xr, every, hi], left))
            self.stages = [self.zc, self.cx, self.cy] + sum(self.cz, [])
            self.stages += [self.m1, self.m2, self.hp, self.hs, self.ho, self.f1, self.f2, self.f3]

        def event(self, k):
            after = {
                1: (self.cx, self.cy), 2: (self.zc, self.m1, self.hp), 3: (self.cy, *self.cz[0]),
                4: (self.m1, self.m2, self.hs), 5: (self.hp, self.f1), 7: (self.m2, self.ho),
                9: (self.hs, self.f2), 11: (self.ho, self.f3),
            }
            if k in after:
                after[k][0].arrive()
                for stage in after[k][1:]:
                    stage.start()
            elif k in (6, 8, 10):
                ring = k // 2 - 2
                for i in range(2):
                    self.cz[ring - 1][i].arrive()
                    if i < len(self.cz[ring]):
                        self.cz[ring][i].start()
            elif k == 12:
                self.cz[3][0].arrive()
            else:
                self.f1.arrive()
                self.f2.arrive()
                self.f3.arrive()

        def all_sent(self):
            for stage in self.stages:
                stage.sent()

    w_gather = Gather(w)
    w_gather.cx.start()
    w_gather.zc.start()
    h_far.start()
    h_near.start()
    halo.start()
    s_slots = [slot() for _ in range(4)]

    def s_copy(group, index):
        return remote(tsend.at[group], sg.at[4 * b + group], index, partner)

    def pair_step(group, p):
        n = group * 8 + 2 * p
        step = group * 4 + p
        for when, event in ((3, 1), (5, 2), (6, 3), (8, 4), (10, 5), (11, 6), (12, 7), (14, 8)):
            @pl.when(step == when)
            def _(event=event):
                w_gather.event(event)

        @pl.when(step == 7)
        def _():
            h_far.arrive()
            h_pass.start()

        win = window[...]
        h0, h1, h2 = sigv[n], sigv[n + 1], sigv[n + 2]
        a0, a1 = h0 * win, h1 * win
        b1, b2 = h1 - a1, h2 - h2 * win
        ev, ov = [], []
        for parity, block in ((0, jnp.concatenate([a0 + b1, a1 + b2], 1)), (1, jnp.concatenate([a0 - b1, a1 - b2], 1))):
            high, low = split(block)
            d_high, d_low = first[parity, 0], first[parity, 1]
            part = dot(d_high, high) + dot(d_high, low) + dot(d_low, high)
            (ev if parity == 0 else ov).append(part)
        pieces = []
        for frame in range(2):
            for parity, part in ((0, ev[0]), (1, ov[0])):
                real = part[:128, 128 * frame:128 * frame + 128]
                imag = part[128:, 128 * frame:128 * frame + 128]
                tc = tcos[128 * parity:128 * parity + 128, :]
                ts = tsin[128 * parity:128 * parity + 128, :]
                piece = jnp.concatenate([real * tc + imag * ts, imag * tc - real * ts], 1)
                if parity == 0:
                    zrow[pl.ds(2 * p + frame, 1), :] = piece[:1]
                pieces.append(piece)
        m_high, m_low = second[b, 0], second[b, 1]
        for frame in range(2):
            high, low = split(jnp.concatenate(pieces[2 * frame:2 * frame + 2], 0))
            out = dot(high, m_high) + dot(low, m_high) + dot(high, m_low)
            real, imag = out[:, :128], out[:, 128:]
            mag[2 * p + frame] = jnp.sqrt(real * real + imag * imag)

    lane = lax.broadcasted_iota(jnp.int32, (128, 128), 1)
    row = lax.broadcasted_iota(jnp.int32, (128, 128), 0)
    mirrored = lane // 32 % 2 == 1
    top = row == 0

    def turn(group, j):
        m = mag[j]
        low = jnp.concatenate([m[:64], m[128:192]], 0)
        high = jnp.concatenate([m[64:128], m[192:]], 0)
        extra = jnp.broadcast_to(mag0[pl.ds(j, 1), :], (128, 128))
        high_row = jnp.broadcast_to(high[:1], (128, 128))
        low = jnp.where(top, jnp.where(mirrored, high_row, extra), low)
        high = jnp.where(top & mirrored, extra, high)
        low, high = low.T, high.T
        for ref, index, off in ((sg, 4 * b + group, 0), (tsend, group, 64)):
            for value, place, part in ((low, 0, 0), (high, 1, 0), (high, 2, 1), (low, 3, 1)):
                ref[index, pl.ds(256 * place + j, 32, stride=8), :] = value[off + 32 * part:off + 32 * part + 32]

    def group_step(group, _):
        @pl.when(group == 0)
        def _():
            loads[0].wait()
            loads[1].wait()

        @pl.when(group == 1)
        def _():
            loads[2].wait()

        @pl.when(group == 2)
        def _():
            loads[3].wait()

        @pl.when(group == 3)
        def _():
            halo.wait_recv()
            sigv[32] = sigv[32] * jnp.where(t * 8 + f == 255, 0.0, 1.0)

        def body(p, _):
            pair_step(group, p)
            return 0

        lax.fori_loop(0, 4, body, 0)
        high, low = split(zrow[...])
        out = dot(high, special[b, 0]) + dot(low, special[b, 0]) + dot(high, special[b, 1])
        mag0[...] = jnp.sqrt(out[:, :128] * out[:, :128] + out[:, 128:] * out[:, 128:])

        def turn_body(j, _):
            turn(group, 2 * j)
            turn(group, 2 * j + 1)
            return 0

        lax.fori_loop(0, 4, turn_body, 0)
        for g in range(4):
            @pl.when(group == g)
            def _(g=g):
                s_copy(g, s_slots[g]).start()
        return 0

    lax.fori_loop(0, 4, group_step, 0)

    h_near.arrive()
    h_pass.arrive()
    rows64 = hg[...].reshape(64, 256)
    ht[...] = jnp.concatenate([rows64, rows64], 0).T
    h2 = ht[pl.ds(pl.multiple_of(64 * z_hi, 64), 64), :]
    for g in range(4):
        s_copy(g, s_slots[g]).wait_recv()

    def frames_block(places):
        cols = []
        for yy, xx, k in places:
            place = pl.multiple_of(((yy * 4 + xx) * 8 + k) * 8, 8)
            cols.append(jnp.concatenate([sg[g, pl.ds(place, 8), :] for g in range(8)], 0))
        return jnp.concatenate(cols, 1)

    def ratio_of(buf, lhs, places):
        wide = jnp.concatenate([buf[place] for place in places], 1)
        high, low = split(wide)
        approx = dot(lhs, jnp.concatenate([high, high, low, low], 0))
        return frames_block(places) / approx, high, low

    def gain_block(buf, lhs, places):
        ratio, high, low = ratio_of(buf, lhs, places)
        r_high, r_low = split(ratio)
        left = jnp.concatenate([r_high, r_low, jnp.ones((16, 128 * len(places)), BF16)], 0)
        acc[...] += dot_t(left, jnp.concatenate([high, low], 0))

    def gain(stage, index):
        total = acc[...]
        part = jnp.concatenate([total[:64] + total[64:128], total[128:136]], 0)
        stage_send, stage_recv = stage
        stage_send[...] = part + pltpu.roll(part, 64, 1)
        copy = remote(stage_send, stage_recv, index, partner)
        copy.start()
        copy.wait_recv()
        both = stage_send[...] + stage_recv[...]
        return both[:64] / both[64:65], copy

    lhs1 = doubled(h2)
    acc[...] = jnp.zeros_like(acc)

    near = [(yy, xx) for yy in (yl, y, yr) for xx in (xl, x, xr)]
    far = [(yo, xx) for xx in (xl, x, xr, xo)] + [(yy, xo) for yy in (yl, y, yr)]

    def gain_all(buf, lhs, gather):
        def run_z(start, stop, which):
            def body(i, _):
                gain_block(buf, lhs, [(yy, xx, (z + i) % 8) for yy, xx in which])
                return 0

            lax.fori_loop(start, stop, body, 0)

        run_z(5, 8, near)
        gather.event(11)
        run_z(8, 12, near)
        gather.event(12)
        run_z(12, 13, near)
        gather.event(13)
        run_z(0, 8, far)

    for event in (9, 10):
        w_gather.event(event)
    gain_all(w, lhs1, w_gather)
    gain1, mid_copy = gain((sx, rx), slot())
    mid = h2 * gain1
    mid_lhs = doubled(mid)
    mid_t = jnp.concatenate([mid, mid], 0).T
    mid_left = doubled(mid_t[:64])

    tsx[...] = jnp.broadcast_to(jnp.sum(mid, axis=0, keepdims=True), (8, 128))
    tx_copies = group(trx, *[(tsx, trx.at[d - 1], at_x(d)) for d in (1, 2, 3)])
    tx_copies.start()

    def num_block(yy, xx):
        ratio, _, _ = ratio_of(w, mid_lhs, [(yy, xx, k) for k in range(8)])
        high, low = split(ratio)
        out = dot(mid_left, jnp.concatenate([high, high, low, low], 0))
        for k in range(8):
            num[yy, xx, k] = out[:, 128 * k:128 * k + 128]

    def num_run(blocks):
        def body(i, _):
            dy, dx = blocks(i)
            num_block((y + dy) % 4, (x + dx) % 4)
            return 0
        return body

    def run(count, blocks):
        lax.fori_loop(0, count, num_run(blocks), 0)

    def part_a(place, part, rows=every):
        return num.at[place, part, rows, lo]

    def part_b(place, part, rows=every):
        return num.at[part, place, rows, hi]

    two, four = num.at[0, pl.ds(0, 2), every, lo], num.at[0, every, every, lo]
    colours = (
        (part_a, (y, yr, yl, yo), (x, xr, xl, xo), ha1, ha2, at_y(1), at_y(3)),
        (part_b, (x, xr, xl, xo), (y, yr, yl, yo), hb1, hb2, at_x(1), at_x(3)),
    )
    travels = {3: 0, 2: 0, 1: 1, 0: 1}

    def wave(like, moves):
        copies = []
        for get, places, parts, once, twice, right, left in colours:
            for place, part, side in moves:
                target = once.at[part] if place == 3 else twice.at[side, part]
                copies.append((get(places[place], parts[part]), target, right if side == 0 else left))
        return group(like, *copies)

    w1 = wave(four, ((3, 3, 0), (3, 1, 1)))
    w2 = wave(four, ((3, 2, 0), (3, 0, 1)))
    e1 = wave(four, ((1, 1, 0), (2, 3, 1)))
    e2 = wave(four, ((1, 0, 0), (2, 2, 1)))
    l1 = wave(four, ((1, 3, 0), (2, 1, 1)))
    l2 = wave(four, ((1, 2, 0), (2, 0, 1)))

    def pass_on(parts_now):
        for get, places, parts, once, twice, right, left in colours:
            for part in parts_now:
                target = get(places[1 + travels[part]], parts[part])
                target[...] = target[...] + once[part]

    def settle(parts_now):
        for get, places, parts, once, twice, right, left in colours:
            for part in parts_now:
                target = get(places[0], parts[part])
                target[...] = target[...] + (twice[0, part] + twice[1, part])

    def mid_moves(like, moves):
        copies = []
        for (get, places, parts, _, _, _, _), (once, twice), right, left in (
            (colours[0], (ma1, ma2), at_x(1), at_x(3)), (colours[1], (mb1, mb2), at_y(1), at_y(3)),
        ):
            for part, h, side in moves:
                target = once.at[side] if part == 3 else twice.at[side, quad[h]]
                copies.append((get(places[0], parts[part], quad[h]), target, right if side == 0 else left))
        return group(like, *copies)

    mf = mid_moves(two, ((3, 0, 0), (3, 1, 1)))
    me1 = mid_moves(num.at[0, 0, every, lo], ((1, 1, 0),))
    me2 = mid_moves(num.at[0, 0, every, lo], ((2, 0, 1),))
    ml = mid_moves(two, ((1, 0, 0), (2, 1, 1)))

    def chosen(order):
        def blocks(i):
            dy = sum(jnp.where(i == k, v[0], 0) for k, v in enumerate(order))
            dx = sum(jnp.where(i == k, v[1], 0) for k, v in enumerate(order))
            return dy, dx
        run(len(order), blocks)

    run(4, lambda i: (2, i))
    w1.start(0, 1)
    w2.start(0, 1)
    run(3, lambda i: ((i + 3) % 4, 2))
    w1.start(2, 3)
    w2.start(2, 3)
    chosen([(1, 1), (1, 0), (3, 3), (0, 1)])
    e1.start()
    chosen([(1, 3), (3, 1), (3, 0), (0, 3), (0, 0)])

    def zz(d):
        return (z + 8 + d) % 8

    ring1 = group(
        c1,
        (num.at[half[0], every, zz(4), end], c1.at[0], at_z(1)), (num.at[half[1], every, zz(4), end], c1.at[1], at_z(7)),
    )
    ring1.start()

    def ring_send(buf, d):
        copies = group(
            buf,
            (num.at[every, every, zz(d), end], buf.at[0], at_z(1)), (num.at[every, every, zz(-d), end], buf.at[1], at_z(7)),
        )
        copies.start()
        return copies

    def ring_add(buf, d):
        for side, place in ((0, zz(d)), (1, zz(-d))):
            target = num.at[every, every, place, end]
            target[...] = target[...] + buf[side]

    tx_copies.arrive()
    tsy[...] = tsx[...] + trx[0] + trx[1] + trx[2]
    ty_copies = group(try_, *[(tsy, try_.at[d - 1], at_y(d)) for d in (1, 2, 3)])
    ty_copies.start()
    w1.arrive()
    pass_on((3, 1))
    l1.start()
    e2.start()
    ring1.arrive()
    for side, place in ((0, zz(3)), (1, zz(-3))):
        target = num.at[half[side], every, place, end]
        target[...] = target[...] + c1[side]
    ring2 = ring_send(c2, 3)
    w2.arrive()
    pass_on((2, 0))
    l2.start()
    ty_copies.arrive()
    tsz[...] = tsy[...] + try_[0] + try_[1] + try_[2]
    tz_copies = group(trz, *[(tsz, trz.at[d - 1], at_z(d)) for d in range(1, 8)])
    tz_copies.start()
    ring2.arrive()
    ring_add(c2, 2)
    ring3 = ring_send(c3, 2)
    e1.arrive()
    l1.arrive()
    settle((3, 1))
    mf.start()
    me1.start()
    ring3.arrive()
    ring_add(c3, 1)
    ring4 = ring_send(c4, 1)
    e2.arrive()
    l2.arrive()
    settle((2, 0))
    me2.start()
    ring4.arrive()
    target = num.at[every, every, z, end]
    target[...] = target[...] + (c4[0] + c4[1])
    cy_copies = group(cyb, *[(num.at[(y + d) % 4, every, z, end], cyb.at[d - 1], at_y(d)) for d in (1, 2, 3)])
    cy_copies.start()
    mf.arrive()
    for get, places, parts, once in ((part_a, (y,), (x, xr, xl), ma1), (part_b, (x,), (y, yr, yl), mb1)):
        for side in (0, 1):
            target = get(places[0], parts[1 + side], quad[side])
            target[...] = target[...] + once[side]
    ml.start()
    tz_copies.arrive()
    totals = tsz[...]
    for d in range(7):
        totals = totals + trz[d]
    totals = jnp.broadcast_to(totals[:1], (128, 128)).T[:64]
    cy_copies.arrive()
    target = num.at[y, every, z, end]
    target[...] = target[...] + (cyb[0] + cyb[1] + cyb[2])
    cx_copies = group(cxb, *[(num.at[y, (x + d) % 4, z, end], cxb.at[d - 1], at_x(d)) for d in (1, 2, 3)])
    cx_copies.start()
    me1.arrive()
    me2.arrive()
    ml.arrive()
    for get, place, part, twice in ((part_a, y, x, ma2), (part_b, x, y, mb2)):
        target = get(place, part)
        target[...] = target[...] + (twice[0] + twice[1])
    z_copies = group(rz, *[(num.at[y, x, zz(d), low_rows], rz.at[d - 1], at_z(d)) for d in range(1, 8)])
    z_copies.start()
    cx_copies.arrive()
    whole = num[y, x, z, end] + (cxb[0] + cxb[1] + cxb[2])
    wn[y, x, z, end] = w[y, x, z, end] * (whole / totals[48:])
    w_gather.all_sent()
    n_gather = Gather(wn)
    n_gather.cx.start()
    z_copies.arrive()
    whole = num[y, x, z, low_rows]
    for d in range(7):
        whole = whole + rz[d]
    wn[y, x, z, low_rows] = w[y, x, z, low_rows] * (whole / totals[:48])
    n_gather.zc.start()

    out_templ[...] = moved(wn[y, x, z], perms[2 * flip + 1])
    acc[...] = jnp.zeros_like(acc)
    for event in (1, 3, 2, 6, 4, 5, 7, 8, 9, 10):
        n_gather.event(event)
    gain_all(wn, mid_lhs, n_gather)
    gain2, last_copy = gain((sy, ry), slot())
    final = mid * gain2
    fin[...] = jnp.concatenate([final, final], 0).T
    f_copies = group(
        fo.at[pl.ds(0, 3)],
        *[
            (fin.at[pl.ds(pl.multiple_of(8 * ((f + d) % 8), 8), 8)], fo.at[z_hi], at_z(d))
            for d in (2, 4, 6)
        ],
    )
    f_copies.start()
    fo[pl.ds(z_hi, 1)] = fin[pl.ds(pl.multiple_of(8 * f, 8), 8), :][None]
    halo.wait_send()
    n_gather.all_sent()
    for g in range(4):
        s_copy(g, s_slots[g]).wait_send()
    sent([mid_copy, last_copy])
    for part in groups:
        part.sent()
    f_copies.arrive()
    out_act[...] = fo[...]


def finish(parts, templ, out_act, out_templ):
    near = lax.broadcasted_iota(jnp.int32, (8, 128), 1) < 64
    out_act[:, :128] = jnp.where(near, parts[0], parts[1])
    out_act[:, 128:] = jnp.where(near, parts[2], parts[3])
    out_templ[...] = templ[...]


COPIES = 64


def on_device(signal, templates, activations):
    tables = build_tables()
    vmem = pl.BlockSpec(memory_space=pltpu.VMEM)
    f32 = lambda *shape: pltpu.VMEM(shape, F32)
    parts, templ = pl.pallas_call(
        kernel,
        out_shape=(jax.ShapeDtypeStruct((4, 8, 128), F32), jax.ShapeDtypeStruct((64, 128), F32)),
        in_specs=[pl.BlockSpec(memory_space=pl.ANY)] + [vmem] * 9,
        out_specs=(vmem, vmem),
        scratch_shapes=[
            f32(33, 256, 128),
            f32(8, 8, 256),
            f32(256, 128),
            f32(8, 256, 128),
            f32(16, 256),
            f32(16, 128),
            f32(8, 1024, 128),
            f32(4, 1024, 128),
            f32(4, 4, 8, 64, 128),
            f32(4, 4, 8, 64, 128),
            f32(4, 4, 8, 64, 128),
            f32(4, 8, 24, 128),
            f32(2, 4, 8, 24, 128),
            f32(4, 8, 24, 128),
            f32(2, 4, 8, 24, 128),
            f32(2, 4, 24, 128),
            f32(2, 8, 24, 128),
            f32(2, 4, 24, 128),
            f32(2, 8, 24, 128),
            f32(2, 2, 4, 16, 128),
            f32(2, 4, 4, 16, 128),
            f32(2, 4, 4, 16, 128),
            f32(2, 4, 4, 16, 128),
            f32(3, 4, 16, 128),
            f32(3, 16, 128),
            f32(7, 48, 128),
            f32(144, 128),
            f32(72, 128), f32(72, 128), f32(72, 128), f32(72, 128),
            f32(8, 128),
            f32(3, 8, 128), f32(3, 8, 128), f32(7, 8, 128),
            f32(8, 128), f32(8, 128),
            f32(128, 128),
            f32(4, 8, 128),
            pltpu.SemaphoreType.DMA((4,)),
            pltpu.SemaphoreType.DMA((COPIES,)),
            pltpu.SemaphoreType.DMA((COPIES,)),
        ],
        compiler_params=pltpu.CompilerParams(
            collective_id=0, has_side_effects=True, vmem_limit_bytes=60 * 1024 * 1024
        ),
    )(signal.reshape(32, 256, 128), templates, activations, *tables)
    return pl.pallas_call(
        finish,
        out_shape=(jax.ShapeDtypeStruct((8, 256), F32), jax.ShapeDtypeStruct((64, 128), F32)),
        in_specs=[vmem, vmem],
        out_specs=(vmem, vmem),
    )(parts, templ)


def solution(mesh):
    return jax.shard_map(
        on_device,
        mesh=mesh,
        in_specs=(P("frames", "freq", None), P(None, ("freq", "frames")), P("freq", "frames")),
        out_specs=(P("freq", "frames"), P(None, ("freq", "frames"))),
        check_vma=False,
    )
```

```python
import math

import jax
import jax.numpy as jnp
import ml_dtypes
import numpy as np
from jax import lax
from jax.experimental import pallas as pl
from jax.experimental.pallas import tpu as pltpu
from jax.sharding import PartitionSpec as P

MESH = pl.DeviceIdType.MESH
F32 = jnp.float32
BF16 = jnp.bfloat16


def halves(table):
    high = table.astype(ml_dtypes.bfloat16)
    low = (table - high.astype(np.float64)).astype(ml_dtypes.bfloat16)
    return high, low


def build_tables():
    rows = np.arange(256)
    lanes = np.arange(128)
    m = (rows[:, None] * 128 + lanes[None, :]).astype(np.float64)
    window = (0.5 - 0.5 * np.cos(2 * math.pi / 65536 * m)).astype(np.float32)
    first = []
    twiddle = []
    for odd in (0, 1):
        k1 = 2 * np.arange(128) + odd
        angle = 2 * math.pi / 512 * (k1[:, None] * rows[None, :] % 512)
        real, imag = np.cos(angle), -np.sin(angle)
        if not odd:
            imag[0] = 1.0 - 2.0 * (rows % 2)
        first.append(np.concatenate([real, imag], 0))
        twiddle.append(2 * math.pi / 65536 * (k1[:, None] * lanes[None, :]))
    twiddle = np.concatenate(twiddle, 0)
    first = np.stack([np.stack(halves(part)) for part in first])
    second = []
    special = []
    lam = np.arange(128)
    z, x, rev, other = lam % 8, lam // 8 % 4, lam // 32 % 2, lam // 64
    for core in (0, 1):
        base = 8 * (2 * (z // 2) + (core ^ other)) + 4 * (z % 2) + x
        k2 = np.where(rev == 1, 127 - base, base)
        angle = 2 * math.pi / 128 * (lanes[:, None] * k2[None, :] % 128)
        cos, sin = np.cos(angle) / 32, np.sin(angle) / 32
        second.append(np.stack(halves(np.concatenate([np.concatenate([cos, -sin], 1), np.concatenate([sin, cos], 1)], 0))))
        angle = 2 * math.pi / 128 * (lanes[:, None] * (base + 0.5 * rev)[None, :])
        cos, sin = np.cos(angle) / 32, np.sin(angle) / 32
        keep, turn = (1 - rev)[None, :], rev[None, :]
        special.append(
            np.stack(
                halves(
                    np.concatenate(
                        [np.concatenate([cos * keep, -sin * keep], 1), np.concatenate([cos * turn, -sin * turn], 1)], 0
                    )
                )
            )
        )
    sigma = np.where(lanes < 64, 2 * lanes, 2 * (lanes - 64) + 1)
    perms = []
    for order in (sigma, (128 - sigma) % 128):
        perm = np.zeros((128, 128))
        perm[order, lanes] = 1.0
        perms += [perm, perm.T]
    perms = np.stack(perms).astype(ml_dtypes.bfloat16)
    return (
        window,
        np.cos(twiddle).astype(np.float32),
        np.sin(twiddle).astype(np.float32),
        first,
        np.stack(second),
        np.stack(special),
        perms,
    )


def split(value):
    high = value.astype(BF16)
    return high, (value - high.astype(F32)).astype(BF16)


def dot(a, b):
    return jnp.dot(a, b, preferred_element_type=F32)


def dot_t(a, b):
    return lax.dot_general(a, b, (((1,), (1,)), ((), ())), preferred_element_type=F32)


def moved(value, perm):
    high = value.astype(BF16)
    rest = value - high.astype(F32)
    middle = rest.astype(BF16)
    low = (rest - middle.astype(F32)).astype(BF16)
    return dot(high, perm) + dot(middle, perm) + dot(low, perm)


def doubled(value):
    high, low = split(value)
    lane = lax.broadcasted_iota(jnp.int32, value.shape, 1)
    both = jnp.where(lane < 64, high.astype(F32), low.astype(F32)).astype(BF16)
    return jnp.concatenate([both, both], 1)


def kernel(
    sig_hbm, templ, act, window, tcos, tsin, first, second, special, perms,
    out_act, out_templ,
    sigv, hg, ht, mag, zrow, mag0, sg, tsend, w, wn, num,
    ha1, ha2, hb1, hb2, ma1, ma2, mb1, mb2, c1, c2, c3, c4, cyb, cxb, rz,
    acc, sx, rx, sy, ry, tsx, trx, try_, trz, tsy, tsz, fin, fo,
    lsem, ssem, rsem,
):
    f = lax.axis_index("freq")
    t = lax.axis_index("frames")
    b = f % 2
    z_hi = f // 2
    z_lo = t // 16
    x = t // 4 % 4
    y = t % 4
    z = z_hi * 2 + z_lo
    partner = (f + 1 - 2 * b, t)

    def at_x(d):
        return (f, z_lo * 16 + (x + d) % 4 * 4 + y)

    def at_y(d):
        return (f, z_lo * 16 + x * 4 + (y + d) % 4)

    def at_z(d):
        other = (z + d) % 8
        return (other // 2 * 2 + b, other % 2 * 16 + x * 4 + y)

    def at_line(d):
        place = (t * 8 + f + d + 256) % 256
        return (place % 8, place // 8)

    greet = [partner] + [at_x(d) for d in (1, 2, 3)] + [at_y(d) for d in (1, 2, 3)]
    greet += [at_z(d) for d in range(1, 8)] + [at_line(-1), at_line(1)]
    barrier = pltpu.get_barrier_semaphore()
    for device in greet:
        pl.semaphore_signal(barrier, inc=1, device_id=device, device_id_type=MESH)
    loads = [
        pltpu.make_async_copy(sig_hbm.at[pl.ds(8 * i, 8)], sigv.at[pl.ds(8 * i, 8)], lsem.at[i]) for i in range(4)
    ]
    for load in loads:
        load.start()
    flip = y // 2
    w[y, x, z] = moved(templ[...], perms[2 * flip])
    hg[pl.ds(f, 1)] = act[...][None]
    zrow[...] = jnp.zeros_like(zrow)
    pl.semaphore_wait(barrier, len(greet))

    used = [0]

    def slot():
        used[0] += 1
        return used[0] - 1

    def remote(src, dst, index, device):
        return pltpu.make_async_remote_copy(
            src_ref=src, dst_ref=dst, send_sem=ssem.at[index], recv_sem=rsem.at[index],
            device_id=device, device_id_type=MESH,
        )

    class Group:
        def __init__(self, index, like, *copies):
            self.index, self.like = index, like
            self.copies = [remote(src, dst, index, device) for src, dst, device in copies]

        def start(self, *which):
            for i in which or range(len(self.copies)):
                self.copies[i].start()

        def arrive(self):
            pltpu.make_async_copy(self.like, self.like, rsem.at[self.index]).wait()

        def sent(self):
            pltpu.make_async_copy(self.like, self.like, ssem.at[self.index]).wait()

    groups = []

    def group(like, *copies):
        groups.append(Group(slot(), like, *copies))
        return groups[-1]

    halo = remote(sig_hbm.at[0], sigv.at[32], slot(), at_line(-1))
    h_far = group(hg.at[pl.ds(0, 3)], *[(act, hg.at[f], at_z(d)) for d in (2, 4, 6)])
    h_near = group(hg.at[0], (act, hg.at[f], partner))
    h_pass = group(hg.at[pl.ds(0, 3)], *[(hg.at[(f + d) % 8], hg.at[(f + d) % 8], partner) for d in (2, 4, 6)])

    lo, hi, low_rows = pl.ds(0, 24), pl.ds(24, 24), pl.ds(0, 48)
    end = pl.ds(48, 16)
    half = (pl.ds(0, 2), pl.ds(2, 2))
    quad = (pl.ds(0, 4), pl.ds(4, 4))
    every = slice(None)
    yl, yr, yo = (y + 3) % 4, (y + 1) % 4, (y + 2) % 4
    xl, xr, xo = (x + 3) % 4, (x + 1) % 4, (x + 2) % 4

    def start(copies):
        for copy in copies:
            copy.start()

    def arrive(copies):
        for copy in copies:
            copy.wait_recv()

    def sent(copies):
        for copy in copies:
            copy.wait_send()

    gather_slots = [slot() for _ in range(18)]

    class Gather:
        def __init__(self, buf):
            count = [0]

            def stage(like, *moves):
                count[0] += 1
                return Group(gather_slots[count[0] - 1], like, *[(region, region, device) for region, device in moves])

            up, down, right, left = at_y(1), at_y(3), at_x(1), at_x(3)
            self.zc = stage(rz, *[(buf.at[y, x, z, low_rows], at_z(d)) for d in range(1, 8)])
            self.cx = stage(cxb, *[(buf.at[y, x, z, end], at_x(d)) for d in (1, 2, 3)])
            self.cy = stage(cyb, *[(buf.at[y, every, z, end], at_y(d)) for d in (1, 2, 3)])
            self.cz = []
            for k in range(4):
                after, before = (z + 8 - k) % 8, (z + k) % 8
                ring = []
                for p, q in ((0, 1), (1, 0)) if k < 3 else ((0, 1),):
                    ring.append(stage(
                        c1, (buf.at[half[p], every, after, end], at_z(1)), (buf.at[half[q], every, before, end], at_z(7)),
                    ))
                self.cz.append(ring)
            two, four = buf.at[0, pl.ds(0, 2), every, lo], buf.at[0, every, every, lo]
            eight = buf.at[pl.ds(0, 2), every, every, lo]
            a_own, b_own = buf.at[y, x, every, lo], buf.at[y, x, every, hi]
            self.m1 = stage(four, (a_own, right), (a_own, left), (b_own, up), (b_own, down))
            self.m2 = stage(
                two,
                (buf.at[y, xl, quad[0], lo], right), (buf.at[y, xr, quad[1], lo], left),
                (buf.at[yl, x, quad[0], hi], up), (buf.at[yr, x, quad[1], hi], down),
            )
            self.hp = stage(four, (a_own, up), (a_own, down), (b_own, right), (b_own, left))

            def bulk(xx, yy):
                a_part, b_part = buf.at[y, xx, every, lo], buf.at[yy, x, every, hi]
                return [(a_part, up), (a_part, down), (b_part, right), (b_part, left)]

            self.hs = stage(eight, *(bulk(xl, yl) + bulk(xr, yr)))
            self.ho = stage(four, *bulk(xo, yo))
            self.f1 = stage(two, (buf.at[yl, x, every, lo], up), (buf.at[y, xl, every, hi], right))
            self.f2 = stage(
                four,
                (buf.at[yl, xl, every, lo], up), (buf.at[yr, xr, every, lo], down),
                (buf.at[yl, xl, every, hi], right), (buf.at[yr, xr, every, hi], left),
            )
            self.f3 = stage(two, (buf.at[yr, xo, every, lo], down), (buf.at[yo, xr, every, hi], left))
            self.stages = [self.zc, self.cx, self.cy] + sum(self.cz, [])
            self.stages += [self.m1, self.m2, self.hp, self.hs, self.ho, self.f1, self.f2, self.f3]

        def event(self, k):
            after = {
                1: (self.cx, self.cy), 2: (self.zc, self.m1, self.hp), 3: (self.cy, *self.cz[0]),
                4: (self.m1, self.m2, self.hs), 5: (self.hp, self.f1), 7: (self.m2, self.ho),
                9: (self.hs, self.f2), 11: (self.ho, self.f3),
            }
            if k in after:
                after[k][0].arrive()
                for stage in after[k][1:]:
                    stage.start()
            elif k in (6, 8, 10):
                ring = k // 2 - 2
                for i in range(2):
                    self.cz[ring - 1][i].arrive()
                    if i < len(self.cz[ring]):
                        self.cz[ring][i].start()
            elif k == 12:
                self.cz[3][0].arrive()
            else:
                self.f1.arrive()
                self.f2.arrive()
                self.f3.arrive()

        def all_sent(self):
            for stage in self.stages:
                stage.sent()

    w_gather = Gather(w)
    w_gather.cx.start()
    w_gather.zc.start()
    h_far.start()
    h_near.start()
    halo.start()
    s_slots = [slot() for _ in range(4)]

    def s_copy(group, index):
        return remote(tsend.at[group], sg.at[4 * b + group], index, partner)

    def pair_step(group, p):
        n = group * 8 + 2 * p
        step = group * 4 + p
        for when, event in ((3, 1), (7, 3), (8, 2), (11, 6), (12, 4), (13, 5), (15, 7)):
            @pl.when(step == when)
            def _(event=event):
                w_gather.event(event)

        @pl.when(step == 7)
        def _():
            h_far.arrive()
            h_pass.start()

        win = window[...]
        h0, h1, h2 = sigv[n], sigv[n + 1], sigv[n + 2]
        a0, a1 = h0 * win, h1 * win
        b1, b2 = h1 - a1, h2 - h2 * win
        ev, ov = [], []
        for parity, block in ((0, jnp.concatenate([a0 + b1, a1 + b2], 1)), (1, jnp.concatenate([a0 - b1, a1 - b2], 1))):
            high, low = split(block)
            d_high, d_low = first[parity, 0], first[parity, 1]
            part = dot(d_high, high) + dot(d_high, low) + dot(d_low, high)
            (ev if parity == 0 else ov).append(part)
        pieces = []
        for frame in range(2):
            for parity, part in ((0, ev[0]), (1, ov[0])):
                real = part[:128, 128 * frame:128 * frame + 128]
                imag = part[128:, 128 * frame:128 * frame + 128]
                tc = tcos[128 * parity:128 * parity + 128, :]
                ts = tsin[128 * parity:128 * parity + 128, :]
                piece = jnp.concatenate([real * tc + imag * ts, imag * tc - real * ts], 1)
                if parity == 0:
                    zrow[pl.ds(2 * p + frame, 1), :] = piece[:1]
                pieces.append(piece)
        m_high, m_low = second[b, 0], second[b, 1]
        for frame in range(2):
            high, low = split(jnp.concatenate(pieces[2 * frame:2 * frame + 2], 0))
            out = dot(high, m_high) + dot(low, m_high) + dot(high, m_low)
            real, imag = out[:, :128], out[:, 128:]
            mag[2 * p + frame] = jnp.sqrt(real * real + imag * imag)

    lane = lax.broadcasted_iota(jnp.int32, (128, 128), 1)
    row = lax.broadcasted_iota(jnp.int32, (128, 128), 0)
    mirrored = lane // 32 % 2 == 1
    top = row == 0

    def turn(group, j):
        m = mag[j]
        low = jnp.concatenate([m[:64], m[128:192]], 0)
        high = jnp.concatenate([m[64:128], m[192:]], 0)
        extra = jnp.broadcast_to(mag0[pl.ds(j, 1), :], (128, 128))
        high_row = jnp.broadcast_to(high[:1], (128, 128))
        low = jnp.where(top, jnp.where(mirrored, high_row, extra), low)
        high = jnp.where(top & mirrored, extra, high)
        low, high = low.T, high.T
        for ref, index, off in ((sg, 4 * b + group, 0), (tsend, group, 64)):
            for value, place, part in ((low, 0, 0), (high, 1, 0), (high, 2, 1), (low, 3, 1)):
                ref[index, pl.ds(256 * place + j, 32, stride=8), :] = value[off + 32 * part:off + 32 * part + 32]

    def group_step(group, _):
        @pl.when(group == 0)
        def _():
            loads[0].wait()
            loads[1].wait()

        @pl.when(group == 1)
        def _():
            loads[2].wait()

        @pl.when(group == 2)
        def _():
            loads[3].wait()

        @pl.when(group == 3)
        def _():
            halo.wait_recv()
            sigv[32] = sigv[32] * jnp.where(t * 8 + f == 255, 0.0, 1.0)

        def body(p, _):
            pair_step(group, p)
            return 0

        lax.fori_loop(0, 4, body, 0)
        high, low = split(zrow[...])
        out = dot(high, special[b, 0]) + dot(low, special[b, 0]) + dot(high, special[b, 1])
        mag0[...] = jnp.sqrt(out[:, :128] * out[:, :128] + out[:, 128:] * out[:, 128:])

        def turn_body(j, _):
            turn(group, 2 * j)
            turn(group, 2 * j + 1)
            return 0

        lax.fori_loop(0, 4, turn_body, 0)
        for g in range(4):
            @pl.when(group == g)
            def _(g=g):
                s_copy(g, s_slots[g]).start()
        return 0

    lax.fori_loop(0, 4, group_step, 0)

    h_near.arrive()
    h_pass.arrive()
    rows64 = hg[...].reshape(64, 256)
    ht[...] = jnp.concatenate([rows64, rows64], 0).T
    h2 = ht[pl.ds(pl.multiple_of(64 * z_hi, 64), 64), :]
    for g in range(4):
        s_copy(g, s_slots[g]).wait_recv()

    def frames_block(places):
        cols = []
        for yy, xx, k in places:
            place = pl.multiple_of(((yy * 4 + xx) * 8 + k) * 8, 8)
            cols.append(jnp.concatenate([sg[g, pl.ds(place, 8), :] for g in range(8)], 0))
        return jnp.concatenate(cols, 1)

    def ratio_of(buf, lhs, places):
        wide = jnp.concatenate([buf[place] for place in places], 1)
        high, low = split(wide)
        approx = dot(lhs, jnp.concatenate([high, high, low, low], 0))
        return frames_block(places) / approx, high, low

    def gain_block(buf, lhs, places):
        ratio, high, low = ratio_of(buf, lhs, places)
        r_high, r_low = split(ratio)
        left = jnp.concatenate([r_high, r_low, jnp.ones((16, 128 * len(places)), BF16)], 0)
        acc[...] += dot_t(left, jnp.concatenate([high, low], 0))

    def gain(stage, index):
        total = acc[...]
        part = jnp.concatenate([total[:64] + total[64:128], total[128:136]], 0)
        stage_send, stage_recv = stage
        stage_send[...] = part + pltpu.roll(part, 64, 1)
        copy = remote(stage_send, stage_recv, index, partner)
        copy.start()
        copy.wait_recv()
        both = stage_send[...] + stage_recv[...]
        return both[:64] / both[64:65], copy

    lhs1 = doubled(h2)
    acc[...] = jnp.zeros_like(acc)

    near = [(yy, xx) for yy in (yl, y, yr) for xx in (xl, x, xr)]
    far = [(yo, xx) for xx in (xl, x, xr, xo)] + [(yy, xo) for yy in (yl, y, yr)]

    def gain_all(buf, lhs, gather):
        def run_z(start, stop, which):
            def body(i, _):
                gain_block(buf, lhs, [(yy, xx, (z + i) % 8) for yy, xx in which])
                return 0

            lax.fori_loop(start, stop, body, 0)

        run_z(5, 8, near)
        gather.event(11)
        run_z(8, 12, near)
        gather.event(12)
        run_z(12, 13, near)
        gather.event(13)
        run_z(0, 8, far)

    for event in (8, 9, 10):
        w_gather.event(event)
    gain_all(w, lhs1, w_gather)
    gain1, mid_copy = gain((sx, rx), slot())
    mid = h2 * gain1
    mid_lhs = doubled(mid)
    mid_t = jnp.concatenate([mid, mid], 0).T
    mid_left = doubled(mid_t[:64])

    tsx[...] = jnp.broadcast_to(jnp.sum(mid, axis=0, keepdims=True), (8, 128))
    tx_copies = group(trx, *[(tsx, trx.at[d - 1], at_x(d)) for d in (1, 2, 3)])
    tx_copies.start()

    def num_block(yy, xx):
        ratio, _, _ = ratio_of(w, mid_lhs, [(yy, xx, k) for k in range(8)])
        high, low = split(ratio)
        out = dot(mid_left, jnp.concatenate([high, high, low, low], 0))
        for k in range(8):
            num[yy, xx, k] = out[:, 128 * k:128 * k + 128]

    def num_run(blocks):
        def body(i, _):
            dy, dx = blocks(i)
            num_block((y + dy) % 4, (x + dx) % 4)
            return 0
        return body

    def run(count, blocks):
        lax.fori_loop(0, count, num_run(blocks), 0)

    def part_a(place, part, rows=every):
        return num.at[place, part, rows, lo]

    def part_b(place, part, rows=every):
        return num.at[part, place, rows, hi]

    two, four = num.at[0, pl.ds(0, 2), every, lo], num.at[0, every, every, lo]
    colours = (
        (part_a, (y, yr, yl, yo), (x, xr, xl, xo), ha1, ha2, at_y(1), at_y(3)),
        (part_b, (x, xr, xl, xo), (y, yr, yl, yo), hb1, hb2, at_x(1), at_x(3)),
    )
    travels = {3: 0, 2: 0, 1: 1, 0: 1}

    def wave(like, moves):
        copies = []
        for get, places, parts, once, twice, right, left in colours:
            for place, part, side in moves:
                target = once.at[part] if place == 3 else twice.at[side, part]
                copies.append((get(places[place], parts[part]), target, right if side == 0 else left))
        return group(like, *copies)

    w1 = wave(four, ((3, 3, 0), (3, 1, 1)))
    w2 = wave(four, ((3, 2, 0), (3, 0, 1)))
    e1 = wave(four, ((1, 1, 0), (2, 3, 1)))
    e2 = wave(four, ((1, 0, 0), (2, 2, 1)))
    l1 = wave(four, ((1, 3, 0), (2, 1, 1)))
    l2 = wave(four, ((1, 2, 0), (2, 0, 1)))

    def pass_on(parts_now):
        for get, places, parts, once, twice, right, left in colours:
            for part in parts_now:
                target = get(places[1 + travels[part]], parts[part])
                target[...] = target[...] + once[part]

    def settle(parts_now):
        for get, places, parts, once, twice, right, left in colours:
            for part in parts_now:
                target = get(places[0], parts[part])
                target[...] = target[...] + (twice[0, part] + twice[1, part])

    def mid_moves(like, moves):
        copies = []
        for (get, places, parts, _, _, _, _), (once, twice), right, left in (
            (colours[0], (ma1, ma2), at_x(1), at_x(3)), (colours[1], (mb1, mb2), at_y(1), at_y(3)),
        ):
            for part, h, side in moves:
                target = once.at[side] if part == 3 else twice.at[side, quad[h]]
                copies.append((get(places[0], parts[part], quad[h]), target, right if side == 0 else left))
        return group(like, *copies)

    mf = mid_moves(two, ((3, 0, 0), (3, 1, 1)))
    me1 = mid_moves(num.at[0, 0, every, lo], ((1, 1, 0),))
    me2 = mid_moves(num.at[0, 0, every, lo], ((2, 0, 1),))
    ml = mid_moves(two, ((1, 0, 0), (2, 1, 1)))

    def chosen(order):
        def blocks(i):
            dy = sum(jnp.where(i == k, v[0], 0) for k, v in enumerate(order))
            dx = sum(jnp.where(i == k, v[1], 0) for k, v in enumerate(order))
            return dy, dx
        run(len(order), blocks)

    run(4, lambda i: (2, i))
    w1.start(0, 1)
    w2.start(0, 1)
    run(3, lambda i: ((i + 3) % 4, 2))
    w1.start(2, 3)
    w2.start(2, 3)
    chosen([(1, 1), (1, 0), (3, 3), (0, 1)])
    e1.start()
    chosen([(1, 3), (3, 1), (3, 0), (0, 3), (0, 0)])

    def zz(d):
        return (z + 8 + d) % 8

    ring1 = group(
        c1,
        (num.at[half[0], every, zz(4), end], c1.at[0], at_z(1)), (num.at[half[1], every, zz(4), end], c1.at[1], at_z(7)),
    )
    ring1.start()

    def ring_send(buf, d):
        copies = group(
            buf,
            (num.at[every, every, zz(d), end], buf.at[0], at_z(1)), (num.at[every, every, zz(-d), end], buf.at[1], at_z(7)),
        )
        copies.start()
        return copies

    def ring_add(buf, d):
        for side, place in ((0, zz(d)), (1, zz(-d))):
            target = num.at[every, every, place, end]
            target[...] = target[...] + buf[side]

    tx_copies.arrive()
    tsy[...] = tsx[...] + trx[0] + trx[1] + trx[2]
    ty_copies = group(try_, *[(tsy, try_.at[d - 1], at_y(d)) for d in (1, 2, 3)])
    ty_copies.start()
    w1.arrive()
    pass_on((3, 1))
    l1.start()
    e2.start()
    ring1.arrive()
    for side, place in ((0, zz(3)), (1, zz(-3))):
        target = num.at[half[side], every, place, end]
        target[...] = target[...] + c1[side]
    ring2 = ring_send(c2, 3)
    w2.arrive()
    pass_on((2, 0))
    l2.start()
    ty_copies.arrive()
    tsz[...] = tsy[...] + try_[0] + try_[1] + try_[2]
    tz_copies = group(trz, *[(tsz, trz.at[d - 1], at_z(d)) for d in range(1, 8)])
    tz_copies.start()
    ring2.arrive()
    ring_add(c2, 2)
    ring3 = ring_send(c3, 2)
    e1.arrive()
    l1.arrive()
    settle((3, 1))
    mf.start()
    me1.start()
    ring3.arrive()
    ring_add(c3, 1)
    ring4 = ring_send(c4, 1)
    e2.arrive()
    l2.arrive()
    settle((2, 0))
    me2.start()
    ring4.arrive()
    target = num.at[every, every, z, end]
    target[...] = target[...] + (c4[0] + c4[1])
    cy_copies = group(cyb, *[(num.at[(y + d) % 4, every, z, end], cyb.at[d - 1], at_y(d)) for d in (1, 2, 3)])
    cy_copies.start()
    mf.arrive()
    for get, places, parts, once in ((part_a, (y,), (x, xr, xl), ma1), (part_b, (x,), (y, yr, yl), mb1)):
        for side in (0, 1):
            target = get(places[0], parts[1 + side], quad[side])
            target[...] = target[...] + once[side]
    ml.start()
    tz_copies.arrive()
    totals = tsz[...]
    for d in range(7):
        totals = totals + trz[d]
    totals = jnp.broadcast_to(totals[:1], (128, 128)).T[:64]
    cy_copies.arrive()
    target = num.at[y, every, z, end]
    target[...] = target[...] + (cyb[0] + cyb[1] + cyb[2])
    cx_copies = group(cxb, *[(num.at[y, (x + d) % 4, z, end], cxb.at[d - 1], at_x(d)) for d in (1, 2, 3)])
    cx_copies.start()
    me1.arrive()
    me2.arrive()
    ml.arrive()
    for get, place, part, twice in ((part_a, y, x, ma2), (part_b, x, y, mb2)):
        target = get(place, part)
        target[...] = target[...] + (twice[0] + twice[1])
    z_copies = group(rz, *[(num.at[y, x, zz(d), low_rows], rz.at[d - 1], at_z(d)) for d in range(1, 8)])
    z_copies.start()
    cx_copies.arrive()
    whole = num[y, x, z, end] + (cxb[0] + cxb[1] + cxb[2])
    wn[y, x, z, end] = w[y, x, z, end] * (whole / totals[48:])
    w_gather.all_sent()
    n_gather = Gather(wn)
    n_gather.cx.start()
    z_copies.arrive()
    whole = num[y, x, z, low_rows]
    for d in range(7):
        whole = whole + rz[d]
    wn[y, x, z, low_rows] = w[y, x, z, low_rows] * (whole / totals[:48])
    n_gather.zc.start()

    out_templ[...] = moved(wn[y, x, z], perms[2 * flip + 1])
    acc[...] = jnp.zeros_like(acc)
    for event in (1, 3, 2, 6, 4, 5, 7, 8, 9, 10):
        n_gather.event(event)
    gain_all(wn, mid_lhs, n_gather)
    gain2, last_copy = gain((sy, ry), slot())
    final = mid * gain2
    fin[...] = jnp.concatenate([final, final], 0).T
    f_copies = group(
        fo.at[pl.ds(0, 3)],
        *[
            (fin.at[pl.ds(pl.multiple_of(8 * ((f + d) % 8), 8), 8)], fo.at[z_hi], at_z(d))
            for d in (2, 4, 6)
        ],
    )
    f_copies.start()
    fo[pl.ds(z_hi, 1)] = fin[pl.ds(pl.multiple_of(8 * f, 8), 8), :][None]
    halo.wait_send()
    n_gather.all_sent()
    for g in range(4):
        s_copy(g, s_slots[g]).wait_send()
    sent([mid_copy, last_copy])
    for part in groups:
        part.sent()
    f_copies.arrive()
    assert used[0] <= COPIES, used[0]
    out_act[...] = fo[...]


def finish(parts, templ, out_act, out_templ):
    near = lax.broadcasted_iota(jnp.int32, (8, 128), 1) < 64
    out_act[:, :128] = jnp.where(near, parts[0], parts[1])
    out_act[:, 128:] = jnp.where(near, parts[2], parts[3])
    out_templ[...] = templ[...]


COPIES = 50


def on_device(signal, templates, activations):
    tables = build_tables()
    vmem = pl.BlockSpec(memory_space=pltpu.VMEM)
    f32 = lambda *shape: pltpu.VMEM(shape, F32)
    parts, templ = pl.pallas_call(
        kernel,
        out_shape=(jax.ShapeDtypeStruct((4, 8, 128), F32), jax.ShapeDtypeStruct((64, 128), F32)),
        in_specs=[pl.BlockSpec(memory_space=pl.ANY)] + [vmem] * 9,
        out_specs=(vmem, vmem),
        scratch_shapes=[
            f32(33, 256, 128),
            f32(8, 8, 256),
            f32(256, 128),
            f32(8, 256, 128),
            f32(16, 256),
            f32(16, 128),
            f32(8, 1024, 128),
            f32(4, 1024, 128),
            f32(4, 4, 8, 64, 128),
            f32(4, 4, 8, 64, 128),
            f32(4, 4, 8, 64, 128),
            f32(4, 8, 24, 128),
            f32(2, 4, 8, 24, 128),
            f32(4, 8, 24, 128),
            f32(2, 4, 8, 24, 128),
            f32(2, 4, 24, 128),
            f32(2, 8, 24, 128),
            f32(2, 4, 24, 128),
            f32(2, 8, 24, 128),
            f32(2, 2, 4, 16, 128),
            f32(2, 4, 4, 16, 128),
            f32(2, 4, 4, 16, 128),
            f32(2, 4, 4, 16, 128),
            f32(3, 4, 16, 128),
            f32(3, 16, 128),
            f32(7, 48, 128),
            f32(144, 128),
            f32(72, 128), f32(72, 128), f32(72, 128), f32(72, 128),
            f32(8, 128),
            f32(3, 8, 128), f32(3, 8, 128), f32(7, 8, 128),
            f32(8, 128), f32(8, 128),
            f32(128, 128),
            f32(4, 8, 128),
            pltpu.SemaphoreType.DMA((4,)),
            pltpu.SemaphoreType.DMA((COPIES,)),
            pltpu.SemaphoreType.DMA((COPIES,)),
        ],
        compiler_params=pltpu.CompilerParams(
            collective_id=0, has_side_effects=True, vmem_limit_bytes=60 * 1024 * 1024
        ),
    )(signal.reshape(32, 256, 128), templates, activations, *tables)
    return pl.pallas_call(
        finish,
        out_shape=(jax.ShapeDtypeStruct((8, 256), F32), jax.ShapeDtypeStruct((64, 128), F32)),
        in_specs=[vmem, vmem],
        out_specs=(vmem, vmem),
    )(parts, templ)


def solution(mesh):
    return jax.shard_map(
        on_device,
        mesh=mesh,
        in_specs=(P("frames", "freq", None), P(None, ("freq", "frames")), P("freq", "frames")),
        out_specs=(P("freq", "frames"), P(None, ("freq", "frames"))),
        check_vma=False,
    )
```
